128 devices in a mesh: view: 8 (over y, core), block: 16 (over z, x).
Axes of the slice: x: 4, y: 4, z: 4, core: 2. Of those that a mesh axis runs over, the one named last changes fastest.
Arguments:
- estimate0: float32 [1024, 64, 256], P('block'), may hold values from 0.5 to 1.5
- pieces: bfloat16 [8, 256, 4, 64, 256], P('view', 'block'), may hold values from 0.19921875 to 2
- dest_block: int32 [8, 256, 1], replicated, may hold values from 0 to 15; in each aligned block of 16 rows (0 to 15, 16 to 31, ..., all dimensions but the last counted through in order) at most 2 rows name the same one
- slot_index: int32 [8, 256], replicated, may hold values from 0 to 15
- psf_shift: int32 [8, 3], replicated, may hold values from -3 to 3
- psf_taps: float32 [8, 3, 21], replicated, may hold values from 0.05 to 1
- background: float32 [8], replicated, may hold values from 0.1 to 0.5
Outputs:
- estimate: float32 [1024, 64, 256], P('block')
The draws below stay inside these ranges and needn't reach their ends.
Inputs may be any that keep to these rules, and one draw needn't show every extreme that they name: `dest_block`: among the 16 pieces held by one device (aligned blocks of 16 rows, views and pieces taken together), no slab is named more than 2 times.
All inputs are finite; a program needn't handle non-finite values.
Results may differ from the reference program's by a relative error of at most 0.0014.
Values may be sent and summed in bfloat16 or wider, within the bound.
No kernel may reach another device: no remote copies, remote signals or barrier semaphores. Data moves between devices by JAX's collectives and lax.ppermute only.
A program may use at most 128 MiB of HBM per device.

```python
import math
import jax
import jax.numpy as jnp
import numpy as np
from jax import lax

NY = 64
NX = 256
SLOTS = 16
CAP = 2
SMAX = 3
ITERS = 2
TAPS = 21
HALO = 13
PZ = 4
VIEWS = 8
PIECES = 256
NZ = 1024
N_BLOCK = 16


def plant(values, stream_key, smallest, largest):
    extent = values.shape
    spot = [jax.random.randint(jax.random.fold_in(stream_key, axis), (), 0, extent[axis]) for axis in range(len(extent))]
    values = values.at[tuple(spot)].set(smallest)
    longest = extent.index(max(extent))
    spot[longest] = (spot[longest] + 1) % extent[longest]
    return values.at[tuple(spot)].set(largest)


def levels(stream_key, dims, split, smallest, largest):
    factor_of, own = 1.0, jax.random.fold_in(stream_key, 6)
    for dim, shards_of in split:
        heights = jnp.exp(jax.random.uniform(jax.random.fold_in(own, dim), (shards_of,), jnp.float32, smallest / len(split), largest / len(split)))
        factor_of = factor_of * jnp.repeat(heights, dims[dim] // shards_of).reshape([-1 if axis == dim else 1 for axis in range(len(dims))])
    return factor_of


def routed_block(own_key, own, number, rows, amount, top, limit, lean):
    sequence = jax.random.permutation(own_key, amount)
    packed, usual = load_shares(amount, rows * top, limit, lean, True), load_shares(amount, rows * top, limit, lean, False)
    places = jnp.arange(amount)

    def named(tallies, turn):
        used = int((tallies > 0).sum())
        fixed = max(1, used // 4)
        moved = fixed + (places - fixed + turn * (used - fixed)) % max(1, amount - fixed)
        return jnp.zeros((amount,), jnp.int32).at[sequence[jnp.where(places < fixed, places, moved)]].set(jnp.asarray(tallies, jnp.int32))

    tallies = jnp.where(number % 4 == 0, named(packed, number // 4), named(usual, number - number // 4 - 1))
    mixed = jax.random.permutation(jax.random.fold_in(own, 3), amount)
    donor, taker = mixed[0:amount // 2 * 2:2], mixed[1:amount // 2 * 2:2]
    room = jnp.minimum(tallies[donor] - 1, limit - tallies[taker]) // 2
    room = jnp.where((donor == sequence[0]) | (taker == sequence[0]) | (tallies[taker] == 0), 0, jnp.maximum(room, 0))
    moved = jax.random.randint(jax.random.fold_in(own, 4), (amount // 2,), 0, 1 << 20) % (room + 1)
    tallies = tallies.at[donor].add(-moved).at[taker].add(moved)
    items = jnp.searchsorted(jnp.cumsum(tallies), jnp.arange(rows * top), side="right").astype(jnp.int32)
    grid = items.reshape(top, rows).T
    grid = grid[jax.random.permutation(jax.random.fold_in(own, 1), rows)]
    turn = jax.random.randint(jax.random.fold_in(own, 2), (rows, 1), 0, top)
    return jnp.take_along_axis(grid, (jnp.arange(top)[None, :] + turn) % top, axis=1)


def load_shares(number_of, total, limit, lean, full):
    loads = [(1 << 20) // math.isqrt(rank ** lean) + 1 for rank in range(1, number_of + 1)]
    largest = limit if full else min(limit, max(-(-total // number_of), total * loads[0] // sum(loads)))
    least = 1 if total - largest >= number_of - 1 else 0
    given, rest = [largest] + [least] * (number_of - 1), total - largest - least * (number_of - 1)
    while rest > 0:
        movable = [i for i in range(1, number_of) if given[i] < largest] or [i for i in range(1, number_of) if given[i] < limit]
        whole, remaining = sum([loads[i] for i in movable]), rest
        for i in movable:
            addition = min(limit - given[i], max(1, remaining * loads[i] // whole), rest)
            given[i] = given[i] + addition
            rest = rest - addition
    return np.array(given)


def setup_inputs(seed: int = 0) -> dict:
    key_of = jax.random.split(jax.random.key(seed), 8)
    estimate0 = jnp.clip(0.5 + 1.0 * jax.random.uniform(key_of[0], (NZ, NY, NX), jnp.float32) ** levels(key_of[0], (NZ, NY, NX), ((0, 16),), -0.2, 0.2), 0.5, 1.5)
    pieces = jnp.clip(0.19921875 + 1.8007812 * jax.random.uniform(key_of[1], (VIEWS, PIECES, PZ, NY, NX), jnp.float32) ** levels(key_of[1], (VIEWS, PIECES, PZ, NY, NX), ((0, 8), (1, 16)), -0.2, 0.2), 0.19921875, 2.0).astype(jnp.bfloat16)
    dest_block_keys = jax.random.split(jax.random.fold_in(key_of[2], 1), VIEWS * PIECES // SLOTS)
    dest_block_turns = jax.random.permutation(jax.random.fold_in(key_of[2], 3), VIEWS * PIECES // SLOTS)
    dest_block = jax.vmap(lambda own, number: routed_block(jax.random.fold_in(key_of[2], 2), own, number, SLOTS, N_BLOCK, 1, CAP, 2))(dest_block_keys, dest_block_turns).reshape((VIEWS, PIECES, 1))
    slot_index = plant(jax.random.randint(key_of[3], (VIEWS, PIECES), 0, SLOTS), jax.random.fold_in(key_of[3], 1), 0, SLOTS - 1).astype(jnp.int32)
    psf_shift = plant(jax.random.randint(key_of[4], (VIEWS, 3), 0 - SMAX, SMAX + 1), jax.random.fold_in(key_of[4], 1), 0 - SMAX, SMAX).astype(jnp.int32)
    psf_taps = jnp.clip(jnp.exp(jax.random.uniform(key_of[5], (VIEWS, 3, TAPS), jnp.float32, math.log(0.05), math.log(1.0))), 0.05, 1.0)
    background = jnp.clip(jnp.exp(jax.random.uniform(key_of[6], (VIEWS,), jnp.float32, math.log(0.1), math.log(0.5))), 0.1, 0.5)
    return {"estimate0": estimate0, "pieces": pieces, "dest_block": dest_block, "slot_index": slot_index, "psf_shift": psf_shift, "psf_taps": psf_taps, "background": background}


HIGHEST = lax.Precision.HIGHEST


def band_matrix(kernel, shift, row_count, column_count, lead_offset):
    tap_count = kernel.shape[0]
    radius = (tap_count - 1) // 2
    difference = (lax.broadcasted_iota(jnp.int32, (row_count, column_count), 1)
                  - lax.broadcasted_iota(jnp.int32, (row_count, column_count), 0)
                  - lead_offset - shift + radius)
    tap_hits = difference[:, :, None] == jnp.arange(tap_count, dtype=jnp.int32)[None, None, :]
    return jnp.sum(jnp.where(tap_hits, kernel[None, None, :], 0.0), axis=2)


def column_sums(kernel, shift, length):
    tap_count = kernel.shape[-1]
    radius = (tap_count - 1) // 2
    source = (jnp.arange(length, dtype=jnp.int32)[None, :, None] - shift[:, None, None]
              - jnp.arange(tap_count, dtype=jnp.int32)[None, None, :] + radius)
    inside = (source >= 0) & (source < length)
    return jnp.sum(jnp.where(inside, kernel[:, None, :], 0.0), axis=2)


def shift_sum(volume, kernel, shift, direction):
    length = volume.shape[0]
    tap_count = kernel.shape[0]
    radius = (tap_count - 1) // 2
    padded = jnp.pad(volume, [(HALO, HALO)] + [(0, 0)] * (volume.ndim - 1))
    result = jnp.zeros_like(volume)
    for tap in range(tap_count):
        start = (HALO + direction * (shift + tap - radius)).astype(jnp.int32)
        result = result + kernel[tap] * lax.dynamic_slice_in_dim(padded, start, length, 0)
    return result


def blur_plane(volume, band_rows, band_columns):
    along_rows = jnp.einsum('yv,zvx->zyx', band_rows, volume, precision=HIGHEST)
    return jnp.einsum('zyv,xv->zyx', along_rows, band_columns, precision=HIGHEST)


def adjoint_plane(volume, band_rows, band_columns):
    along_rows = jnp.einsum('vy,zvx->zyx', band_rows, volume, precision=HIGHEST)
    return jnp.einsum('zyv,vx->zyx', along_rows, band_columns, precision=HIGHEST)


def reference(estimate0, pieces, dest_block, slot_index, psf_shift, psf_taps, background):
    kernel = psf_taps / jnp.sum(psf_taps, axis=2, keepdims=True)
    slot_total = N_BLOCK * SLOTS
    global_slot = (dest_block[:, :, 0] * SLOTS + slot_index).astype(jnp.int32)
    averages = []
    band_list = []
    depth_weights = []
    for viewer in range(VIEWS):
        counts = jax.ops.segment_sum(jnp.ones((PIECES,), jnp.int32), global_slot[viewer], num_segments=slot_total)
        placed = jax.ops.segment_sum(pieces[viewer].astype(jnp.float32).reshape(PIECES, PZ * NY * NX),
                                     global_slot[viewer], num_segments=slot_total)
        average = placed / jnp.maximum(counts, 1).astype(jnp.float32)[:, None]
        averages.append(average.reshape(NZ, NY, NX))
        plane_mask = jnp.repeat((counts > 0).astype(jnp.float32), PZ)
        depth_weights.append(shift_sum(plane_mask, kernel[viewer, 0], psf_shift[viewer, 0], -1))
        band_list.append((band_matrix(kernel[viewer, 1], psf_shift[viewer, 1], NY, NY, 0),
                          band_matrix(kernel[viewer, 2], psf_shift[viewer, 2], NX, NX, 0)))
    weight_depth = jnp.stack(depth_weights)
    weight_rows = column_sums(kernel[:, 1], psf_shift[:, 1], NY)
    weight_columns = column_sums(kernel[:, 2], psf_shift[:, 2], NX)
    weight = jnp.einsum('vz,vy,vx->zyx', weight_depth, weight_rows, weight_columns, precision=HIGHEST)
    floor_weight = jnp.maximum(weight, 1.0)
    estimate = estimate0
    for iteration in range(ITERS):
        summed = jnp.zeros_like(estimate)
        for viewer in range(VIEWS):
            band_rows, band_columns = band_list[viewer]
            blurred = blur_plane(shift_sum(estimate, kernel[viewer, 0], psf_shift[viewer, 0], 1),
                                 band_rows, band_columns) + background[viewer]
            quotient = averages[viewer] / blurred
            summed = summed + shift_sum(adjoint_plane(quotient, band_rows, band_columns),
                                        kernel[viewer, 0], psf_shift[viewer, 0], -1)
        estimate = estimate * summed / floor_weight
    return estimate
```

```python
import jax
import jax.numpy as jnp
from jax import lax
from jax.experimental import pallas as pl
from jax.experimental.pallas import tpu as pltpu
from jax.sharding import PartitionSpec as P

CAP = 2
TAPS = 21
HALO = 16
VIEWS = 8
SLOTS = 16
NY = 64
PART = 32
ROWS = 256

F32 = jnp.float32
BF16 = jnp.bfloat16
I32 = jnp.int32


def lane_block(shape):
    return lax.broadcasted_iota(I32, shape, len(shape) - 1) // PART


def rotate(value, amount):
    return pltpu.roll(value, amount % 128, value.ndim - 1)


def digit_swap(shape):
    row = lax.broadcasted_iota(I32, shape, 0)
    column = lax.broadcasted_iota(I32, shape, 1)
    target = ((row // PART) % 4) * 128 + (row // 128) * PART + row % PART
    return jnp.where(column == target, 1.0, 0.0).astype(BF16)


def vmem(count):
    return [pl.BlockSpec(memory_space=pltpu.VMEM)] * count


def smem(count):
    return [pl.BlockSpec(memory_space=pltpu.SMEM)] * count


def band_kernel(taps_ref, shift_ref, ky_ref, kyt_ref, kx_ref, kxt_ref, bzf_ref, bza_ref):
    radius = (TAPS - 1) // 2

    def fill(difference, view, axis):
        result = jnp.zeros(difference.shape, F32)
        for tap in range(TAPS):
            result = jnp.where(difference == tap, taps_ref[(view * 3 + axis) * TAPS + tap], result)
        return result

    def one_view(view, carry):
        shift_y = shift_ref[view * 3 + 1]
        shift_x = shift_ref[view * 3 + 2]
        row = lax.broadcasted_iota(I32, (NY, ROWS), 0)
        lane = lax.broadcasted_iota(I32, (NY, ROWS), 1)
        offset = lane % NY - row
        forward = fill(offset - shift_y + radius, view, 1)
        backward = fill(-offset - shift_y + radius, view, 1)
        for block in range(4):
            mine = lane // NY == block
            ky_ref[view, block * NY:(block + 1) * NY, :] = jnp.where(mine, forward, 0.0).astype(BF16)
            kyt_ref[view, block * NY:(block + 1) * NY, :] = jnp.where(mine, backward, 0.0).astype(BF16)
        row = lax.broadcasted_iota(I32, (PART, 128), 0)
        lane = lax.broadcasted_iota(I32, (PART, 128), 1)
        for half in range(2):
            base = fill(half * PART + row - (lane % PART + HALO) - shift_x + radius, view, 2)
            for block in range(4):
                first = half * 128 + block * PART
                kx_ref[view, first:first + PART, :] = jnp.where(lane // PART == block, base, 0.0).astype(BF16)
            base = fill(half * PART + lane % PART - (row + HALO) - shift_x + radius, view, 2)
            for block in range(4):
                kxt_ref[view, block * PART:(block + 1) * PART, half * 128:(half + 1) * 128] = jnp.where(
                    lane // PART == block, base, 0.0).astype(BF16)
        row = lax.broadcasted_iota(I32, (16, 48), 0)
        lane = lax.broadcasted_iota(I32, (16, 48), 1)
        bzf_ref[view] = fill(lane - 16 - row - shift_ref[view * 3] + radius, view, 0).astype(BF16)
        return carry

    lax.fori_loop(0, VIEWS, one_view, 0)
    row = lax.broadcasted_iota(I32, (48, 128), 0)
    lane = lax.broadcasted_iota(I32, (48, 128), 1)
    total = jnp.zeros((48, 128), F32)
    for view in range(VIEWS):
        band = fill(row - 16 - lane % 16 - shift_ref[view * 3] + radius, view, 0)
        total = jnp.where(lane // 16 == view, band, total)
    bza_ref[...] = total.astype(BF16)


def build_bands(taps, shifts):
    return pl.pallas_call(
        band_kernel,
        out_shape=(
            jax.ShapeDtypeStruct((VIEWS, ROWS, ROWS), BF16),
            jax.ShapeDtypeStruct((VIEWS, ROWS, ROWS), BF16),
            jax.ShapeDtypeStruct((VIEWS, ROWS, 128), BF16),
            jax.ShapeDtypeStruct((VIEWS, 128, ROWS), BF16),
            jax.ShapeDtypeStruct((VIEWS, 16, 48), BF16),
            jax.ShapeDtypeStruct((48, 128), BF16),
        ),
        in_specs=smem(2),
        out_specs=tuple(vmem(6)),
        name="bands",
    )(taps, shifts)


def pack_kernel(target_ref, pieces_ref, out_ref, swap_ref):
    swap_ref[...] = digit_swap((512, 512))
    count = pieces_ref.shape[0]

    def one_piece(piece, carry):
        target = target_ref[piece]
        rank = jnp.int32(0)
        for other in range(count):
            rank = rank + jnp.where((target_ref[other] == target) & (other < piece), 1, 0)
        slot = target * CAP + rank
        for half in range(2):
            planes = [pieces_ref[piece, q, :, half * 128:(half + 1) * 128] for q in range(4)]
            mixed = jnp.dot(jnp.concatenate(planes, axis=1), swap_ref[...], preferred_element_type=F32)
            for part in range(4):
                out_ref[half * 4 + part, slot] = mixed[:, part * 128:(part + 1) * 128].astype(BF16)
        return carry

    lax.fori_loop(0, count, one_piece, 0)


def pack_pieces(targets, pieces, block_count):
    return pl.pallas_call(
        pack_kernel,
        out_shape=jax.ShapeDtypeStruct((VIEWS, block_count * CAP, NY, 128), BF16),
        in_specs=smem(1) + vmem(1),
        out_specs=vmem(1)[0],
        scratch_shapes=[pltpu.VMEM((512, 512), BF16)],
        name="pack",
    )(targets, pieces)


def window_kernel(index_ref, estimate_ref, main_ref, low_ref, high_ref):
    part = index_ref[0]
    block = lane_block((NY, 128))
    lane = lax.broadcasted_iota(I32, (NY, 128), 1) % PART

    def one_plane(j, carry):
        for half in range(2):
            result = jnp.zeros((NY, 128), F32)
            for h in range(4):
                plane = estimate_ref[h * 16 + j]
                amount = (16 - PART * part - PART * half + PART * h + 512) % 256
                moved = pltpu.roll(plane, amount, 1)[:, :128]
                result = jnp.where(block == h, moved, result)
            column = (part + half) * PART - HALO + lane
            result = jnp.where((column >= 0) & (column < 256), result, 0.0)
            main_ref[half, pl.ds(j, NY, stride=16), :] = result
        return carry

    lax.fori_loop(0, 16, one_plane, 0)
    block = lane_block((16, 128))

    def pack_ends(y, carry):
        rows = pl.ds(y * 16, 16)
        left = main_ref[0, rows, :]
        right = main_ref[1, rows, :]
        low_ref[y] = jnp.where(block == 0, left, rotate(right, 32)).astype(BF16)
        high_ref[y] = jnp.where(block == 3, right, rotate(left, 96)).astype(BF16)
        return carry

    lax.fori_loop(0, NY, pack_ends, 0)


def window_estimate(index, estimate):
    return pl.pallas_call(
        window_kernel,
        out_shape=(
            jax.ShapeDtypeStruct((2, NY * 16, 128), F32),
            jax.ShapeDtypeStruct((NY, 16, 128), BF16),
            jax.ShapeDtypeStruct((NY, 16, 128), BF16),
        ),
        in_specs=smem(1) + vmem(1),
        out_specs=tuple(vmem(3)),
        name="window",
    )(index, estimate)


def tail_kernel(from_low_ref, from_high_ref, tail_ref):
    block = lane_block((16, 128))

    def one_row(y, carry):
        low = from_low_ref[y].astype(F32)
        high = from_high_ref[y].astype(F32)
        result = jnp.where(block == 0, rotate(low, 64), high)
        result = jnp.where(block == 1, rotate(high, 32), result)
        result = jnp.where(block == 2, rotate(low, 96), result)
        result = jnp.where(block == 3, rotate(high, 64), result)
        tail_ref[y] = result
        return carry

    lax.fori_loop(0, NY, one_row, 0)


def build_tail(from_low, from_high):
    return pl.pallas_call(
        tail_kernel,
        out_shape=jax.ShapeDtypeStruct((NY, 16, 128), F32),
        in_specs=vmem(2),
        out_specs=vmem(1)[0],
        name="tail",
    )(from_low, from_high)


def weight_kernel(rows_ref, main_ref, tail_ref, out_main_ref, out_tail_ref):
    def one_row(y, carry):
        for half in range(2):
            total = jnp.zeros((16, 128), F32)
            for view in range(VIEWS):
                total = total + rows_ref[view * NY + y] * main_ref[view, half]
            out_main_ref[half, pl.ds(y * 16, 16), :] = 1.0 / jnp.maximum(total, 1.0)
        total = jnp.zeros((16, 128), F32)
        for view in range(VIEWS):
            total = total + rows_ref[view * NY + y] * tail_ref[view]
        out_tail_ref[y] = 1.0 / jnp.maximum(total, 1.0)
        return carry

    lax.fori_loop(0, NY, one_row, 0)


def build_weights(rows, main, tail):
    return pl.pallas_call(
        weight_kernel,
        out_shape=(
            jax.ShapeDtypeStruct((2, NY * 16, 128), F32),
            jax.ShapeDtypeStruct((NY, 16, 128), F32),
        ),
        in_specs=smem(1) + vmem(2),
        out_specs=tuple(vmem(2)),
        name="weights",
    )(rows, main, tail)


def forward_kernel(main_ref, tail_ref, bzf_ref, ky_ref, kx_ref, out_ref, left_ref, right_ref):
    block = lane_block((16, 128))

    def along_z(y, carry):
        rows = pl.ds(y * 16, 16)
        left = main_ref[0, rows, :]
        right = main_ref[1, rows, :]
        tail = tail_ref[y]
        turned = rotate(tail, 64)
        lower = jnp.concatenate([jnp.where(block == 0, tail, rotate(left, 32)),
                                 jnp.where(block == 0, turned, rotate(right, 32))], axis=1)
        upper = jnp.concatenate([jnp.where(block == 3, turned, rotate(left, 96)),
                                 jnp.where(block == 3, tail, rotate(right, 96))], axis=1)
        stacked = jnp.concatenate([lower, jnp.concatenate([left, right], axis=1), upper], axis=0).astype(BF16)
        blurred = jnp.dot(bzf_ref[...], stacked, preferred_element_type=F32)
        left_ref[pl.ds(y, 128, stride=NY), :] = blurred[:, :128]
        right_ref[pl.ds(y, 128, stride=NY), :] = blurred[:, 128:]
        return carry

    lax.fori_loop(0, NY, along_z, 0, unroll=4)

    def in_plane(group, carry):
        rows = pl.ds(pl.multiple_of(group * ROWS, ROWS), ROWS)
        view = group // 4
        volume = jnp.concatenate([left_ref[rows, :], right_ref[rows, :]], axis=1).astype(BF16)
        along_y = jnp.dot(ky_ref[view], volume, preferred_element_type=F32).astype(BF16)
        out_ref[rows, :] = jnp.dot(along_y, kx_ref[view], preferred_element_type=F32)
        return carry

    lax.fori_loop(0, VIEWS * 4, in_plane, 0, unroll=2)


def forward(main, tail, bzf, ky, kx):
    return pl.pallas_call(
        forward_kernel,
        out_shape=jax.ShapeDtypeStruct((VIEWS * 1024, 128), F32),
        in_specs=vmem(5),
        out_specs=vmem(1)[0],
        scratch_shapes=[pltpu.VMEM((VIEWS * 1024, 128), F32)] * 2,
        name="forward",
    )(main, tail, bzf, ky, kx)


def adjoint_body(average_of, offset_ref, blurred_ref, bza_ref, kyt_ref, kxt_ref, main_ref, tail_ref, to_left_ref,
                 to_right_ref, left_ref, right_ref):
    def in_plane(group, carry):
        rows = pl.ds(pl.multiple_of(group * ROWS, ROWS), ROWS)
        view = group // 4
        quotient = (average_of(group, rows) / (blurred_ref[rows, :] + offset_ref[view])).astype(BF16)
        along_x = jnp.dot(quotient, kxt_ref[view], preferred_element_type=F32).astype(BF16)
        along_y = jnp.dot(kyt_ref[view], along_x, preferred_element_type=F32)
        left_ref[rows, :] = along_y[:, :128]
        right_ref[rows, :] = along_y[:, 128:]
        return carry

    lax.fori_loop(0, VIEWS * 4, in_plane, 0, unroll=2)
    block = lane_block((16, 128))
    low_half = block < 2

    def along_z(y):
        volume = jnp.concatenate([left_ref[pl.ds(y, 128, stride=NY), :],
                                  right_ref[pl.ds(y, 128, stride=NY), :]], axis=1).astype(BF16)
        summed = jnp.dot(bza_ref[...], volume, preferred_element_type=F32)
        mains = []
        for half in range(2):
            lanes = slice(half * 128, (half + 1) * 128)
            lower = jnp.where(block < 3, rotate(summed[:16, lanes], 96), 0.0)
            upper = jnp.where(block > 0, rotate(summed[32:, lanes], 32), 0.0)
            mains.append(summed[16:32, lanes] + lower + upper)
        tail = jnp.where(block == 0, summed[:16, :128], summed[32:, 128:])
        tail = jnp.where(block == 1, rotate(summed[32:, :128], 64), tail)
        tail = jnp.where(block == 2, rotate(summed[:16, 128:], 64), tail)
        return mains, tail

    def pair(y, carry):
        tails = []
        for row in (y, y + NY // 2):
            mains, tail = along_z(row)
            for half in range(2):
                main_ref[half, pl.ds(row * 16, 16), :] = mains[half]
            tail_ref[row] = tail
            to_left_ref[row] = mains[0].astype(BF16)
            to_right_ref[row] = mains[1].astype(BF16)
            tails.append(tail)
        to_left_ref[NY + y] = jnp.where(low_half, tails[0], rotate(tails[1], 64)).astype(BF16)
        to_right_ref[NY + y] = jnp.where(low_half, rotate(tails[0], 64), tails[1]).astype(BF16)
        return carry

    lax.fori_loop(0, NY // 2, pair, 0, unroll=2)


def first_adjoint_kernel(start_ref, order_ref, inverse_ref, offset_ref, incoming_ref, blurred_ref, bza_ref, kyt_ref,
                         kxt_ref, main_ref, tail_ref, to_left_ref, to_right_ref, average_ref, left_ref, right_ref,
                         swap_ref):
    swap_ref[...] = digit_swap((512, 512))

    def average_of(group, rows):
        view = group // 4
        remainder = group % 4
        parts = []
        for h in range(4):
            slot = view * SLOTS + h * 4 + remainder

            def add(position, total):
                return total + incoming_ref[view, order_ref[view * 32 + position]].astype(F32)

            total = lax.fori_loop(start_ref[slot + view], start_ref[slot + view + 1], add, jnp.zeros((NY, 128), F32))
            parts.append((total * inverse_ref[slot]).astype(BF16))
        mixed = jnp.dot(jnp.concatenate(parts, axis=1), swap_ref[...], preferred_element_type=F32)
        average = jnp.concatenate([mixed[:, q * 128:(q + 1) * 128] for q in range(4)], axis=0)
        average_ref[rows, :] = average.astype(BF16)
        return average

    adjoint_body(average_of, offset_ref, blurred_ref, bza_ref, kyt_ref, kxt_ref, main_ref, tail_ref, to_left_ref,
                 to_right_ref, left_ref, right_ref)


def next_adjoint_kernel(offset_ref, average_ref, blurred_ref, bza_ref, kyt_ref, kxt_ref, main_ref, tail_ref,
                        to_left_ref, to_right_ref, left_ref, right_ref):
    def average_of(group, rows):
        return average_ref[rows, :].astype(F32)

    adjoint_body(average_of, offset_ref, blurred_ref, bza_ref, kyt_ref, kxt_ref, main_ref, tail_ref, to_left_ref,
                 to_right_ref, left_ref, right_ref)


PARTIAL_SHAPES = (
    jax.ShapeDtypeStruct((2, NY * 16, 128), F32),
    jax.ShapeDtypeStruct((NY, 16, 128), F32),
    jax.ShapeDtypeStruct((NY + NY // 2, 16, 128), BF16),
    jax.ShapeDtypeStruct((NY + NY // 2, 16, 128), BF16),
)


def first_adjoint(start, order, inverse, offset, incoming, blurred, bza, kyt, kxt):
    return pl.pallas_call(
        first_adjoint_kernel,
        out_shape=PARTIAL_SHAPES + (jax.ShapeDtypeStruct((VIEWS * 1024, 128), BF16),),
        in_specs=smem(4) + vmem(5),
        out_specs=tuple(vmem(5)),
        scratch_shapes=[pltpu.VMEM((VIEWS * 1024, 128), F32)] * 2 + [pltpu.VMEM((512, 512), BF16)],
        name="first_adjoint",
    )(start, order, inverse, offset, incoming, blurred, bza, kyt, kxt)


def next_adjoint(offset, average, blurred, bza, kyt, kxt):
    return pl.pallas_call(
        next_adjoint_kernel,
        out_shape=PARTIAL_SHAPES,
        in_specs=smem(1) + vmem(5),
        out_specs=tuple(vmem(4)),
        scratch_shapes=[pltpu.VMEM((VIEWS * 1024, 128), F32)] * 2,
        name="next_adjoint",
    )(offset, average, blurred, bza, kyt, kxt)


def join_columns_kernel(main_ref, tail_ref, from_left_ref, from_right_ref, out_main_ref, out_tail_ref, low_ref,
                        high_ref):
    block = lane_block((16, 128))
    low_half = block < 2

    def pair(y, carry):
        packed_left = from_left_ref[NY + y].astype(F32)
        packed_right = from_right_ref[NY + y].astype(F32)
        for second, row in enumerate((y, y + NY // 2)):
            rows = pl.ds(row * 16, 16)
            left = main_ref[0, rows, :] + from_left_ref[row].astype(F32)
            right = main_ref[1, rows, :] + from_right_ref[row].astype(F32)
            if second:
                extra = jnp.where(low_half, rotate(packed_left, 64), packed_right)
            else:
                extra = jnp.where(low_half, packed_left, rotate(packed_right, 64))
            tail = tail_ref[row] + extra
            out_main_ref[0, rows, :] = left
            out_main_ref[1, rows, :] = right
            out_tail_ref[row] = tail
            low = jnp.where(block == 1, rotate(left, 32), tail)
            low = jnp.where(block == 3, rotate(right, 96), low)
            high = jnp.where(block == 0, rotate(left, 32), tail)
            high = jnp.where(block == 2, rotate(right, 96), high)
            low_ref[row] = low.astype(BF16)
            high_ref[row] = high.astype(BF16)
        return carry

    lax.fori_loop(0, NY // 2, pair, 0, unroll=2)


def join_columns(main, tail, from_left, from_right):
    return pl.pallas_call(
        join_columns_kernel,
        out_shape=(
            jax.ShapeDtypeStruct((2, NY * 16, 128), F32),
            jax.ShapeDtypeStruct((NY, 16, 128), F32),
            jax.ShapeDtypeStruct((NY, 16, 128), BF16),
            jax.ShapeDtypeStruct((NY, 16, 128), BF16),
        ),
        in_specs=vmem(4),
        out_specs=tuple(vmem(4)),
        name="join_columns",
    )(main, tail, from_left, from_right)


def joined_planes(y, block, main_ref, tail_ref, from_low_ref, from_high_ref):
    rows = pl.ds(y * 16, 16)
    low = from_low_ref[y].astype(F32)
    high = from_high_ref[y].astype(F32)
    left = main_ref[0, rows, :]
    left = left + jnp.where(block == 0, rotate(low, 96), 0.0) + jnp.where(block == 3, rotate(high, 96), 0.0)
    right = main_ref[1, rows, :]
    right = right + jnp.where(block == 0, rotate(low, 32), 0.0) + jnp.where(block == 3, rotate(high, 32), 0.0)
    tail = tail_ref[y] + jnp.where(block % 2 == 0, low, high)
    return left, right, tail


def update_kernel(main_ref, tail_ref, from_low_ref, from_high_ref, estimate_main_ref, estimate_tail_ref,
                  scale_main_ref, scale_tail_ref, out_main_ref, out_tail_ref):
    block = lane_block((16, 128))

    def one_row(y, carry):
        rows = pl.ds(y * 16, 16)
        left, right, tail = joined_planes(y, block, main_ref, tail_ref, from_low_ref, from_high_ref)
        out_main_ref[0, rows, :] = estimate_main_ref[0, rows, :] * left * scale_main_ref[0, rows, :]
        out_main_ref[1, rows, :] = estimate_main_ref[1, rows, :] * right * scale_main_ref[1, rows, :]
        out_tail_ref[y] = estimate_tail_ref[y] * tail * scale_tail_ref[y]
        return carry

    lax.fori_loop(0, NY, one_row, 0, unroll=4)


def update(main, tail, from_low, from_high, estimate_main, estimate_tail, scale_main, scale_tail):
    return pl.pallas_call(
        update_kernel,
        out_shape=(
            jax.ShapeDtypeStruct((2, NY * 16, 128), F32),
            jax.ShapeDtypeStruct((NY, 16, 128), F32),
        ),
        in_specs=vmem(8),
        out_specs=tuple(vmem(2)),
        name="update",
    )(main, tail, from_low, from_high, estimate_main, estimate_tail, scale_main, scale_tail)


def finish_kernel(main_ref, tail_ref, from_low_ref, from_high_ref, estimate_ref, scale_ref, out_ref):
    block = lane_block((16, 128))
    lane = lax.broadcasted_iota(I32, (16, 128), 1) % PART

    def one_row(y, carry):
        rows = pl.ds(y * 16, 16)
        left, right, _ = joined_planes(y, block, main_ref, tail_ref, from_low_ref, from_high_ref)
        left = estimate_ref[0, rows, :] * left * scale_ref[0, rows, :]
        right = estimate_ref[1, rows, :] * right * scale_ref[1, rows, :]
        out_ref[rows, :] = jnp.where(lane < HALO, rotate(left, 112), rotate(right, 16))
        return carry

    lax.fori_loop(0, NY, one_row, 0, unroll=4)


def finish(main, tail, from_low, from_high, estimate, scale):
    return pl.pallas_call(
        finish_kernel,
        out_shape=jax.ShapeDtypeStruct((NY * 16, 128), F32),
        in_specs=vmem(6),
        out_specs=vmem(1)[0],
        name="finish",
    )(main, tail, from_low, from_high, estimate, scale)


def assemble_kernel(index_ref, *refs):
    chunk_refs, out_ref, buffer_ref = refs[:8], refs[8], refs[9]
    part = index_ref[0]
    for step in range(4):
        chip = (part // 2 + step) % 4
        buffer_ref[chip * 2 + part % 2] = chunk_refs[step][...]
        buffer_ref[chip * 2 + 1 - part % 2] = chunk_refs[4 + step][...]
    block = lane_block((NY, 128))

    def one_plane(j, carry):
        for half in range(2):
            chunks = [buffer_ref[half * 4 + k, pl.ds(j, NY, stride=16), :] for k in range(4)]
            for h in range(4):
                result = rotate(chunks[0], -PART * h)
                for k in range(1, 4):
                    result = jnp.where(block == k, rotate(chunks[k], PART * (k - h)), result)
                out_ref[h * 16 + j, :, half * 128:(half + 1) * 128] = result
        return carry

    lax.fori_loop(0, 16, one_plane, 0)


def assemble(index, chunks):
    return pl.pallas_call(
        assemble_kernel,
        out_shape=jax.ShapeDtypeStruct((64, NY, 256), F32),
        in_specs=smem(1) + vmem(8),
        out_specs=vmem(1)[0],
        scratch_shapes=[pltpu.VMEM((VIEWS, NY * 16, 128), F32)],
        name="assemble",
    )(index, *chunks)


def to_neighbours(upward, downward, axis):
    count = lax.axis_size(axis)
    from_low = lax.ppermute(upward, axis, [(i, i + 1) for i in range(count - 1)])
    from_high = lax.ppermute(downward, axis, [(i + 1, i) for i in range(count - 1)])
    return from_low, from_high


def gather_parts(own):
    parts = [own] + [
        lax.ppermute(own, "view", [((i + 2 * step) % VIEWS, i) for i in range(VIEWS)]) for step in (1, 3, 2)
    ]
    parts = [parts[0], parts[1], parts[3], parts[2]]
    return parts, [lax.ppermute(part, "view", [(i, i ^ 1) for i in range(VIEWS)]) for part in parts]


def column_sums(kernel, shift, positions, length):
    radius = (TAPS - 1) // 2
    source = (positions[None, :, None] - shift[:, None, None]
              - jnp.arange(TAPS, dtype=I32)[None, None, :] + radius)
    inside = (source >= 0) & (source < length)
    return jnp.sum(jnp.where(inside, kernel[:, None, :], 0.0), axis=2)


def shards(estimate0, pieces, dest_block, slot_index, psf_shift, psf_taps, background):
    block_count = lax.axis_size("block")
    my_view = lax.axis_index("view")
    my_block = lax.axis_index("block")
    targets = dest_block[:, :, 0].reshape(VIEWS, block_count, SLOTS)
    slots = slot_index.reshape(VIEWS, block_count, SLOTS)

    own_targets = lax.dynamic_slice(targets, (my_view, my_block, 0), (1, 1, SLOTS)).reshape(SLOTS)
    outgoing = pack_pieces(own_targets, pieces[0], block_count)
    incoming = lax.all_to_all(
        outgoing.reshape(VIEWS * block_count, CAP, NY, 128), ("view", "block"), 0, 0, tiled=True
    ).reshape(VIEWS, block_count * CAP, NY, 128)

    kernel = psf_taps / jnp.sum(psf_taps, axis=2, keepdims=True)
    ky, kyt, kx, kxt, bzf, bza = build_bands(kernel.reshape(-1), psf_shift.reshape(-1))
    bzf = bzf.reshape(VIEWS * 16, 48)

    index = my_view.reshape(1).astype(I32)
    main, low, high = window_estimate(index, estimate0)
    from_low, from_high = to_neighbours(high, low, "block")
    tail = build_tail(from_low, from_high)
    blurred = forward(main, tail, bzf, ky, kx)

    earlier = jnp.tril(jnp.ones((SLOTS, SLOTS), jnp.bool_), -1)
    same = (targets[:, :, :, None] == targets[:, :, None, :]) & earlier[None, None]
    ranks = jnp.sum(same.astype(I32), axis=3)
    mine = targets == my_block
    received = jnp.arange(CAP, dtype=I32)
    slot_of = jnp.sum(
        jnp.where(mine[..., None] & (ranks[..., None] == received), slots[..., None] + 1, 0), axis=2
    ).reshape(VIEWS, block_count * CAP) - 1
    slot_ids = jnp.arange(SLOTS, dtype=I32)
    hits = slot_of[:, :, None] == slot_ids
    counts = jnp.sum(hits.astype(I32), axis=1)
    start = jnp.sum(jnp.where((slot_of[:, :, None] >= 0)
                              & (slot_of[:, :, None] < jnp.arange(SLOTS + 1, dtype=I32)), 1, 0), axis=1)
    number = jnp.arange(block_count * CAP, dtype=I32)
    before = (slot_of[:, None, :] >= 0) & (
        (slot_of[:, None, :] < slot_of[:, :, None])
        | ((slot_of[:, None, :] == slot_of[:, :, None]) & (number[None, None, :] < number[None, :, None]))
    )
    position = jnp.where(slot_of >= 0, jnp.sum(before.astype(I32), axis=2), -1)
    order = jnp.sum(jnp.where(position[:, :, None] == number, number[None, :, None], 0), axis=1)
    inverse = 1.0 / jnp.maximum(counts, 1).astype(F32)

    global_slot = (targets * SLOTS + slots).reshape(VIEWS, block_count * SLOTS)
    all_slots = jnp.arange(block_count * SLOTS, dtype=I32)
    occupied = jnp.any(global_slot[:, :, None] == all_slots, axis=1)
    mask = jnp.repeat(occupied.astype(F32), 4, axis=1)
    padded = jnp.pad(mask, ((0, 0), (2 * HALO, 2 * HALO)))
    window = lax.dynamic_slice_in_dim(padded, my_block * 64, 128, 1)
    depth = lax.broadcasted_iota(I32, (96, 128), 0) + HALO - lax.broadcasted_iota(I32, (96, 128), 1)
    tap = depth[None] - psf_shift[:, 0, None, None] + (TAPS - 1) // 2
    weight_depth = jnp.zeros((VIEWS, 96), F32)
    band = jnp.zeros((VIEWS, 96, 128), F32)
    for j in range(TAPS):
        band = jnp.where(tap == j, kernel[:, 0, j, None, None], band)
    weight_depth = jnp.sum(band * window[:, None, :], axis=2)
    weight_rows = column_sums(kernel[:, 1], psf_shift[:, 1], jnp.arange(NY, dtype=I32), NY)
    columns = my_view * PART - HALO + jnp.arange(2 * PART, dtype=I32)
    weight_columns = column_sums(kernel[:, 2], psf_shift[:, 2], columns, 256).reshape(VIEWS, 2, PART)
    by_group = weight_depth.reshape(VIEWS, 6, 16)
    planes = by_group[:, :, :, None, None] * weight_columns[:, None, None, :, :]
    planes = planes.transpose(0, 3, 2, 1, 4)
    weight_main = planes[:, :, :, 1:5].reshape(VIEWS, 2, 16, 128)
    weight_tail = jnp.stack([planes[:, :, :, 0], planes[:, :, :, 5]], axis=3)
    weight_tail = weight_tail.transpose(0, 2, 1, 3, 4).reshape(VIEWS, 16, 128)
    scale_main, scale_tail = build_weights(weight_rows.reshape(-1), weight_main, weight_tail)

    part_main, part_tail, to_left, to_right, average = first_adjoint(
        start.reshape(-1), order.reshape(-1), inverse.reshape(-1), background, incoming, blurred, bza, kyt, kxt)
    from_left, from_right = to_neighbours(to_right, to_left, "view")
    part_main, part_tail, low, high = join_columns(part_main, part_tail, from_left, from_right)
    from_low, from_high = to_neighbours(high, low, "block")
    main, tail = update(part_main, part_tail, from_low, from_high, main, tail, scale_main, scale_tail)

    blurred = forward(main, tail, bzf, ky, kx)
    part_main, part_tail, to_left, to_right = next_adjoint(background, average, blurred, bza, kyt, kxt)
    from_left, from_right = to_neighbours(to_right, to_left, "view")
    part_main, part_tail, low, high = join_columns(part_main, part_tail, from_left, from_right)
    from_low, from_high = to_neighbours(high, low, "block")
    own = finish(part_main, part_tail, from_low, from_high, main, scale_main)

    mine, partners = gather_parts(own)
    return assemble(index, mine + partners)


def solution(mesh):
    return jax.shard_map(
        shards,
        mesh=mesh,
        in_specs=(
            P("block", None, None),
            P("view", "block", None, None, None),
            P(),
            P(),
            P(),
            P(),
            P(),
        ),
        out_specs=P("block", None, None),
        check_vma=False,
    )
```

```python
import jax
import jax.numpy as jnp
from jax import lax
from jax.experimental import pallas as pl
from jax.experimental.pallas import tpu as pltpu
from jax.sharding import PartitionSpec as P


CAP = 2
TAPS = 21
HALO = 16
VIEWS = 8
SLOTS = 16
NY = 64
PART = 32
ROWS = 256
QUADS = 16

F32 = jnp.float32
BF16 = jnp.bfloat16
I32 = jnp.int32
I16 = jnp.int16


def lane_block(shape):
    return lax.broadcasted_iota(I32, shape, len(shape) - 1) // PART


def rotate(value, amount):
    return pltpu.roll(value, amount % 128, value.ndim - 1)


def digit_swap(shape):
    row = lax.broadcasted_iota(I32, shape, 0)
    column = lax.broadcasted_iota(I32, shape, 1)
    target = ((row // PART) % 4) * 128 + (row // 128) * PART + row % PART
    return jnp.where(column == target, 1.0, 0.0).astype(BF16)


def swap_fours(first, second):
    upper = lax.broadcasted_iota(I32, first.shape, 0) < 4
    return (jnp.where(upper, first, pltpu.roll(second, 4, 0)),
            jnp.where(upper, pltpu.roll(first, 4, 0), second))


def vmem(count):
    return [pl.BlockSpec(memory_space=pltpu.VMEM)] * count


def smem(count):
    return [pl.BlockSpec(memory_space=pltpu.SMEM)] * count


def to_fixed(value, scale):
    return (value * scale + 0.5).astype(I32).astype(I16)


def from_fixed(value, step):
    return value.astype(I32).astype(F32) * step


def partial_bound(offset_ref):
    total = 0.0
    for view in range(VIEWS):
        total = total + 2.0 / jnp.full((8, 128), offset_ref[view], F32)
    return total * 1.05


def band_kernel(taps_ref, shift_ref, ky_ref, kyt_ref, kx_ref, kxt_ref, bzf_ref, bza_ref):
    radius = (TAPS - 1) // 2

    def fill(difference, view, axis):
        result = jnp.zeros(difference.shape, F32)
        for tap in range(TAPS):
            result = jnp.where(difference == tap, taps_ref[(view * 3 + axis) * TAPS + tap], result)
        return result

    def one_view(view, carry):
        shift_z = shift_ref[view * 3]
        shift_y = shift_ref[view * 3 + 1]
        shift_x = shift_ref[view * 3 + 2]
        row = lax.broadcasted_iota(I32, (16, 2 * ROWS), 0)
        lane = lax.broadcasted_iota(I32, (16, 2 * ROWS), 1)
        offset = (lane // 16 - 16) * 4 + lane % 4 - row % 4
        same = (lane // 4) % 4 == row // 4
        for strip, target_ref in ((jnp.where(same, offset - shift_y + radius, -1), ky_ref),
                                  (jnp.where(same, -offset - shift_y + radius, -1), kyt_ref)):
            values = fill(strip, view, 1)
            for quad in range(QUADS):
                target_ref[view, quad * 16:(quad + 1) * 16, :] = values[
                    :, ROWS - quad * 16:2 * ROWS - quad * 16].astype(BF16)
        row = lax.broadcasted_iota(I32, (PART, 128), 0)
        lane = lax.broadcasted_iota(I32, (PART, 128), 1)
        for half in range(2):
            base = fill(half * PART + row - (lane % PART + HALO) - shift_x + radius, view, 2)
            for block in range(4):
                first = half * 128 + block * PART
                kx_ref[view, first:first + PART, :] = jnp.where(lane // PART == block, base, 0.0).astype(BF16)
            base = fill(half * PART + lane % PART - (row + HALO) - shift_x + radius, view, 2)
            for block in range(4):
                kxt_ref[view, block * PART:(block + 1) * PART, half * 128:(half + 1) * 128] = jnp.where(
                    lane // PART == block, base, 0.0).astype(BF16)
        row = lax.broadcasted_iota(I32, (64, 192), 0)
        lane = lax.broadcasted_iota(I32, (64, 192), 1)
        difference = jnp.where(lane % 4 == row % 4, lane // 4 - 16 - row // 4 - shift_z + radius, -1)
        bzf_ref[pl.ds(pl.multiple_of(view * 64, 64), 64), :] = fill(difference, view, 0).astype(BF16)
        return carry

    lax.fori_loop(0, VIEWS, one_view, 0)
    row = lax.broadcasted_iota(I32, (192, 128), 0)
    lane = lax.broadcasted_iota(I32, (192, 128), 1)
    left = lane < 64
    for pair in range(VIEWS // 2):
        shift = jnp.where(left, shift_ref[pair * 6], shift_ref[pair * 6 + 3])
        difference = jnp.where(lane % 4 == row % 4, row // 4 - 16 - (lane // 4) % 16 - shift + radius, -1)
        total = jnp.zeros((192, 128), F32)
        for tap in range(TAPS):
            value = jnp.where(left, taps_ref[pair * 6 * TAPS + tap], taps_ref[(pair * 6 + 3) * TAPS + tap])
            total = jnp.where(difference == tap, value, total)
        bza_ref[:, pair * 128:(pair + 1) * 128] = total.astype(BF16)


def build_bands(taps, shifts):
    return pl.pallas_call(
        band_kernel,
        out_shape=(
            jax.ShapeDtypeStruct((VIEWS, ROWS, ROWS), BF16),
            jax.ShapeDtypeStruct((VIEWS, ROWS, ROWS), BF16),
            jax.ShapeDtypeStruct((VIEWS, ROWS, 128), BF16),
            jax.ShapeDtypeStruct((VIEWS, 128, ROWS), BF16),
            jax.ShapeDtypeStruct((VIEWS * 64, 192), BF16),
            jax.ShapeDtypeStruct((192, VIEWS * 64), BF16),
        ),
        in_specs=smem(2),
        out_specs=tuple(vmem(6)),
        name="bands",
    )(taps, shifts)


def pack_kernel(target_ref, pieces_ref, out_ref, swap_ref):
    swap_ref[...] = digit_swap((512, 512))
    count = pieces_ref.shape[0]

    def four_pieces(group, carry):
        rows = []
        for k in range(4):
            for half in range(2):
                rows.append(jnp.concatenate(
                    [pieces_ref[group * 4 + k, q, :, half * 128:(half + 1) * 128] for q in range(4)], axis=1))
        mixed = jnp.dot(jnp.concatenate(rows, axis=0), swap_ref[...], preferred_element_type=F32).astype(BF16)
        for k in range(4):
            piece = group * 4 + k
            target = target_ref[piece]
            rank = jnp.int32(0)
            for other in range(count):
                rank = rank + jnp.where((target_ref[other] == target) & (other < piece), 1, 0)
            slot = target * CAP + rank
            for half in range(2):
                first = (k * 2 + half) * NY
                for part in range(4):
                    out_ref[half * 4 + part, slot] = mixed[first:first + NY, part * 128:(part + 1) * 128]
        return carry

    lax.fori_loop(0, count // 4, four_pieces, 0)


def pack_pieces(targets, pieces, block_count):
    return pl.pallas_call(
        pack_kernel,
        out_shape=jax.ShapeDtypeStruct((VIEWS, block_count * CAP, NY, 128), BF16),
        in_specs=smem(1) + vmem(1),
        out_specs=vmem(1)[0],
        scratch_shapes=[pltpu.VMEM((512, 512), BF16)],
        name="pack",
    )(targets, pieces)


def window_kernel(index_ref, estimate_ref, main_ref):
    part = index_ref[0]
    block = lane_block((NY, 128))
    lane = lax.broadcasted_iota(I32, (NY, 128), 1) % PART

    def two_planes(step, carry):
        for half in range(2):
            column = (part + half) * PART - HALO + lane
            inside = (column >= 0) & (column < 256)
            planes = []
            for odd in range(2):
                result = jnp.zeros((NY, 128), F32)
                for h in range(4):
                    plane = estimate_ref[h * 16 + step * 2 + odd]
                    amount = (16 - PART * part - PART * half + PART * h + 512) % 256
                    result = jnp.where(block == h, pltpu.roll(plane, amount, 1)[:, :128], result)
                planes.append(jnp.where(inside, result, 0.0))
            for m in range(8):
                low, high = swap_fours(planes[0][m * 8:m * 8 + 8], planes[1][m * 8:m * 8 + 8])
                main_ref[half, pl.ds(pl.multiple_of(m * 128 + step * 8, 8), 8), :] = low
                main_ref[half, pl.ds(pl.multiple_of(m * 128 + 64 + step * 8, 8), 8), :] = high
        return carry

    lax.fori_loop(0, 8, two_planes, 0)


def window_estimate(index, estimate):
    return pl.pallas_call(
        window_kernel,
        out_shape=jax.ShapeDtypeStruct((2, 1024, 128), F32),
        in_specs=smem(1) + vmem(1),
        out_specs=vmem(1)[0],
        name="window",
    )(index, estimate)


def ends_kernel(index_ref, first_ref, last_ref, low_ref, high_ref):
    part = index_ref[0]
    amount = (16 - PART * part + 256) % 256
    lane = lax.broadcasted_iota(I32, (32, 128), 1)
    column = part * PART - HALO + lane % 64
    inside = (column >= 0) & (column < 256)

    def four_planes(step, carry):
        for source_ref, target_ref in ((first_ref, low_ref), (last_ref, high_ref)):
            planes = []
            for k in range(4):
                plane = source_ref[step * 4 + k]
                top = pltpu.roll(plane[:32], amount, 1)[:, :128]
                bottom = pltpu.roll(plane[32:], (amount + 64) % 256, 1)[:, :128]
                planes.append(jnp.where(inside, jnp.where(lane < 64, top, bottom), 0.0))
            for m in range(4):
                rows = slice(m * 8, m * 8 + 8)
                front = swap_fours(planes[0][rows], planes[1][rows])
                back = swap_fours(planes[2][rows], planes[3][rows])
                for odd in range(2):
                    target_ref[m * 2 + odd, pl.ds(pl.multiple_of(step * 16, 16), 16), :] = jnp.concatenate(
                        [front[odd], back[odd]], axis=0).astype(BF16)
        return carry

    lax.fori_loop(0, 4, four_planes, 0)


def window_ends(index, estimate):
    return pl.pallas_call(
        ends_kernel,
        grid=(1,),
        out_shape=(jax.ShapeDtypeStruct((8, 64, 128), BF16),) * 2,
        in_specs=smem(1) + [pl.BlockSpec((16, NY, 256), lambda step: (0, 0, 0)),
                            pl.BlockSpec((16, NY, 256), lambda step: (3, 0, 0))],
        out_specs=tuple(vmem(2)),
        name="ends",
    )(index, estimate, estimate)


def build_tail(edge_ref, from_low_ref, from_high_ref, tail_ref):
    block = lane_block((64, 128))

    def two_quads(quad, carry):
        low = from_low_ref[quad].astype(F32) * edge_ref[2]
        high = from_high_ref[quad].astype(F32) * edge_ref[3]
        for member in range(2):
            base = member * 64
            result = jnp.where(block == 0, rotate(low, -base), rotate(low, 32 - base))
            result = jnp.where(block == 1, rotate(high, 32 - base), result)
            tail_ref[quad + member * 8] = jnp.where(block == 3, rotate(high, 64 - base), result)
        return carry

    lax.fori_loop(0, QUADS // 2, two_quads, 0)


def weight_kernel(rows_ref, main_ref, tail_ref, out_main_ref, out_tail_ref):
    quarter = lax.broadcasted_iota(I32, (64, 128), 0) % 4

    def one_quad(quad, carry):
        rows = pl.ds(pl.multiple_of(quad * 64, 64), 64)
        totals = [jnp.zeros((64, 128), F32) for _ in range(3)]
        for view in range(VIEWS):
            factor = jnp.full((64, 128), rows_ref[view * NY + quad * 4], F32)
            for k in range(1, 4):
                factor = jnp.where(quarter == k, rows_ref[view * NY + quad * 4 + k], factor)
            totals[0] = totals[0] + factor * main_ref[view, 0]
            totals[1] = totals[1] + factor * main_ref[view, 1]
            totals[2] = totals[2] + factor * tail_ref[view]
        out_main_ref[0, rows, :] = 1.0 / jnp.maximum(totals[0], 1.0)
        out_main_ref[1, rows, :] = 1.0 / jnp.maximum(totals[1], 1.0)
        out_tail_ref[quad] = 1.0 / jnp.maximum(totals[2], 1.0)
        return carry

    lax.fori_loop(0, QUADS, one_quad, 0)


def build_weights(rows, main, tail):
    return pl.pallas_call(
        weight_kernel,
        out_shape=(
            jax.ShapeDtypeStruct((2, 1024, 128), F32),
            jax.ShapeDtypeStruct((QUADS, 64, 128), F32),
        ),
        in_specs=smem(1) + vmem(2),
        out_specs=tuple(vmem(2)),
        name="weights",
    )(rows, main, tail)


def forward_depth(main_ref, tail_ref, bzf_ref, planes_ref):
    block = lane_block((64, 128))

    def stacked(quad):
        rows = pl.ds(pl.multiple_of(quad * 64, 64), 64)
        left = main_ref[0, rows, :]
        right = main_ref[1, rows, :]
        tail = tail_ref[quad]
        turned = rotate(tail, 64)
        lower = jnp.concatenate([jnp.where(block == 0, tail, rotate(left, 32)),
                                 jnp.where(block == 0, turned, rotate(right, 32))], axis=1)
        upper = jnp.concatenate([jnp.where(block == 3, turned, rotate(left, 96)),
                                 jnp.where(block == 3, tail, rotate(right, 96))], axis=1)
        return jnp.concatenate([lower, jnp.concatenate([left, right], axis=1), upper], axis=0).astype(BF16)

    def two_quads(step, carry):
        both = jnp.concatenate([stacked(step * 2), stacked(step * 2 + 1)], axis=1)
        blurred = jnp.dot(bzf_ref[...], both, preferred_element_type=F32).astype(BF16)
        for member in range(2):
            first = pl.multiple_of(step * 32 + member * 16, 16)
            for group in range(VIEWS * 4):
                planes_ref[group, pl.ds(first, 16), :] = blurred[
                    group * 16:(group + 1) * 16, member * ROWS:(member + 1) * ROWS]
        return carry

    lax.fori_loop(0, QUADS // 2, two_quads, 0, unroll=2)


def forward_plane(view, planes_ref, ky, kx):
    volume = planes_ref[pl.ds(view * 4, 4)].reshape(4 * ROWS, ROWS)
    along_x = jnp.concatenate([jnp.dot(volume[r * 512:(r + 1) * 512], kx, preferred_element_type=F32)
                               for r in range(2)], axis=0).astype(BF16)
    side = jnp.concatenate([along_x[r * ROWS:(r + 1) * ROWS] for r in range(4)], axis=1)
    return jnp.dot(ky, side, preferred_element_type=F32)


def adjoint_plane(view, quotient, kyt, kxt, depth_ref):
    along_y = jnp.dot(kyt, quotient.astype(BF16), preferred_element_type=F32).astype(BF16)
    stacked = jnp.concatenate([along_y[:, r * 128:(r + 1) * 128] for r in range(4)], axis=0)
    along_x = jnp.concatenate([jnp.dot(stacked[r * 512:(r + 1) * 512], kxt, preferred_element_type=F32)
                               for r in range(2)], axis=0).astype(BF16)
    for r in range(4):
        first = pl.multiple_of(view * 64 + r * 16, 16)
        for quad in range(QUADS):
            depth_ref[quad, pl.ds(first, 16), :] = along_x[r * ROWS + quad * 16:r * ROWS + quad * 16 + 16]


def adjoint_depth(scale, bza_ref, depth_ref, main_ref, tail_ref, to_left_ref, to_right_ref):
    block = lane_block((64, 128))
    low_half = block < 2

    def pair(quad, carry):
        tails = []
        members = (quad, quad + QUADS // 2)
        both = jnp.concatenate([depth_ref[member] for member in members], axis=1)
        summed_both = jnp.dot(bza_ref[...], both, preferred_element_type=F32)
        for index, member in enumerate(members):
            summed = summed_both[:, index * ROWS:(index + 1) * ROWS]
            mains = []
            for half in range(2):
                lanes = slice(half * 128, (half + 1) * 128)
                lower = jnp.where(block < 3, rotate(summed[:64, lanes], 96), 0.0)
                upper = jnp.where(block > 0, rotate(summed[128:, lanes], 32), 0.0)
                mains.append(summed[64:128, lanes] + lower + upper)
            tail = jnp.where(block == 0, summed[:64, :128], summed[128:, 128:])
            tail = jnp.where(block == 1, rotate(summed[128:, :128], 64), tail)
            tail = jnp.where(block == 2, rotate(summed[:64, 128:], 64), tail)
            rows = pl.ds(pl.multiple_of(member * 64, 64), 64)
            main_ref[0, rows, :] = mains[0]
            main_ref[1, rows, :] = mains[1]
            tail_ref[member] = tail
            to_left_ref[member] = to_fixed(mains[0], scale)
            to_right_ref[member] = to_fixed(mains[1], scale)
            tails.append(tail)
        to_left_ref[QUADS + quad] = to_fixed(jnp.where(low_half, tails[0], rotate(tails[1], 64)), scale)
        to_right_ref[QUADS + quad] = to_fixed(jnp.where(low_half, rotate(tails[0], 64), tails[1]), scale)
        return carry

    lax.fori_loop(0, QUADS // 2, pair, 0, unroll=2)


def tall(value):
    return jnp.concatenate([value] * 8, axis=0)


def forward_kernel(edge_ref, main_ref, from_low_ref, from_high_ref, bzf_ref, ky_ref, kx_ref, out_ref, tail_ref,
                   planes_ref):
    build_tail(edge_ref, from_low_ref, from_high_ref, tail_ref)
    forward_depth(main_ref, tail_ref, bzf_ref, planes_ref)

    def one_view(view, carry):
        out_ref[view] = forward_plane(view, planes_ref, ky_ref[view], kx_ref[view]).astype(BF16)
        return carry

    lax.fori_loop(0, VIEWS, one_view, 0)


def forward(edges, main, from_low, from_high, bzf, ky, kx):
    return pl.pallas_call(
        forward_kernel,
        out_shape=(
            jax.ShapeDtypeStruct((VIEWS, ROWS, 2 * ROWS), BF16),
            jax.ShapeDtypeStruct((QUADS, 64, 128), F32),
        ),
        in_specs=smem(1) + vmem(6),
        out_specs=tuple(vmem(2)),
        scratch_shapes=[pltpu.VMEM((VIEWS * 4, ROWS, ROWS), BF16)],
        name="forward",
    )(edges, main, from_low, from_high, bzf, ky, kx)


def per_view(*shape):
    return pl.BlockSpec((1,) + shape, lambda view: (view,) + (0,) * len(shape))


PARTIAL_SHAPES = (
    jax.ShapeDtypeStruct((2, 1024, 128), F32),
    jax.ShapeDtypeStruct((QUADS, 64, 128), F32),
    jax.ShapeDtypeStruct((QUADS + QUADS // 2, 64, 128), I16),
    jax.ShapeDtypeStruct((QUADS + QUADS // 2, 64, 128), I16),
)


def first_adjoint_kernel(start_ref, source_ref, place_ref, inverse_ref, offset_ref, incoming_ref, blurred_ref, kyt_ref,
                         kxt_ref, bza_ref, main_ref, tail_ref, to_left_ref, to_right_ref, average_ref, total_ref,
                         depth_ref, swap_ref):
    view = pl.program_id(0)

    @pl.when(view == 0)
    def _():
        swap_ref[...] = digit_swap((512, 512))

    for slot in range(SLOTS):
        total_ref[slot] = jnp.zeros((NY, 128), F32)

    def add(entry, carry):
        place = place_ref[entry]
        piece = incoming_ref[source_ref[entry] - view * incoming_ref.shape[0]].astype(F32)
        slot = place - view * SLOTS
        total_ref[slot] = total_ref[slot] + piece * inverse_ref[place]
        return carry

    lax.fori_loop(start_ref[view], start_ref[view + 1], add, 0)
    rows = []
    for r in range(4):
        rows.append(jnp.concatenate([total_ref[h * 4 + r].astype(BF16) for h in range(4)], axis=1))
    mixed = jnp.dot(jnp.concatenate(rows, axis=0), swap_ref[...], preferred_element_type=F32)
    for r in range(4):
        lanes = slice(r * 128, r * 128 + 128)
        for m in range(8):
            first = r * NY + m * 8
            ends = []
            for q in (0, 2):
                ends.append(swap_fours(mixed[first:first + 8, q * 128:(q + 1) * 128],
                                       mixed[first:first + 8, (q + 1) * 128:(q + 2) * 128]))
            for odd in range(2):
                quad = 2 * m + odd
                average_ref[0, quad * 16:quad * 16 + 16, lanes] = jnp.concatenate(
                    [ends[0][odd], ends[1][odd]], axis=0).astype(BF16)
    quotient = average_ref[0].astype(F32) / (blurred_ref[0].astype(F32) + offset_ref[view])
    adjoint_plane(view, quotient, kyt_ref[0], kxt_ref[0], depth_ref)

    @pl.when(view == VIEWS - 1)
    def _():
        scale = tall(32767.0 / partial_bound(offset_ref))
        adjoint_depth(scale, bza_ref, depth_ref, main_ref, tail_ref, to_left_ref, to_right_ref)


def first_adjoint(start, source, place, inverse, offset, incoming, blurred, kyt, kxt, bza):
    held = incoming.shape[0] // VIEWS
    return pl.pallas_call(
        first_adjoint_kernel,
        grid=(VIEWS,),
        out_shape=PARTIAL_SHAPES + (jax.ShapeDtypeStruct((VIEWS, ROWS, 2 * ROWS), BF16),),
        in_specs=smem(5) + [pl.BlockSpec((held, NY, 128), lambda view: (view, 0, 0)), per_view(ROWS, 2 * ROWS),
                            per_view(ROWS, ROWS), per_view(128, ROWS)] + vmem(1),
        out_specs=tuple(vmem(4)) + (per_view(ROWS, 2 * ROWS),),
        scratch_shapes=[pltpu.VMEM((SLOTS, NY, 128), F32), pltpu.VMEM((QUADS, VIEWS * 64, ROWS), BF16),
                        pltpu.VMEM((512, 512), BF16)],
        name="first_adjoint",
    )(start, source, place, inverse, offset, incoming, blurred, kyt, kxt, bza)


def join_columns_kernel(offset_ref, edge_ref, main_ref, tail_ref, from_left_ref, from_right_ref, out_main_ref, out_tail_ref,
                        low_ref, high_ref):
    block = lane_block((64, 128))
    low_half = block < 2
    bound = partial_bound(offset_ref)
    scale = tall(32767.0 / bound)
    left_step = tall(bound * (edge_ref[0] / 32767.0))
    right_step = tall(bound * (edge_ref[1] / 32767.0))

    def pair(quad, carry):
        packed_left = from_fixed(from_left_ref[QUADS + quad], left_step)
        packed_right = from_fixed(from_right_ref[QUADS + quad], right_step)
        for second, member in enumerate((quad, quad + QUADS // 2)):
            rows = pl.ds(pl.multiple_of(member * 64, 64), 64)
            left = main_ref[0, rows, :] + from_fixed(from_left_ref[member], left_step)
            right = main_ref[1, rows, :] + from_fixed(from_right_ref[member], right_step)
            if second:
                extra = jnp.where(low_half, rotate(packed_left, 64), packed_right)
            else:
                extra = jnp.where(low_half, packed_left, rotate(packed_right, 64))
            tail = tail_ref[member] + extra
            out_main_ref[0, rows, :] = left
            out_main_ref[1, rows, :] = right
            out_tail_ref[member] = tail
            low = jnp.where(block == 1, rotate(left, 32), tail)
            low = jnp.where(block == 3, rotate(right, 96), low)
            high = jnp.where(block == 0, rotate(left, 32), tail)
            high = jnp.where(block == 2, rotate(right, 96), high)
            low_ref[member] = to_fixed(low, scale)
            high_ref[member] = to_fixed(high, scale)
        return carry

    lax.fori_loop(0, QUADS // 2, pair, 0)


def join_columns(offset, edges, main, tail, from_left, from_right):
    return pl.pallas_call(
        join_columns_kernel,
        out_shape=(
            jax.ShapeDtypeStruct((2, 1024, 128), F32),
            jax.ShapeDtypeStruct((QUADS, 64, 128), F32),
            jax.ShapeDtypeStruct((QUADS, 64, 128), I16),
            jax.ShapeDtypeStruct((QUADS, 64, 128), I16),
        ),
        in_specs=smem(2) + vmem(4),
        out_specs=tuple(vmem(4)),
        name="join_columns",
    )(offset, edges, main, tail, from_left, from_right)


def joined_planes(quad, steps, block, main_ref, tail_ref, from_low_ref, from_high_ref):
    rows = pl.ds(pl.multiple_of(quad * 64, 64), 64)
    low = from_fixed(from_low_ref[quad], steps[0])
    high = from_fixed(from_high_ref[quad], steps[1])
    left = main_ref[0, rows, :]
    left = left + jnp.where(block == 0, rotate(low, 96), 0.0) + jnp.where(block == 3, rotate(high, 96), 0.0)
    right = main_ref[1, rows, :]
    right = right + jnp.where(block == 0, rotate(low, 32), 0.0) + jnp.where(block == 3, rotate(high, 32), 0.0)
    if tail_ref is None:
        return rows, left, right
    tail = tail_ref[quad] + jnp.where(block % 2 == 0, low, high)
    return rows, left, right, tail


def depth_steps(bound, edge_ref):
    return tall(bound * (edge_ref[2] / 32767.0)), tall(bound * (edge_ref[3] / 32767.0))


def second_kernel(offset_ref, edge_ref, part_main_ref, part_tail_ref, from_low_ref, from_high_ref, estimate_main_ref,
                  estimate_tail_ref, scale_main_ref, scale_tail_ref, bzf_ref, bza_ref, average_ref, ky_ref, kx_ref,
                  kyt_ref, kxt_ref, out_estimate_ref, main_ref, tail_ref, to_left_ref, to_right_ref, tail_estimate_ref,
                  planes_ref, depth_ref):
    view = pl.program_id(0)

    @pl.when(view == 0)
    def _():
        block = lane_block((64, 128))
        steps = depth_steps(partial_bound(offset_ref), edge_ref)

        def renew(quad, carry):
            rows, left, right, tail = joined_planes(
                quad, steps, block, part_main_ref, part_tail_ref, from_low_ref, from_high_ref)
            out_estimate_ref[0, rows, :] = estimate_main_ref[0, rows, :] * left * scale_main_ref[0, rows, :]
            out_estimate_ref[1, rows, :] = estimate_main_ref[1, rows, :] * right * scale_main_ref[1, rows, :]
            tail_estimate_ref[quad] = estimate_tail_ref[quad] * tail * scale_tail_ref[quad]
            return carry

        lax.fori_loop(0, QUADS, renew, 0)
        forward_depth(out_estimate_ref, tail_estimate_ref, bzf_ref, planes_ref)

    blurred = forward_plane(view, planes_ref, ky_ref[0], kx_ref[0]) + offset_ref[view]
    adjoint_plane(view, average_ref[0].astype(F32) / blurred, kyt_ref[0], kxt_ref[0], depth_ref)

    @pl.when(view == VIEWS - 1)
    def _():
        scale = tall(32767.0 / partial_bound(offset_ref))
        adjoint_depth(scale, bza_ref, depth_ref, main_ref, tail_ref, to_left_ref, to_right_ref)


def second(offset, edges, *operands):
    return pl.pallas_call(
        second_kernel,
        grid=(VIEWS,),
        out_shape=(jax.ShapeDtypeStruct((2, 1024, 128), F32),) + PARTIAL_SHAPES,
        in_specs=smem(2) + vmem(10) + [per_view(ROWS, 2 * ROWS), per_view(ROWS, ROWS), per_view(ROWS, 128),
                                       per_view(ROWS, ROWS), per_view(128, ROWS)],
        out_specs=tuple(vmem(5)),
        scratch_shapes=[pltpu.VMEM((QUADS, 64, 128), F32), pltpu.VMEM((VIEWS * 4, ROWS, ROWS), BF16),
                        pltpu.VMEM((QUADS, VIEWS * 64, ROWS), BF16)],
        name="second",
    )(offset, edges, *operands)


def finish_kernel(offset_ref, edge_ref, main_ref, from_low_ref, from_high_ref, estimate_ref, scale_ref, out_ref,
                  value_ref):
    block = lane_block((64, 128))
    lane = lax.broadcasted_iota(I32, (64, 128), 1) % PART
    steps = depth_steps(partial_bound(offset_ref), edge_ref)

    def one_quad(quad, largest):
        rows, left, right = joined_planes(quad, steps, block, main_ref, None, from_low_ref, from_high_ref)
        left = estimate_ref[0, rows, :] * left * scale_ref[0, rows, :]
        right = estimate_ref[1, rows, :] * right * scale_ref[1, rows, :]
        value = jnp.where(lane < HALO, rotate(left, 112), rotate(right, 16))
        value_ref[rows, :] = value
        return jnp.maximum(largest, value)

    largest = lax.fori_loop(0, QUADS, one_quad, jnp.zeros((64, 128), F32))
    unit = (jnp.max(largest) * 64.0).astype(I32) + 1
    vector = jnp.full((16, 128), unit, I32)
    out_ref[1024:1040, :] = (vector >> 15).astype(I16)
    out_ref[1040:1056, :] = (vector & 32767).astype(I16)
    factor = (32767.0 * 64.0) / tall(vector[:8].astype(F32))

    def round_quad(quad, carry):
        rows = pl.ds(pl.multiple_of(quad * 64, 64), 64)
        out_ref[rows, :] = to_fixed(value_ref[rows, :], factor)
        return carry

    lax.fori_loop(0, QUADS, round_quad, 0)


def finish(offset, edges, main, from_low, from_high, estimate, scale):
    return pl.pallas_call(
        finish_kernel,
        out_shape=jax.ShapeDtypeStruct((1056, 128), I16),
        in_specs=smem(2) + vmem(5),
        out_specs=vmem(1)[0],
        scratch_shapes=[pltpu.VMEM((1024, 128), F32)],
        name="finish",
    )(offset, edges, main, from_low, from_high, estimate, scale)


def assemble_kernel(index_ref, *refs):
    chunk_refs, out_ref, buffer_ref = refs[:8], refs[8], refs[9]
    part = index_ref[0]

    @pl.when(pl.program_id(0) == 0)
    def _():
        for place in range(8):
            owner = ((part // 2 + place % 4) % 4) * 2 + (part % 2 if place < 4 else 1 - part % 2)
            buffer_ref[owner] = chunk_refs[place][...]

    units = []
    for k in range(8):
        digits = buffer_ref[k, 1024:1040, :].astype(I32) * 32768 + buffer_ref[k, 1040:1056, :].astype(I32)
        units.append(digits.astype(F32) * (1.0 / (64.0 * 32767.0)))
    block = lane_block((8, 128))
    even = block % 2 == 0
    first = pl.multiple_of(pl.program_id(0) * 16, 16)

    def eight_rows(m, carry):
        low = pl.ds(pl.multiple_of(m * 128 + first, 16), 16)
        high = pl.ds(pl.multiple_of(m * 128 + 64 + first, 16), 16)
        for half in range(2):
            values = []
            for k in range(4):
                place = half * 4 + k
                below = from_fixed(buffer_ref[place, low, :], units[place])
                above = from_fixed(buffer_ref[place, high, :], units[place])
                values.append(swap_fours(below[:8], above[:8]) + swap_fours(below[8:], above[8:]))
            for j in range(4):
                c0, c1, c2, c3 = (values[k][j] for k in range(4))
                a0 = jnp.where(block < 2, c0, rotate(c2, 64))
                a1 = jnp.where(block < 2, c1, rotate(c3, 64))
                a2 = jnp.where(block < 2, rotate(c0, 64), c2)
                a3 = jnp.where(block < 2, rotate(c1, 64), c3)
                results = (jnp.where(even, a0, rotate(a1, 32)), jnp.where(even, rotate(a0, 96), a1),
                           jnp.where(even, a2, rotate(a3, 32)), jnp.where(even, rotate(a2, 96), a3))
                for h in range(4):
                    out_ref[h, 0, j, pl.ds(pl.multiple_of(m * 8, 8), 8), half * 128:(half + 1) * 128] = results[h]
        return carry

    lax.fori_loop(0, 8, eight_rows, 0)


def assemble(index, chunks):
    return pl.pallas_call(
        assemble_kernel,
        grid=(4,),
        out_shape=jax.ShapeDtypeStruct((4, 4, 4, NY, 256), F32),
        in_specs=smem(1) + vmem(8),
        out_specs=pl.BlockSpec((4, 1, 4, NY, 256), lambda step: (0, step, 0, 0, 0)),
        scratch_shapes=[pltpu.VMEM((VIEWS, 1056, 128), I16)],
        name="assemble",
    )(index, *chunks).reshape(64, NY, 256)


def to_neighbours(upward, downward, axis):
    count = lax.axis_size(axis)
    from_low = lax.ppermute(upward, axis, [(i, (i + 1) % count) for i in range(count)])
    from_high = lax.ppermute(downward, axis, [((i + 1) % count, i) for i in range(count)])
    return from_low, from_high


def gather_parts(own):
    parts = [own] + [
        lax.ppermute(own, "view", [((i + 2 * step) % VIEWS, i) for i in range(VIEWS)]) for step in (1, 3, 2)
    ]
    parts = [parts[0], parts[1], parts[3], parts[2]]
    return parts, [lax.ppermute(part, "view", [(i, i ^ 1) for i in range(VIEWS)]) for part in parts]


def column_sums(kernel, shift, positions, length):
    radius = (TAPS - 1) // 2
    source = (positions[None, :, None] - shift[:, None, None]
              - jnp.arange(TAPS, dtype=I32)[None, None, :] + radius)
    inside = (source >= 0) & (source < length)
    return jnp.sum(jnp.where(inside, kernel[:, None, :], 0.0), axis=2)


def program(estimate0, pieces, dest_block, slot_index, psf_shift, psf_taps, background):
    block_count = lax.axis_size("block")
    my_view = lax.axis_index("view")
    my_block = lax.axis_index("block")
    edges = jnp.stack([my_view > 0, my_view < VIEWS - 1, my_block > 0, my_block < block_count - 1]).astype(F32)
    targets = dest_block[:, :, 0].reshape(VIEWS, block_count, SLOTS)
    slots = slot_index.reshape(VIEWS, block_count, SLOTS)

    index = my_view.reshape(1).astype(I32)
    low, high = window_ends(index, estimate0)
    from_low, from_high = to_neighbours(high, low, "block")

    own_targets = lax.dynamic_slice(targets, (my_view, my_block, 0), (1, 1, SLOTS)).reshape(SLOTS)
    own_targets, low, high = lax.optimization_barrier((own_targets, low, high))
    outgoing = pack_pieces(own_targets, pieces[0], block_count)
    incoming = lax.all_to_all(outgoing.reshape(VIEWS * block_count, CAP, NY, 128), ("view", "block"), 0, 0, tiled=True)
    incoming = incoming.reshape(VIEWS * block_count * CAP, NY, 128)

    main = window_estimate(index, estimate0)
    kernel = psf_taps / jnp.sum(psf_taps, axis=2, keepdims=True)
    ky, kyt, kx, kxt, bzf, bza = build_bands(kernel.reshape(-1), psf_shift.reshape(-1))
    blurred, tail = forward(edges, main, from_low, from_high, bzf, ky, kx)

    earlier = jnp.tril(jnp.ones((SLOTS, SLOTS), jnp.bool_), -1)
    same = (targets[:, :, :, None] == targets[:, :, None, :]) & earlier[None, None]
    ranks = jnp.sum(same.astype(I32), axis=3)
    mine = targets == my_block
    received = jnp.arange(CAP, dtype=I32)
    slot_of = jnp.sum(
        jnp.where(mine[..., None] & (ranks[..., None] == received), slots[..., None] + 1, 0), axis=2
    ).reshape(VIEWS, block_count * CAP) - 1
    hits = slot_of[:, :, None] == jnp.arange(SLOTS, dtype=I32)
    counts = jnp.sum(hits.astype(I32), axis=1)
    inverse = 1.0 / jnp.maximum(counts, 1).astype(F32)
    entries = VIEWS * block_count * CAP
    number = jnp.arange(entries, dtype=I32)
    place_of = jnp.where(slot_of >= 0, slot_of + jnp.arange(VIEWS, dtype=I32)[:, None] * SLOTS, -1).reshape(entries)
    before = (place_of[None, :] >= 0) & (number[None, :] < number[:, None])
    position = jnp.where(place_of >= 0, jnp.sum(before.astype(I32), axis=1), -1)
    chosen = position[:, None] == number[None, :]
    source = jnp.sum(jnp.where(chosen, number[:, None], 0), axis=0)
    place = jnp.sum(jnp.where(chosen, place_of[:, None], 0), axis=0)
    start = jnp.sum(((place_of >= 0)[:, None]
                     & (number[:, None] // (block_count * CAP) < jnp.arange(VIEWS + 1))).astype(I32), axis=0)

    global_slot = (targets * SLOTS + slots).reshape(VIEWS, block_count * SLOTS)
    all_slots = jnp.arange(block_count * SLOTS, dtype=I32)
    occupied = jnp.any(global_slot[:, :, None] == all_slots, axis=1)
    mask = jnp.repeat(occupied.astype(F32), 4, axis=1)
    padded = jnp.pad(mask, ((0, 0), (2 * HALO, 2 * HALO)))
    window = lax.dynamic_slice_in_dim(padded, my_block * 64, 128, 1)
    depth = lax.broadcasted_iota(I32, (96, 128), 0) + HALO - lax.broadcasted_iota(I32, (96, 128), 1)
    tap = depth[None] - psf_shift[:, 0, None, None] + (TAPS - 1) // 2
    weight_depth = jnp.zeros((VIEWS, 96), F32)
    band = jnp.zeros((VIEWS, 96, 128), F32)
    for j in range(TAPS):
        band = jnp.where(tap == j, kernel[:, 0, j, None, None], band)
    weight_depth = jnp.sum(band * window[:, None, :], axis=2)
    weight_rows = column_sums(kernel[:, 1], psf_shift[:, 1], jnp.arange(NY, dtype=I32), NY)
    columns = my_view * PART - HALO + jnp.arange(2 * PART, dtype=I32)
    weight_columns = column_sums(kernel[:, 2], psf_shift[:, 2], columns, 256).reshape(VIEWS, 2, PART)
    by_group = weight_depth.reshape(VIEWS, 6, 16)
    planes = by_group[:, :, :, None, None] * weight_columns[:, None, None, :, :]
    planes = planes.transpose(0, 3, 2, 1, 4)
    weight_main = planes[:, :, :, 1:5].reshape(VIEWS, 2, 16, 128)
    weight_tail = jnp.stack([planes[:, :, :, 0], planes[:, :, :, 5]], axis=3)
    weight_tail = weight_tail.transpose(0, 2, 1, 3, 4).reshape(VIEWS, 16, 128)
    scale_main, scale_tail = build_weights(
        weight_rows.reshape(-1), jnp.repeat(weight_main, 4, axis=2), jnp.repeat(weight_tail, 4, axis=1))

    part_main, part_tail, to_left, to_right, average = first_adjoint(
        start, source, place, inverse.reshape(-1), background, incoming, blurred, kyt, kxt, bza)
    from_left, from_right = to_neighbours(to_right, to_left, "view")
    part_main, part_tail, low, high = join_columns(background, edges, part_main, part_tail, from_left, from_right)
    from_low, from_high = to_neighbours(high, low, "block")

    main, part_main, part_tail, to_left, to_right = second(
        background, edges, part_main, part_tail, from_low, from_high, main, tail, scale_main, scale_tail,
        bzf, bza, average, ky, kx, kyt, kxt)
    from_left, from_right = to_neighbours(to_right, to_left, "view")
    part_main, part_tail, low, high = join_columns(background, edges, part_main, part_tail, from_left, from_right)
    from_low, from_high = to_neighbours(high, low, "block")
    own = finish(background, edges, part_main, from_low, from_high, main, scale_main)

    mine, partners = gather_parts(own)
    return assemble(index, mine + partners)


def solution(mesh):
    return jax.shard_map(
        program,
        mesh=mesh,
        in_specs=(
            P("block", None, None),
            P("view", "block", None, None, None),
            P(),
            P(),
            P(),
            P(),
            P(),
        ),
        out_specs=P("block", None, None),
        check_vma=False,
    )
```

```python
import jax
import jax.numpy as jnp
from jax import lax
from jax.experimental import pallas as pl
from jax.experimental.pallas import tpu as pltpu
from jax.sharding import PartitionSpec as P


CAP = 2
TAPS = 21
HALO = 16
VIEWS = 8
SLOTS = 16
NY = 64
PART = 32
ROWS = 256
QUADS = 16

F32 = jnp.float32
BF16 = jnp.bfloat16
I32 = jnp.int32
I16 = jnp.int16


def lane_block(shape):
    return lax.broadcasted_iota(I32, shape, len(shape) - 1) // PART


def rotate(value, amount):
    return pltpu.roll(value, amount % 128, value.ndim - 1)


def digit_swap(shape):
    row = lax.broadcasted_iota(I32, shape, 0)
    column = lax.broadcasted_iota(I32, shape, 1)
    target = ((row // PART) % 4) * 128 + (row // 128) * PART + row % PART
    return jnp.where(column == target, 1.0, 0.0).astype(BF16)


def swap_fours(first, second):
    upper = lax.broadcasted_iota(I32, first.shape, 0) < 4
    return (jnp.where(upper, first, pltpu.roll(second, 4, 0)),
            jnp.where(upper, pltpu.roll(first, 4, 0), second))


def held(shape, dtype):
    return pltpu.VMEM(shape, dtype)


def stay(*arrays):
    return tuple(pltpu.with_memory_space_constraint(array, pltpu.VMEM) for array in arrays)


def room(mebibytes):
    return pltpu.CompilerParams(vmem_limit_bytes=mebibytes << 20)


def vmem(count):
    return [pl.BlockSpec(memory_space=pltpu.VMEM)] * count


def smem(count):
    return [pl.BlockSpec(memory_space=pltpu.SMEM)] * count


def to_fixed(value, scale):
    return (value * scale + 0.5).astype(I32).astype(I16)


def from_fixed(value, step):
    return value.astype(I32).astype(F32) * step


def partial_bound(offset_ref):
    total = 0.0
    for view in range(VIEWS):
        total = total + 2.0 / jnp.full((8, 128), offset_ref[view], F32)
    return total * 1.05


def band_kernel(taps_ref, shift_ref, ky_ref, kyt_ref, kx_ref, kxt_ref, bzf_ref, bza_ref):
    radius = (TAPS - 1) // 2

    def fill(difference, view, axis):
        result = jnp.zeros(difference.shape, F32)
        for tap in range(TAPS):
            result = jnp.where(difference == tap, taps_ref[(view * 3 + axis) * TAPS + tap], result)
        return result

    def one_view(view, carry):
        shift_z = shift_ref[view * 3]
        shift_y = shift_ref[view * 3 + 1]
        shift_x = shift_ref[view * 3 + 2]
        row = lax.broadcasted_iota(I32, (16, 2 * ROWS), 0)
        lane = lax.broadcasted_iota(I32, (16, 2 * ROWS), 1)
        offset = (lane // 16 - 16) * 4 + lane % 4 - row % 4
        same = (lane // 4) % 4 == row // 4
        for strip, target_ref in ((jnp.where(same, offset - shift_y + radius, -1), ky_ref),
                                  (jnp.where(same, -offset - shift_y + radius, -1), kyt_ref)):
            values = fill(strip, view, 1)
            for quad in range(QUADS):
                target_ref[view, quad * 16:(quad + 1) * 16, :] = values[
                    :, ROWS - quad * 16:2 * ROWS - quad * 16].astype(BF16)
        row = lax.broadcasted_iota(I32, (PART, 128), 0)
        lane = lax.broadcasted_iota(I32, (PART, 128), 1)
        for half in range(2):
            base = fill(half * PART + row - (lane % PART + HALO) - shift_x + radius, view, 2)
            for block in range(4):
                first = half * 128 + block * PART
                kx_ref[view, first:first + PART, :] = jnp.where(lane // PART == block, base, 0.0).astype(BF16)
            base = fill(half * PART + lane % PART - (row + HALO) - shift_x + radius, view, 2)
            for block in range(4):
                kxt_ref[view, block * PART:(block + 1) * PART, half * 128:(half + 1) * 128] = jnp.where(
                    lane // PART == block, base, 0.0).astype(BF16)
        row = lax.broadcasted_iota(I32, (64, 192), 0)
        lane = lax.broadcasted_iota(I32, (64, 192), 1)
        difference = jnp.where(lane % 4 == row % 4, lane // 4 - 16 - row // 4 - shift_z + radius, -1)
        bzf_ref[pl.ds(pl.multiple_of(view * 64, 64), 64), :] = fill(difference, view, 0).astype(BF16)
        return carry

    lax.fori_loop(0, VIEWS, one_view, 0)
    row = lax.broadcasted_iota(I32, (192, 128), 0)
    lane = lax.broadcasted_iota(I32, (192, 128), 1)
    left = lane < 64
    for pair in range(VIEWS // 2):
        shift = jnp.where(left, shift_ref[pair * 6], shift_ref[pair * 6 + 3])
        difference = jnp.where(lane % 4 == row % 4, row // 4 - 16 - (lane // 4) % 16 - shift + radius, -1)
        total = jnp.zeros((192, 128), F32)
        for tap in range(TAPS):
            value = jnp.where(left, taps_ref[pair * 6 * TAPS + tap], taps_ref[(pair * 6 + 3) * TAPS + tap])
            total = jnp.where(difference == tap, value, total)
        bza_ref[:, pair * 128:(pair + 1) * 128] = total.astype(BF16)


def build_bands(taps, shifts):
    return pl.pallas_call(
        band_kernel,
        out_shape=(
            jax.ShapeDtypeStruct((VIEWS, ROWS, ROWS), BF16),
            jax.ShapeDtypeStruct((VIEWS, ROWS, ROWS), BF16),
            jax.ShapeDtypeStruct((VIEWS, ROWS, 128), BF16),
            jax.ShapeDtypeStruct((VIEWS, 128, ROWS), BF16),
            jax.ShapeDtypeStruct((VIEWS * 64, 192), BF16),
            jax.ShapeDtypeStruct((192, VIEWS * 64), BF16),
        ),
        in_specs=smem(2),
        out_specs=tuple(vmem(6)),
        name="bands",
    )(taps, shifts)


def pack_kernel(target_ref, pieces_ref, out_ref, swap_ref):
    swap_ref[...] = digit_swap((512, 512))
    count = pieces_ref.shape[0]

    def four_pieces(group, carry):
        rows = []
        for k in range(4):
            for half in range(2):
                rows.append(jnp.concatenate(
                    [pieces_ref[group * 4 + k, q, :, half * 128:(half + 1) * 128] for q in range(4)], axis=1))
        mixed = jnp.dot(jnp.concatenate(rows, axis=0), swap_ref[...], preferred_element_type=F32).astype(BF16)
        for k in range(4):
            piece = group * 4 + k
            target = target_ref[piece]
            rank = jnp.int32(0)
            for other in range(count):
                rank = rank + jnp.where((target_ref[other] == target) & (other < piece), 1, 0)
            slot = target * CAP + rank
            for half in range(2):
                first = (k * 2 + half) * NY
                for part in range(4):
                    out_ref[half * 4 + part, slot] = mixed[first:first + NY, part * 128:(part + 1) * 128]
        return carry

    lax.fori_loop(0, count // 4, four_pieces, 0)


def pack_pieces(targets, pieces, block_count):
    return pl.pallas_call(
        pack_kernel,
        out_shape=jax.ShapeDtypeStruct((VIEWS, block_count * CAP, NY, 128), BF16),
        in_specs=smem(1) + vmem(1),
        out_specs=vmem(1)[0],
        scratch_shapes=[pltpu.VMEM((512, 512), BF16)],
        name="pack",
    )(targets, pieces)


def window_kernel(index_ref, estimate_ref, main_ref):
    part = index_ref[0]
    block = lane_block((NY, 128))
    lane = lax.broadcasted_iota(I32, (NY, 128), 1) % PART

    def two_planes(step, carry):
        for half in range(2):
            column = (part + half) * PART - HALO + lane
            inside = (column >= 0) & (column < 256)
            planes = []
            for odd in range(2):
                result = jnp.zeros((NY, 128), F32)
                for h in range(4):
                    plane = estimate_ref[h * 16 + step * 2 + odd]
                    amount = (16 - PART * part - PART * half + PART * h + 512) % 256
                    result = jnp.where(block == h, pltpu.roll(plane, amount, 1)[:, :128], result)
                planes.append(jnp.where(inside, result, 0.0))
            for m in range(8):
                low, high = swap_fours(planes[0][m * 8:m * 8 + 8], planes[1][m * 8:m * 8 + 8])
                main_ref[half, pl.ds(pl.multiple_of(m * 128 + step * 8, 8), 8), :] = low
                main_ref[half, pl.ds(pl.multiple_of(m * 128 + 64 + step * 8, 8), 8), :] = high
        return carry

    lax.fori_loop(0, 8, two_planes, 0)


def window_estimate(index, estimate):
    return pl.pallas_call(
        window_kernel,
        out_shape=jax.ShapeDtypeStruct((2, 1024, 128), F32),
        in_specs=smem(1) + vmem(1),
        out_specs=vmem(1)[0],
        name="window",
    )(index, estimate)


def ends_kernel(index_ref, first_ref, last_ref, low_ref, high_ref):
    part = index_ref[0]
    amount = (16 - PART * part + 256) % 256
    lane = lax.broadcasted_iota(I32, (32, 128), 1)
    column = part * PART - HALO + lane % 64
    inside = (column >= 0) & (column < 256)

    def four_planes(step, carry):
        for source_ref, target_ref in ((first_ref, low_ref), (last_ref, high_ref)):
            planes = []
            for k in range(4):
                plane = source_ref[step * 4 + k]
                top = pltpu.roll(plane[:32], amount, 1)[:, :128]
                bottom = pltpu.roll(plane[32:], (amount + 64) % 256, 1)[:, :128]
                planes.append(jnp.where(inside, jnp.where(lane < 64, top, bottom), 0.0))
            for m in range(4):
                rows = slice(m * 8, m * 8 + 8)
                front = swap_fours(planes[0][rows], planes[1][rows])
                back = swap_fours(planes[2][rows], planes[3][rows])
                for odd in range(2):
                    target_ref[m * 2 + odd, pl.ds(pl.multiple_of(step * 16, 16), 16), :] = jnp.concatenate(
                        [front[odd], back[odd]], axis=0).astype(BF16)
        return carry

    lax.fori_loop(0, 4, four_planes, 0)


def window_ends(index, estimate):
    return pl.pallas_call(
        ends_kernel,
        grid=(1,),
        out_shape=(jax.ShapeDtypeStruct((8, 64, 128), BF16),) * 2,
        in_specs=smem(1) + [pl.BlockSpec((16, NY, 256), lambda step: (0, 0, 0)),
                            pl.BlockSpec((16, NY, 256), lambda step: (3, 0, 0))],
        out_specs=tuple(vmem(2)),
        name="ends",
    )(index, estimate, estimate)


def build_tail(edge_ref, from_low_ref, from_high_ref, tail_ref):
    block = lane_block((64, 128))

    def two_quads(quad, carry):
        low = from_low_ref[quad].astype(F32) * edge_ref[2]
        high = from_high_ref[quad].astype(F32) * edge_ref[3]
        for member in range(2):
            base = member * 64
            result = jnp.where(block == 0, rotate(low, -base), rotate(low, 32 - base))
            result = jnp.where(block == 1, rotate(high, 32 - base), result)
            tail_ref[quad + member * 8] = jnp.where(block == 3, rotate(high, 64 - base), result)
        return carry

    lax.fori_loop(0, QUADS // 2, two_quads, 0)


def weight_kernel(rows_ref, main_ref, tail_ref, out_main_ref, out_tail_ref):
    quarter = lax.broadcasted_iota(I32, (64, 128), 0) % 4

    def one_quad(quad, carry):
        rows = pl.ds(pl.multiple_of(quad * 64, 64), 64)
        totals = [jnp.zeros((64, 128), F32) for _ in range(3)]
        for view in range(VIEWS):
            factor = jnp.full((64, 128), rows_ref[view * NY + quad * 4], F32)
            for k in range(1, 4):
                factor = jnp.where(quarter == k, rows_ref[view * NY + quad * 4 + k], factor)
            totals[0] = totals[0] + factor * main_ref[view, 0]
            totals[1] = totals[1] + factor * main_ref[view, 1]
            totals[2] = totals[2] + factor * tail_ref[view]
        out_main_ref[0, rows, :] = 1.0 / jnp.maximum(totals[0], 1.0)
        out_main_ref[1, rows, :] = 1.0 / jnp.maximum(totals[1], 1.0)
        out_tail_ref[quad] = 1.0 / jnp.maximum(totals[2], 1.0)
        return carry

    lax.fori_loop(0, QUADS, one_quad, 0)


def build_weights(rows, main, tail):
    return pl.pallas_call(
        weight_kernel,
        out_shape=(
            jax.ShapeDtypeStruct((2, 1024, 128), F32),
            jax.ShapeDtypeStruct((QUADS, 64, 128), F32),
        ),
        in_specs=smem(1) + vmem(2),
        out_specs=tuple(vmem(2)),
        name="weights",
    )(rows, main, tail)


def forward_depth(main_ref, tail_ref, bzf_ref, planes_ref):
    block = lane_block((64, 128))

    def stacked(quad):
        rows = pl.ds(pl.multiple_of(quad * 64, 64), 64)
        left = main_ref[0, rows, :]
        right = main_ref[1, rows, :]
        tail = tail_ref[quad]
        turned = rotate(tail, 64)
        lower = jnp.concatenate([jnp.where(block == 0, tail, rotate(left, 32)),
                                 jnp.where(block == 0, turned, rotate(right, 32))], axis=1)
        upper = jnp.concatenate([jnp.where(block == 3, turned, rotate(left, 96)),
                                 jnp.where(block == 3, tail, rotate(right, 96))], axis=1)
        return jnp.concatenate([lower, jnp.concatenate([left, right], axis=1), upper], axis=0).astype(BF16)

    def two_quads(step, carry):
        both = jnp.concatenate([stacked(step * 2), stacked(step * 2 + 1)], axis=1)
        blurred = jnp.dot(bzf_ref[...], both, preferred_element_type=F32).astype(BF16)
        for member in range(2):
            first = pl.multiple_of(step * 32 + member * 16, 16)
            for group in range(VIEWS * 4):
                planes_ref[group, pl.ds(first, 16), :] = blurred[
                    group * 16:(group + 1) * 16, member * ROWS:(member + 1) * ROWS]
        return carry

    lax.fori_loop(0, QUADS // 2, two_quads, 0, unroll=2)


def forward_plane(view, planes_ref, ky, kx):
    volume = planes_ref[pl.ds(view * 4, 4)].reshape(4 * ROWS, ROWS)
    along_x = jnp.concatenate([jnp.dot(volume[r * 512:(r + 1) * 512], kx, preferred_element_type=F32)
                               for r in range(2)], axis=0).astype(BF16)
    side = jnp.concatenate([along_x[r * ROWS:(r + 1) * ROWS] for r in range(4)], axis=1)
    return jnp.dot(ky, side, preferred_element_type=F32)


def adjoint_plane(view, quotient, kyt, kxt, depth_ref):
    along_y = jnp.dot(kyt, quotient.astype(BF16), preferred_element_type=F32).astype(BF16)
    stacked = jnp.concatenate([along_y[:, r * 128:(r + 1) * 128] for r in range(4)], axis=0)
    along_x = jnp.concatenate([jnp.dot(stacked[r * 512:(r + 1) * 512], kxt, preferred_element_type=F32)
                               for r in range(2)], axis=0).astype(BF16)
    for r in range(4):
        first = pl.multiple_of(view * 64 + r * 16, 16)
        for quad in range(QUADS):
            depth_ref[quad, pl.ds(first, 16), :] = along_x[r * ROWS + quad * 16:r * ROWS + quad * 16 + 16]


def own_lanes(left, right):
    lane = lax.broadcasted_iota(I32, left.shape, 1) % PART
    return jnp.where(lane < HALO, rotate(left, 112), rotate(right, 16))


def adjoint_depth(scale, bza_ref, depth_ref, main_ref, tail_ref, to_left_ref, to_right_ref, last=False):
    block = lane_block((64, 128))
    low_half = block < 2
    near = lax.broadcasted_iota(I32, (64, 128), 1) % PART < HALO

    def pair(quad, carry):
        tails = []
        members = (quad, quad + QUADS // 2)
        both = jnp.concatenate([depth_ref[member] for member in members], axis=1)
        summed_both = jnp.dot(bza_ref[...], both, preferred_element_type=F32)
        for index, member in enumerate(members):
            summed = summed_both[:, index * ROWS:(index + 1) * ROWS]
            mains = []
            for half in range(2):
                lanes = slice(half * 128, (half + 1) * 128)
                lower = jnp.where(block < 3, rotate(summed[:64, lanes], 96), 0.0)
                upper = jnp.where(block > 0, rotate(summed[128:, lanes], 32), 0.0)
                mains.append(summed[64:128, lanes] + lower + upper)
            tail = jnp.where(block == 0, summed[:64, :128], summed[128:, 128:])
            tail = jnp.where(block == 1, rotate(summed[128:, :128], 64), tail)
            tail = jnp.where(block == 2, rotate(summed[:64, 128:], 64), tail)
            if last:
                main_ref[member] = own_lanes(*mains)
                tail_ref[member] = jnp.where(near, rotate(tail, 112), rotate(tail, 80))
                to_left_ref[member] = to_fixed(jnp.where(near, mains[0], rotate(tail, 16)), scale)
                to_right_ref[member] = to_fixed(jnp.where(near, rotate(tail, 48), mains[1]), scale)
                continue
            rows = pl.ds(pl.multiple_of(member * 64, 64), 64)
            main_ref[0, rows, :] = mains[0]
            main_ref[1, rows, :] = mains[1]
            tail_ref[member] = tail
            to_left_ref[member] = to_fixed(mains[0], scale)
            to_right_ref[member] = to_fixed(mains[1], scale)
            tails.append(tail)
        if last:
            return carry
        to_left_ref[QUADS + quad] = to_fixed(jnp.where(low_half, tails[0], rotate(tails[1], 64)), scale)
        to_right_ref[QUADS + quad] = to_fixed(jnp.where(low_half, rotate(tails[0], 64), tails[1]), scale)
        return carry

    lax.fori_loop(0, QUADS // 2, pair, 0, unroll=2)


def tall(value):
    return jnp.concatenate([value] * 8, axis=0)


def forward_kernel(edge_ref, main_ref, from_low_ref, from_high_ref, bzf_ref, ky_ref, kx_ref, out_ref, tail_ref,
                   planes_ref):
    build_tail(edge_ref, from_low_ref, from_high_ref, tail_ref)
    forward_depth(main_ref, tail_ref, bzf_ref, planes_ref)

    def one_view(view, carry):
        out_ref[view] = forward_plane(view, planes_ref, ky_ref[view], kx_ref[view]).astype(BF16)
        return carry

    lax.fori_loop(0, VIEWS, one_view, 0)


def forward(edges, main, from_low, from_high, bzf, ky, kx):
    return pl.pallas_call(
        forward_kernel,
        out_shape=(
            jax.ShapeDtypeStruct((VIEWS, ROWS, 2 * ROWS), BF16),
            jax.ShapeDtypeStruct((QUADS, 64, 128), F32),
        ),
        in_specs=smem(1) + vmem(6),
        out_specs=tuple(vmem(2)),
        scratch_shapes=[pltpu.VMEM((VIEWS * 4, ROWS, ROWS), BF16)],
        name="forward",
    )(edges, main, from_low, from_high, bzf, ky, kx)


def per_view(*shape):
    return pl.BlockSpec((1,) + shape, lambda view: (view,) + (0,) * len(shape))


PARTIAL_SHAPES = (
    held((2, 1024, 128), F32),
    held((QUADS, 64, 128), F32),
    held((QUADS + QUADS // 2, 64, 128), I16),
    held((QUADS + QUADS // 2, 64, 128), I16),
)


def first_adjoint_kernel(start_ref, source_ref, place_ref, inverse_ref, offset_ref, incoming_ref, blurred_ref, kyt_ref,
                         kxt_ref, bza_ref, main_ref, tail_ref, to_left_ref, to_right_ref, average_ref, total_ref,
                         depth_ref, swap_ref):
    view = pl.program_id(0)

    @pl.when(view == 0)
    def _():
        swap_ref[...] = digit_swap((512, 512))

    for slot in range(SLOTS):
        total_ref[slot] = jnp.zeros((NY, 128), F32)

    def add(entry, carry):
        place = place_ref[entry]
        piece = incoming_ref[source_ref[entry] - view * incoming_ref.shape[0]].astype(F32)
        slot = place - view * SLOTS
        total_ref[slot] = total_ref[slot] + piece * inverse_ref[place]
        return carry

    lax.fori_loop(start_ref[view], start_ref[view + 1], add, 0)
    rows = []
    for r in range(4):
        rows.append(jnp.concatenate([total_ref[h * 4 + r].astype(BF16) for h in range(4)], axis=1))
    mixed = jnp.dot(jnp.concatenate(rows, axis=0), swap_ref[...], preferred_element_type=F32)
    for r in range(4):
        lanes = slice(r * 128, r * 128 + 128)
        for m in range(8):
            first = r * NY + m * 8
            ends = []
            for q in (0, 2):
                ends.append(swap_fours(mixed[first:first + 8, q * 128:(q + 1) * 128],
                                       mixed[first:first + 8, (q + 1) * 128:(q + 2) * 128]))
            for odd in range(2):
                quad = 2 * m + odd
                average_ref[0, quad * 16:quad * 16 + 16, lanes] = jnp.concatenate(
                    [ends[0][odd], ends[1][odd]], axis=0).astype(BF16)
    quotient = average_ref[0].astype(F32) / (blurred_ref[0].astype(F32) + offset_ref[view])
    adjoint_plane(view, quotient, kyt_ref[0], kxt_ref[0], depth_ref)

    @pl.when(view == VIEWS - 1)
    def _():
        scale = tall(32767.0 / partial_bound(offset_ref))
        adjoint_depth(scale, bza_ref, depth_ref, main_ref, tail_ref, to_left_ref, to_right_ref)


def first_adjoint(start, source, place, inverse, offset, incoming, blurred, kyt, kxt, bza):
    held = incoming.shape[0] // VIEWS
    return pl.pallas_call(
        first_adjoint_kernel,
        grid=(VIEWS,),
        out_shape=PARTIAL_SHAPES + (jax.ShapeDtypeStruct((VIEWS, ROWS, 2 * ROWS), BF16),),
        in_specs=smem(5) + [pl.BlockSpec((held, NY, 128), lambda view: (view, 0, 0)), per_view(ROWS, 2 * ROWS),
                            per_view(ROWS, ROWS), per_view(128, ROWS)] + vmem(1),
        out_specs=tuple(vmem(4)) + (per_view(ROWS, 2 * ROWS),),
        scratch_shapes=[pltpu.VMEM((SLOTS, NY, 128), F32), pltpu.VMEM((QUADS, VIEWS * 64, ROWS), BF16),
                        pltpu.VMEM((512, 512), BF16)],
        name="first_adjoint",
        compiler_params=room(60),
    )(start, source, place, inverse, offset, incoming, blurred, kyt, kxt, bza)


def join_columns_kernel(offset_ref, edge_ref, main_ref, tail_ref, from_left_ref, from_right_ref, out_main_ref, out_tail_ref,
                        low_ref, high_ref):
    block = lane_block((64, 128))
    low_half = block < 2
    bound = partial_bound(offset_ref)
    scale = tall(32767.0 / bound)
    left_step = tall(bound * (edge_ref[0] / 32767.0))
    right_step = tall(bound * (edge_ref[1] / 32767.0))

    def pair(quad, carry):
        packed_left = from_fixed(from_left_ref[QUADS + quad], left_step)
        packed_right = from_fixed(from_right_ref[QUADS + quad], right_step)
        for second, member in enumerate((quad, quad + QUADS // 2)):
            rows = pl.ds(pl.multiple_of(member * 64, 64), 64)
            left = main_ref[0, rows, :] + from_fixed(from_left_ref[member], left_step)
            right = main_ref[1, rows, :] + from_fixed(from_right_ref[member], right_step)
            if second:
                extra = jnp.where(low_half, rotate(packed_left, 64), packed_right)
            else:
                extra = jnp.where(low_half, packed_left, rotate(packed_right, 64))
            tail = tail_ref[member] + extra
            out_main_ref[0, rows, :] = left
            out_main_ref[1, rows, :] = right
            out_tail_ref[member] = tail
            low = jnp.where(block == 1, rotate(left, 32), tail)
            low = jnp.where(block == 3, rotate(right, 96), low)
            high = jnp.where(block == 0, rotate(left, 32), tail)
            high = jnp.where(block == 2, rotate(right, 96), high)
            low_ref[member] = to_fixed(low, scale)
            high_ref[member] = to_fixed(high, scale)
        return carry

    lax.fori_loop(0, QUADS // 2, pair, 0)


def join_columns(offset, edges, main, tail, from_left, from_right):
    return pl.pallas_call(
        join_columns_kernel,
        out_shape=(
            held((2, 1024, 128), F32),
            held((QUADS, 64, 128), F32),
            held((QUADS, 64, 128), I16),
            held((QUADS, 64, 128), I16),
        ),
        in_specs=smem(2) + vmem(4),
        out_specs=tuple(vmem(4)),
        name="join_columns",
        compiler_params=room(48),
    )(offset, edges, *stay(main, tail, from_left, from_right))


def joined_planes(quad, steps, block, main_ref, tail_ref, from_low_ref, from_high_ref):
    rows = pl.ds(pl.multiple_of(quad * 64, 64), 64)
    low = from_fixed(from_low_ref[quad], steps[0])
    high = from_fixed(from_high_ref[quad], steps[1])
    left = main_ref[0, rows, :]
    left = left + jnp.where(block == 0, rotate(low, 96), 0.0) + jnp.where(block == 3, rotate(high, 96), 0.0)
    right = main_ref[1, rows, :]
    right = right + jnp.where(block == 0, rotate(low, 32), 0.0) + jnp.where(block == 3, rotate(high, 32), 0.0)
    tail = tail_ref[quad] + jnp.where(block % 2 == 0, low, high)
    return rows, left, right, tail


def depth_steps(bound, edge_ref):
    return tall(bound * (edge_ref[2] / 32767.0)), tall(bound * (edge_ref[3] / 32767.0))


def second_kernel(offset_ref, edge_ref, part_main_ref, part_tail_ref, from_low_ref, from_high_ref, estimate_main_ref,
                  estimate_tail_ref, scale_main_ref, scale_tail_ref, bzf_ref, bza_ref, average_ref, ky_ref, kx_ref,
                  kyt_ref, kxt_ref, own_estimate_ref, own_ref, own_tail_ref, to_left_ref, to_right_ref, new_main_ref,
                  tail_estimate_ref, planes_ref, depth_ref):
    view = pl.program_id(0)

    @pl.when(view == 0)
    def _():
        block = lane_block((64, 128))
        steps = depth_steps(partial_bound(offset_ref), edge_ref)

        def renew(quad, carry):
            rows, left, right, tail = joined_planes(
                quad, steps, block, part_main_ref, part_tail_ref, from_low_ref, from_high_ref)
            left = estimate_main_ref[0, rows, :] * left * scale_main_ref[0, rows, :]
            right = estimate_main_ref[1, rows, :] * right * scale_main_ref[1, rows, :]
            new_main_ref[0, rows, :] = left
            new_main_ref[1, rows, :] = right
            own_estimate_ref[quad] = own_lanes(left * scale_main_ref[0, rows, :], right * scale_main_ref[1, rows, :])
            tail_estimate_ref[quad] = estimate_tail_ref[quad] * tail * scale_tail_ref[quad]
            return carry

        lax.fori_loop(0, QUADS, renew, 0)
        forward_depth(new_main_ref, tail_estimate_ref, bzf_ref, planes_ref)

    blurred = forward_plane(view, planes_ref, ky_ref[0], kx_ref[0]) + offset_ref[view]
    adjoint_plane(view, average_ref[0].astype(F32) / blurred, kyt_ref[0], kxt_ref[0], depth_ref)

    @pl.when(view == VIEWS - 1)
    def _():
        scale = tall(32767.0 / partial_bound(offset_ref))
        adjoint_depth(scale, bza_ref, depth_ref, own_ref, own_tail_ref, to_left_ref, to_right_ref, last=True)


def second(offset, edges, *operands):
    return pl.pallas_call(
        second_kernel,
        grid=(VIEWS,),
        out_shape=(held((QUADS, 64, 128), F32),) * 3 + (held((QUADS, 64, 128), I16),) * 2,
        in_specs=smem(2) + vmem(10) + [per_view(ROWS, 2 * ROWS), per_view(ROWS, ROWS), per_view(ROWS, 128),
                                       per_view(ROWS, ROWS), per_view(128, ROWS)],
        out_specs=tuple(vmem(5)),
        scratch_shapes=[pltpu.VMEM((2, 1024, 128), F32), pltpu.VMEM((QUADS, 64, 128), F32),
                        pltpu.VMEM((VIEWS * 4, ROWS, ROWS), BF16), pltpu.VMEM((QUADS, VIEWS * 64, ROWS), BF16)],
        name="second",
        compiler_params=room(52),
    )(offset, edges, *stay(*operands[:4]), *operands[4:])


def join_own_kernel(offset_ref, edge_ref, own_ref, tail_ref, from_left_ref, from_right_ref, out_ref, low_ref, high_ref):
    block = lane_block((64, 128))
    near = lax.broadcasted_iota(I32, (64, 128), 1) % PART < HALO
    bound = partial_bound(offset_ref)
    scale = tall(32767.0 / bound)
    left_step = tall(bound * (edge_ref[0] / 32767.0))
    right_step = tall(bound * (edge_ref[1] / 32767.0))

    def four_quads(quad, carry):
        low = jnp.zeros((64, 128), F32)
        high = jnp.zeros((64, 128), F32)
        for k in range(4):
            member = quad + k * 4
            left = from_fixed(from_left_ref[member], left_step)
            right = from_fixed(from_right_ref[member], right_step)
            out_ref[member] = own_ref[member] + own_lanes(left, right)
            tail = tail_ref[member] + jnp.where(near, left, right)
            low = jnp.where(block == k, rotate(tail, PART * k), low)
            high = jnp.where(block == k, rotate(tail, PART * k - PART), high)
        low_ref[quad] = to_fixed(low, scale)
        high_ref[quad] = to_fixed(high, scale)
        return carry

    lax.fori_loop(0, QUADS // 4, four_quads, 0)


def join_own(offset, edges, own, tail, from_left, from_right):
    return pl.pallas_call(
        join_own_kernel,
        out_shape=(held((QUADS, 64, 128), F32), held((QUADS // 4, 64, 128), I16), held((QUADS // 4, 64, 128), I16)),
        in_specs=smem(2) + vmem(4),
        out_specs=tuple(vmem(3)),
        name="join_own",
        compiler_params=room(48),
    )(offset, edges, *stay(own, tail, from_left, from_right))


def finish_kernel(offset_ref, edge_ref, own_ref, from_low_ref, from_high_ref, estimate_ref, out_ref, value_ref):
    block = lane_block((64, 128))
    steps = depth_steps(partial_bound(offset_ref), edge_ref)

    def four_quads(quad, largest):
        low = from_fixed(from_low_ref[quad], steps[0])
        high = from_fixed(from_high_ref[quad], steps[1])
        for k in range(4):
            member = quad + k * 4
            summed = own_ref[member] + jnp.where(block == 0, rotate(low, -PART * k), 0.0)
            summed = summed + jnp.where(block == 3, rotate(high, 96 - PART * k), 0.0)
            value = estimate_ref[member] * summed
            value_ref[member] = value
            largest = jnp.maximum(largest, value)
        return largest

    largest = lax.fori_loop(0, QUADS // 4, four_quads, jnp.zeros((64, 128), F32))
    unit = (jnp.max(largest) * 64.0).astype(I32) + 1
    vector = jnp.full((16, 128), unit, I32)
    out_ref[1024:1040, :] = (vector >> 15).astype(I16)
    out_ref[1040:1056, :] = (vector & 32767).astype(I16)
    factor = (32767.0 * 64.0) / vector.astype(F32)

    def sixteen_rows(n, carry):
        for j in range(0, 16, 2):
            rows = slice(j * 4, j * 4 + 8)
            ends = [swap_fours(value_ref[n * 4 + 2 * m, rows, :], value_ref[n * 4 + 2 * m + 1, rows, :])
                    for m in range(2)]
            for odd in range(2):
                first = pl.multiple_of((j + odd) * NY + n * 16, 16)
                out_ref[pl.ds(first, 16), :] = to_fixed(
                    jnp.concatenate([ends[0][odd], ends[1][odd]], axis=0), factor)
        return carry

    lax.fori_loop(0, 4, sixteen_rows, 0)


def finish(offset, edges, own, from_low, from_high, estimate):
    return pl.pallas_call(
        finish_kernel,
        out_shape=held((1056, 128), I16),
        in_specs=smem(2) + vmem(4),
        out_specs=vmem(1)[0],
        scratch_shapes=[pltpu.VMEM((QUADS, 64, 128), F32)],
        name="finish",
        compiler_params=room(52),
    )(offset, edges, *stay(own, from_low, from_high, estimate))


def assemble_kernel(index_ref, *refs):
    chunk_refs, out_ref, buffer_ref = refs[:8], refs[8], refs[9]
    part = index_ref[0]

    @pl.when(pl.program_id(0) == 0)
    def _():
        for place in range(8):
            owner = ((part // 2 + place % 4) % 4) * 2 + (part % 2 if place < 4 else 1 - part % 2)
            buffer_ref[owner] = chunk_refs[place][...]

    block = lane_block((16, 128))
    even = block % 2 == 0
    units = []
    for half in range(2):
        unit = jnp.zeros((16, 128), F32)
        for k in range(4):
            digits = (buffer_ref[half * 4 + k, 1024:1040, :].astype(I32) * 32768
                      + buffer_ref[half * 4 + k, 1040:1056, :].astype(I32))
            unit = jnp.where(block == k, digits.astype(F32) * (1.0 / (64.0 * 32767.0)), unit)
        units.append(unit)
    step = pl.program_id(0)

    def sixteen_rows(n, carry):
        for j in range(4):
            rows = pl.ds(pl.multiple_of((step * 4 + j) * NY + n * 16, 16), 16)
            for half in range(2):
                c0, c1, c2, c3 = (buffer_ref[half * 4 + k, rows, :].astype(I32).astype(F32) for k in range(4))
                a0 = jnp.where(block < 2, c0, rotate(c2, 64))
                a1 = jnp.where(block < 2, c1, rotate(c3, 64))
                a2 = jnp.where(block < 2, rotate(c0, 64), c2)
                a3 = jnp.where(block < 2, rotate(c1, 64), c3)
                results = (jnp.where(even, a0, rotate(a1, 32)), jnp.where(even, rotate(a0, 96), a1),
                           jnp.where(even, a2, rotate(a3, 32)), jnp.where(even, rotate(a2, 96), a3))
                for h in range(4):
                    out_ref[h, 0, j, pl.ds(pl.multiple_of(n * 16, 16), 16), half * 128:(half + 1) * 128] = (
                        results[h] * units[half])
        return carry

    lax.fori_loop(0, 4, sixteen_rows, 0)


def assemble(index, chunks):
    return pl.pallas_call(
        assemble_kernel,
        grid=(4,),
        out_shape=jax.ShapeDtypeStruct((4, 4, 4, NY, 256), F32),
        in_specs=smem(1) + vmem(8),
        out_specs=pl.BlockSpec((4, 1, 4, NY, 256), lambda step: (0, step, 0, 0, 0)),
        scratch_shapes=[pltpu.VMEM((VIEWS, 1056, 128), I16)],
        name="assemble",
        compiler_params=room(58),
    )(index, *stay(*chunks)).reshape(64, NY, 256)


def to_neighbours(upward, downward, axis):
    count = lax.axis_size(axis)
    from_low = lax.ppermute(upward, axis, [(i, (i + 1) % count) for i in range(count)])
    from_high = lax.ppermute(downward, axis, [((i + 1) % count, i) for i in range(count)])
    return from_low, from_high


def gather_parts(own):
    parts = [own] + [
        lax.ppermute(own, "view", [((i + 2 * step) % VIEWS, i) for i in range(VIEWS)]) for step in (1, 3, 2)
    ]
    parts = [parts[0], parts[1], parts[3], parts[2]]
    return parts, [lax.ppermute(part, "view", [(i, i ^ 1) for i in range(VIEWS)]) for part in parts]


def column_sums(kernel, shift, positions, length):
    radius = (TAPS - 1) // 2
    source = (positions[None, :, None] - shift[:, None, None]
              - jnp.arange(TAPS, dtype=I32)[None, None, :] + radius)
    inside = (source >= 0) & (source < length)
    return jnp.sum(jnp.where(inside, kernel[:, None, :], 0.0), axis=2)


def program(estimate0, pieces, dest_block, slot_index, psf_shift, psf_taps, background):
    block_count = lax.axis_size("block")
    my_view = lax.axis_index("view")
    my_block = lax.axis_index("block")
    edges = jnp.stack([my_view > 0, my_view < VIEWS - 1, my_block > 0, my_block < block_count - 1]).astype(F32)
    targets = dest_block[:, :, 0].reshape(VIEWS, block_count, SLOTS)
    slots = slot_index.reshape(VIEWS, block_count, SLOTS)

    index = my_view.reshape(1).astype(I32)
    low, high = window_ends(index, estimate0)
    from_low, from_high = to_neighbours(high, low, "block")

    own_targets = lax.dynamic_slice(targets, (my_view, my_block, 0), (1, 1, SLOTS)).reshape(SLOTS)
    own_targets, low, high = lax.optimization_barrier((own_targets, low, high))
    outgoing = pack_pieces(own_targets, pieces[0], block_count)
    incoming = lax.all_to_all(outgoing.reshape(VIEWS * block_count, CAP, NY, 128), ("view", "block"), 0, 0, tiled=True)
    incoming = incoming.reshape(VIEWS * block_count * CAP, NY, 128)

    main = window_estimate(index, estimate0)
    kernel = psf_taps / jnp.sum(psf_taps, axis=2, keepdims=True)
    ky, kyt, kx, kxt, bzf, bza = build_bands(kernel.reshape(-1), psf_shift.reshape(-1))
    blurred, tail = forward(edges, main, from_low, from_high, bzf, ky, kx)

    earlier = jnp.tril(jnp.ones((SLOTS, SLOTS), jnp.bool_), -1)
    same = (targets[:, :, :, None] == targets[:, :, None, :]) & earlier[None, None]
    ranks = jnp.sum(same.astype(I32), axis=3)
    mine = targets == my_block
    received = jnp.arange(CAP, dtype=I32)
    slot_of = jnp.sum(
        jnp.where(mine[..., None] & (ranks[..., None] == received), slots[..., None] + 1, 0), axis=2
    ).reshape(VIEWS, block_count * CAP) - 1
    hits = slot_of[:, :, None] == jnp.arange(SLOTS, dtype=I32)
    counts = jnp.sum(hits.astype(I32), axis=1)
    inverse = 1.0 / jnp.maximum(counts, 1).astype(F32)
    entries = VIEWS * block_count * CAP
    number = jnp.arange(entries, dtype=I32)
    place_of = jnp.where(slot_of >= 0, slot_of + jnp.arange(VIEWS, dtype=I32)[:, None] * SLOTS, -1).reshape(entries)
    before = (place_of[None, :] >= 0) & (number[None, :] < number[:, None])
    position = jnp.where(place_of >= 0, jnp.sum(before.astype(I32), axis=1), -1)
    chosen = position[:, None] == number[None, :]
    source = jnp.sum(jnp.where(chosen, number[:, None], 0), axis=0)
    place = jnp.sum(jnp.where(chosen, place_of[:, None], 0), axis=0)
    start = jnp.sum(((place_of >= 0)[:, None]
                     & (number[:, None] // (block_count * CAP) < jnp.arange(VIEWS + 1))).astype(I32), axis=0)

    global_slot = (targets * SLOTS + slots).reshape(VIEWS, block_count * SLOTS)
    all_slots = jnp.arange(block_count * SLOTS, dtype=I32)
    occupied = jnp.any(global_slot[:, :, None] == all_slots, axis=1)
    mask = jnp.repeat(occupied.astype(F32), 4, axis=1)
    padded = jnp.pad(mask, ((0, 0), (2 * HALO, 2 * HALO)))
    window = lax.dynamic_slice_in_dim(padded, my_block * 64, 128, 1)
    depth = lax.broadcasted_iota(I32, (96, 128), 0) + HALO - lax.broadcasted_iota(I32, (96, 128), 1)
    tap = depth[None] - psf_shift[:, 0, None, None] + (TAPS - 1) // 2
    weight_depth = jnp.zeros((VIEWS, 96), F32)
    band = jnp.zeros((VIEWS, 96, 128), F32)
    for j in range(TAPS):
        band = jnp.where(tap == j, kernel[:, 0, j, None, None], band)
    weight_depth = jnp.sum(band * window[:, None, :], axis=2)
    weight_rows = column_sums(kernel[:, 1], psf_shift[:, 1], jnp.arange(NY, dtype=I32), NY)
    columns = my_view * PART - HALO + jnp.arange(2 * PART, dtype=I32)
    weight_columns = column_sums(kernel[:, 2], psf_shift[:, 2], columns, 256).reshape(VIEWS, 2, PART)
    by_group = weight_depth.reshape(VIEWS, 6, 16)
    planes = by_group[:, :, :, None, None] * weight_columns[:, None, None, :, :]
    planes = planes.transpose(0, 3, 2, 1, 4)
    weight_main = planes[:, :, :, 1:5].reshape(VIEWS, 2, 16, 128)
    weight_tail = jnp.stack([planes[:, :, :, 0], planes[:, :, :, 5]], axis=3)
    weight_tail = weight_tail.transpose(0, 2, 1, 3, 4).reshape(VIEWS, 16, 128)
    scale_main, scale_tail = build_weights(
        weight_rows.reshape(-1), jnp.repeat(weight_main, 4, axis=2), jnp.repeat(weight_tail, 4, axis=1))

    incoming, scale_main, scale_tail = lax.optimization_barrier((incoming, scale_main, scale_tail))
    part_main, part_tail, to_left, to_right, average = first_adjoint(
        start, source, place, inverse.reshape(-1), background, incoming, blurred, kyt, kxt, bza)
    from_left, from_right = to_neighbours(to_right, to_left, "view")
    part_main, part_tail, low, high = join_columns(background, edges, part_main, part_tail, from_left, from_right)
    from_low, from_high = to_neighbours(high, low, "block")

    estimate, own, own_tail, to_left, to_right = second(
        background, edges, part_main, part_tail, from_low, from_high, main, tail, scale_main, scale_tail,
        bzf, bza, average, ky, kx, kyt, kxt)
    from_left, from_right = to_neighbours(to_right, to_left, "view")
    own, low, high = join_own(background, edges, own, own_tail, from_left, from_right)
    from_low, from_high = to_neighbours(high, low, "block")
    own = finish(background, edges, own, from_low, from_high, estimate)

    mine, partners = gather_parts(own)
    return assemble(index, mine + partners)


def solution(mesh):
    return jax.shard_map(
        program,
        mesh=mesh,
        in_specs=(
            P("block", None, None),
            P("view", "block", None, None, None),
            P(),
            P(),
            P(),
            P(),
            P(),
        ),
        out_specs=P("block", None, None),
        check_vma=False,
    )
```

```python
import jax
import jax.numpy as jnp
from jax import lax
from jax.experimental import pallas as pl
from jax.experimental.pallas import tpu as pltpu
from jax.sharding import PartitionSpec as P


CAP = 2
TAPS = 21
HALO = 16
VIEWS = 8
SLOTS = 16
NY = 64
PART = 32
ROWS = 256
QUADS = 16

F32 = jnp.float32
BF16 = jnp.bfloat16
I32 = jnp.int32
I16 = jnp.int16


def lane_block(shape):
    return lax.broadcasted_iota(I32, shape, len(shape) - 1) // PART


def rotate(value, amount):
    return pltpu.roll(value, amount % 128, value.ndim - 1)


def digit_swap(shape):
    row = lax.broadcasted_iota(I32, shape, 0)
    column = lax.broadcasted_iota(I32, shape, 1)
    target = ((row // PART) % 4) * 128 + (row // 128) * PART + row % PART
    return jnp.where(column == target, 1.0, 0.0).astype(BF16)


def swap_fours(first, second):
    upper = lax.broadcasted_iota(I32, first.shape, 0) < 4
    return (jnp.where(upper, first, pltpu.roll(second, 4, 0)),
            jnp.where(upper, pltpu.roll(first, 4, 0), second))


def held(shape, dtype):
    return pltpu.VMEM(shape, dtype)


def stay(*arrays):
    return tuple(pltpu.with_memory_space_constraint(array, pltpu.VMEM) for array in arrays)


def room(mebibytes):
    return pltpu.CompilerParams(vmem_limit_bytes=mebibytes << 20)


def vmem(count):
    return [pl.BlockSpec(memory_space=pltpu.VMEM)] * count


def smem(count):
    return [pl.BlockSpec(memory_space=pltpu.SMEM)] * count


def to_fixed(value, scale):
    return (value * scale + 0.5).astype(I32).astype(I16)


def from_fixed(value, step):
    return value.astype(I32).astype(F32) * step


def partial_bound(offset_ref):
    total = 0.0
    for view in range(VIEWS):
        total = total + 2.0 / jnp.full((8, 128), offset_ref[view], F32)
    return total * 1.05


def band_kernel(taps_ref, shift_ref, ky_ref, kyt_ref, kx_ref, kxt_ref, bzf_ref, bza_ref):
    radius = (TAPS - 1) // 2

    def fill(difference, view, axis):
        result = jnp.zeros(difference.shape, F32)
        for tap in range(TAPS):
            result = jnp.where(difference == tap, taps_ref[(view * 3 + axis) * TAPS + tap], result)
        return result

    def one_view(view, carry):
        shift_z = shift_ref[view * 3]
        shift_y = shift_ref[view * 3 + 1]
        shift_x = shift_ref[view * 3 + 2]
        row = lax.broadcasted_iota(I32, (16, 2 * ROWS), 0)
        lane = lax.broadcasted_iota(I32, (16, 2 * ROWS), 1)
        offset = (lane // 16 - 16) * 4 + lane % 4 - row % 4
        same = (lane // 4) % 4 == row // 4
        for strip, target_ref in ((jnp.where(same, offset - shift_y + radius, -1), ky_ref),
                                  (jnp.where(same, -offset - shift_y + radius, -1), kyt_ref)):
            values = fill(strip, view, 1)
            for quad in range(QUADS):
                target_ref[view, quad * 16:(quad + 1) * 16, :] = values[
                    :, ROWS - quad * 16:2 * ROWS - quad * 16].astype(BF16)
        row = lax.broadcasted_iota(I32, (PART, 128), 0)
        lane = lax.broadcasted_iota(I32, (PART, 128), 1)
        for half in range(2):
            base = fill(half * PART + row - (lane % PART + HALO) - shift_x + radius, view, 2)
            for block in range(4):
                first = half * 128 + block * PART
                kx_ref[view, first:first + PART, :] = jnp.where(lane // PART == block, base, 0.0).astype(BF16)
            base = fill(half * PART + lane % PART - (row + HALO) - shift_x + radius, view, 2)
            for block in range(4):
                kxt_ref[view, block * PART:(block + 1) * PART, half * 128:(half + 1) * 128] = jnp.where(
                    lane // PART == block, base, 0.0).astype(BF16)
        row = lax.broadcasted_iota(I32, (64, 192), 0)
        lane = lax.broadcasted_iota(I32, (64, 192), 1)
        difference = jnp.where(lane % 4 == row % 4, lane // 4 - 16 - row // 4 - shift_z + radius, -1)
        bzf_ref[pl.ds(pl.multiple_of(view * 64, 64), 64), :] = fill(difference, view, 0).astype(BF16)
        return carry

    lax.fori_loop(0, VIEWS, one_view, 0)
    row = lax.broadcasted_iota(I32, (192, 128), 0)
    lane = lax.broadcasted_iota(I32, (192, 128), 1)
    left = lane < 64
    for pair in range(VIEWS // 2):
        shift = jnp.where(left, shift_ref[pair * 6], shift_ref[pair * 6 + 3])
        difference = jnp.where(lane % 4 == row % 4, row // 4 - 16 - (lane // 4) % 16 - shift + radius, -1)
        total = jnp.zeros((192, 128), F32)
        for tap in range(TAPS):
            value = jnp.where(left, taps_ref[pair * 6 * TAPS + tap], taps_ref[(pair * 6 + 3) * TAPS + tap])
            total = jnp.where(difference == tap, value, total)
        bza_ref[:, pair * 128:(pair + 1) * 128] = total.astype(BF16)


def build_bands(taps, shifts):
    return pl.pallas_call(
        band_kernel,
        out_shape=(
            jax.ShapeDtypeStruct((VIEWS, ROWS, ROWS), BF16),
            jax.ShapeDtypeStruct((VIEWS, ROWS, ROWS), BF16),
            jax.ShapeDtypeStruct((VIEWS, ROWS, 128), BF16),
            jax.ShapeDtypeStruct((VIEWS, 128, ROWS), BF16),
            jax.ShapeDtypeStruct((VIEWS * 64, 192), BF16),
            jax.ShapeDtypeStruct((192, VIEWS * 64), BF16),
        ),
        in_specs=smem(2),
        out_specs=tuple(vmem(6)),
        name="bands",
    )(taps, shifts)


def pack_kernel(target_ref, pieces_ref, out_ref, swap_ref):
    group = pl.program_id(0)
    count = target_ref.shape[0]

    @pl.when(group == 0)
    def _():
        swap_ref[...] = digit_swap((512, 512))

    def four_pieces():
        rows = []
        for k in range(4):
            for half in range(2):
                rows.append(jnp.concatenate(
                    [pieces_ref[k, q, :, half * 128:(half + 1) * 128] for q in range(4)], axis=1))
        mixed = jnp.dot(jnp.concatenate(rows, axis=0), swap_ref[...], preferred_element_type=F32).astype(BF16)
        for k in range(4):
            piece = group * 4 + k
            target = target_ref[piece]
            rank = jnp.int32(0)
            for other in range(count):
                rank = rank + jnp.where((target_ref[other] == target) & (other < piece), 1, 0)
            slot = target * CAP + rank
            for half in range(2):
                first = (k * 2 + half) * NY
                for part in range(4):
                    out_ref[half * 4 + part, slot] = mixed[first:first + NY, part * 128:(part + 1) * 128]

    four_pieces()


def pack_pieces(targets, pieces, block_count):
    return pl.pallas_call(
        pack_kernel,
        grid=(pieces.shape[0] // 4,),
        out_shape=jax.ShapeDtypeStruct((VIEWS, block_count * CAP, NY, 128), BF16),
        in_specs=smem(1) + [pl.BlockSpec((4,) + pieces.shape[1:], lambda group: (group, 0, 0, 0))],
        out_specs=vmem(1)[0],
        scratch_shapes=[pltpu.VMEM((512, 512), BF16)],
        name="pack",
    )(targets, pieces)


def window_kernel(index_ref, estimate_ref, main_ref):
    part = index_ref[0]
    block = lane_block((NY, 128))
    lane = lax.broadcasted_iota(I32, (NY, 128), 1) % PART

    def two_planes(step, carry):
        for half in range(2):
            column = (part + half) * PART - HALO + lane
            inside = (column >= 0) & (column < 256)
            planes = []
            for odd in range(2):
                result = jnp.zeros((NY, 128), F32)
                for h in range(4):
                    plane = estimate_ref[h * 16 + step * 2 + odd]
                    amount = (16 - PART * part - PART * half + PART * h + 512) % 256
                    result = jnp.where(block == h, pltpu.roll(plane, amount, 1)[:, :128], result)
                planes.append(jnp.where(inside, result, 0.0))
            for m in range(8):
                low, high = swap_fours(planes[0][m * 8:m * 8 + 8], planes[1][m * 8:m * 8 + 8])
                main_ref[half, pl.ds(pl.multiple_of(m * 128 + step * 8, 8), 8), :] = low
                main_ref[half, pl.ds(pl.multiple_of(m * 128 + 64 + step * 8, 8), 8), :] = high
        return carry

    lax.fori_loop(0, 8, two_planes, 0)


def window_estimate(index, estimate):
    return pl.pallas_call(
        window_kernel,
        out_shape=jax.ShapeDtypeStruct((2, 1024, 128), F32),
        in_specs=smem(1) + vmem(1),
        out_specs=vmem(1)[0],
        name="window",
    )(index, estimate)


def ends_kernel(index_ref, first_ref, last_ref, low_ref, high_ref):
    part = index_ref[0]
    amount = (16 - PART * part + 256) % 256
    lane = lax.broadcasted_iota(I32, (32, 128), 1)
    column = part * PART - HALO + lane % 64
    inside = (column >= 0) & (column < 256)

    def four_planes(step, carry):
        for source_ref, target_ref in ((first_ref, low_ref), (last_ref, high_ref)):
            planes = []
            for k in range(4):
                plane = source_ref[step * 4 + k]
                top = pltpu.roll(plane[:32], amount, 1)[:, :128]
                bottom = pltpu.roll(plane[32:], (amount + 64) % 256, 1)[:, :128]
                planes.append(jnp.where(inside, jnp.where(lane < 64, top, bottom), 0.0))
            for m in range(4):
                rows = slice(m * 8, m * 8 + 8)
                front = swap_fours(planes[0][rows], planes[1][rows])
                back = swap_fours(planes[2][rows], planes[3][rows])
                for odd in range(2):
                    target_ref[m * 2 + odd, pl.ds(pl.multiple_of(step * 16, 16), 16), :] = jnp.concatenate(
                        [front[odd], back[odd]], axis=0).astype(BF16)
        return carry

    lax.fori_loop(0, 4, four_planes, 0)


def window_ends(index, estimate):
    return pl.pallas_call(
        ends_kernel,
        grid=(1,),
        out_shape=(jax.ShapeDtypeStruct((8, 64, 128), BF16),) * 2,
        in_specs=smem(1) + [pl.BlockSpec((16, NY, 256), lambda step: (0, 0, 0)),
                            pl.BlockSpec((16, NY, 256), lambda step: (3, 0, 0))],
        out_specs=tuple(vmem(2)),
        name="ends",
    )(index, estimate, estimate)


def build_tail(edge_ref, from_low_ref, from_high_ref, tail_ref):
    block = lane_block((64, 128))

    def two_quads(quad, carry):
        low = from_low_ref[quad].astype(F32) * edge_ref[2]
        high = from_high_ref[quad].astype(F32) * edge_ref[3]
        for member in range(2):
            base = member * 64
            result = jnp.where(block == 0, rotate(low, -base), rotate(low, 32 - base))
            result = jnp.where(block == 1, rotate(high, 32 - base), result)
            tail_ref[quad + member * 8] = jnp.where(block == 3, rotate(high, 64 - base), result)
        return carry

    lax.fori_loop(0, QUADS // 2, two_quads, 0)


def weight_kernel(rows_ref, main_ref, tail_ref, out_main_ref, out_tail_ref):
    quarter = lax.broadcasted_iota(I32, (64, 128), 0) % 4

    def one_quad(quad, carry):
        rows = pl.ds(pl.multiple_of(quad * 64, 64), 64)
        totals = [jnp.zeros((64, 128), F32) for _ in range(3)]
        for view in range(VIEWS):
            factor = jnp.full((64, 128), rows_ref[view * NY + quad * 4], F32)
            for k in range(1, 4):
                factor = jnp.where(quarter == k, rows_ref[view * NY + quad * 4 + k], factor)
            totals[0] = totals[0] + factor * main_ref[view, 0]
            totals[1] = totals[1] + factor * main_ref[view, 1]
            totals[2] = totals[2] + factor * tail_ref[view]
        out_main_ref[0, rows, :] = 1.0 / jnp.maximum(totals[0], 1.0)
        out_main_ref[1, rows, :] = 1.0 / jnp.maximum(totals[1], 1.0)
        out_tail_ref[quad] = 1.0 / jnp.maximum(totals[2], 1.0)
        return carry

    lax.fori_loop(0, QUADS, one_quad, 0)


def build_weights(rows, main, tail):
    return pl.pallas_call(
        weight_kernel,
        out_shape=(
            jax.ShapeDtypeStruct((2, 1024, 128), F32),
            jax.ShapeDtypeStruct((QUADS, 64, 128), F32),
        ),
        in_specs=smem(1) + vmem(2),
        out_specs=tuple(vmem(2)),
        name="weights",
    )(rows, main, tail)


def forward_depth(main_ref, tail_ref, bzf_ref, planes_ref):
    block = lane_block((64, 128))

    def stacked(quad):
        rows = pl.ds(pl.multiple_of(quad * 64, 64), 64)
        left = main_ref[0, rows, :]
        right = main_ref[1, rows, :]
        tail = tail_ref[quad]
        turned = rotate(tail, 64)
        lower = jnp.concatenate([jnp.where(block == 0, tail, rotate(left, 32)),
                                 jnp.where(block == 0, turned, rotate(right, 32))], axis=1)
        upper = jnp.concatenate([jnp.where(block == 3, turned, rotate(left, 96)),
                                 jnp.where(block == 3, tail, rotate(right, 96))], axis=1)
        return jnp.concatenate([lower, jnp.concatenate([left, right], axis=1), upper], axis=0).astype(BF16)

    def two_quads(step, carry):
        both = jnp.concatenate([stacked(step * 2), stacked(step * 2 + 1)], axis=1)
        blurred = jnp.dot(bzf_ref[...], both, preferred_element_type=F32).astype(BF16)
        for member in range(2):
            first = pl.multiple_of(step * 32 + member * 16, 16)
            for group in range(VIEWS * 4):
                planes_ref[group, pl.ds(first, 16), :] = blurred[
                    group * 16:(group + 1) * 16, member * ROWS:(member + 1) * ROWS]
        return carry

    lax.fori_loop(0, QUADS // 2, two_quads, 0, unroll=2)


def forward_plane(view, planes_ref, ky, kx):
    volume = planes_ref[pl.ds(view * 4, 4)].reshape(4 * ROWS, ROWS)
    along_x = jnp.concatenate([jnp.dot(volume[r * 512:(r + 1) * 512], kx, preferred_element_type=F32)
                               for r in range(2)], axis=0).astype(BF16)
    side = jnp.concatenate([along_x[r * ROWS:(r + 1) * ROWS] for r in range(4)], axis=1)
    return jnp.dot(ky, side, preferred_element_type=F32)


def adjoint_plane(view, quotient, kyt, kxt, depth_ref):
    along_y = jnp.dot(kyt, quotient.astype(BF16), preferred_element_type=F32).astype(BF16)
    stacked = jnp.concatenate([along_y[:, r * 128:(r + 1) * 128] for r in range(4)], axis=0)
    along_x = jnp.concatenate([jnp.dot(stacked[r * 512:(r + 1) * 512], kxt, preferred_element_type=F32)
                               for r in range(2)], axis=0).astype(BF16)
    for r in range(4):
        first = pl.multiple_of(view * 64 + r * 16, 16)
        for quad in range(QUADS):
            depth_ref[quad, pl.ds(first, 16), :] = along_x[r * ROWS + quad * 16:r * ROWS + quad * 16 + 16]


def own_lanes(left, right):
    lane = lax.broadcasted_iota(I32, left.shape, 1) % PART
    return jnp.where(lane < HALO, rotate(left, 112), rotate(right, 16))


def adjoint_depth(scale, bza_ref, depth_ref, main_ref, tail_ref, to_left_ref, to_right_ref, last=False):
    block = lane_block((64, 128))
    low_half = block < 2
    near = lax.broadcasted_iota(I32, (64, 128), 1) % PART < HALO

    def pair(quad, carry):
        tails = []
        members = (quad, quad + QUADS // 2)
        both = jnp.concatenate([depth_ref[member] for member in members], axis=1)
        summed_both = jnp.dot(bza_ref[...], both, preferred_element_type=F32)
        for index, member in enumerate(members):
            summed = summed_both[:, index * ROWS:(index + 1) * ROWS]
            mains = []
            for half in range(2):
                lanes = slice(half * 128, (half + 1) * 128)
                lower = jnp.where(block < 3, rotate(summed[:64, lanes], 96), 0.0)
                upper = jnp.where(block > 0, rotate(summed[128:, lanes], 32), 0.0)
                mains.append(summed[64:128, lanes] + lower + upper)
            tail = jnp.where(block == 0, summed[:64, :128], summed[128:, 128:])
            tail = jnp.where(block == 1, rotate(summed[128:, :128], 64), tail)
            tail = jnp.where(block == 2, rotate(summed[:64, 128:], 64), tail)
            if last:
                main_ref[member] = own_lanes(*mains)
                tail_ref[member] = jnp.where(near, rotate(tail, 112), rotate(tail, 80))
                to_left_ref[member] = to_fixed(jnp.where(near, mains[0], rotate(tail, 16)), scale)
                to_right_ref[member] = to_fixed(jnp.where(near, rotate(tail, 48), mains[1]), scale)
                continue
            rows = pl.ds(pl.multiple_of(member * 64, 64), 64)
            main_ref[0, rows, :] = mains[0]
            main_ref[1, rows, :] = mains[1]
            tail_ref[member] = tail
            to_left_ref[member] = to_fixed(mains[0], scale)
            to_right_ref[member] = to_fixed(mains[1], scale)
            tails.append(tail)
        if last:
            return carry
        to_left_ref[QUADS + quad] = to_fixed(jnp.where(low_half, tails[0], rotate(tails[1], 64)), scale)
        to_right_ref[QUADS + quad] = to_fixed(jnp.where(low_half, rotate(tails[0], 64), tails[1]), scale)
        return carry

    lax.fori_loop(0, QUADS // 2, pair, 0, unroll=2)


def tall(value):
    return jnp.concatenate([value] * 8, axis=0)


def forward_kernel(edge_ref, main_ref, from_low_ref, from_high_ref, bzf_ref, ky_ref, kx_ref, out_ref, tail_ref,
                   planes_ref):
    build_tail(edge_ref, from_low_ref, from_high_ref, tail_ref)
    forward_depth(main_ref, tail_ref, bzf_ref, planes_ref)

    def one_view(view, carry):
        out_ref[view] = forward_plane(view, planes_ref, ky_ref[view], kx_ref[view]).astype(BF16)
        return carry

    lax.fori_loop(0, VIEWS, one_view, 0)


def forward(edges, main, from_low, from_high, bzf, ky, kx):
    return pl.pallas_call(
        forward_kernel,
        out_shape=(
            jax.ShapeDtypeStruct((VIEWS, ROWS, 2 * ROWS), BF16),
            jax.ShapeDtypeStruct((QUADS, 64, 128), F32),
        ),
        in_specs=smem(1) + vmem(6),
        out_specs=tuple(vmem(2)),
        scratch_shapes=[pltpu.VMEM((VIEWS * 4, ROWS, ROWS), BF16)],
        name="forward",
    )(edges, main, from_low, from_high, bzf, ky, kx)


def per_view(*shape):
    return pl.BlockSpec((2,) + shape, lambda step: (step,) + (0,) * len(shape))


PARTIAL_SHAPES = (
    held((2, 1024, 128), F32),
    held((QUADS, 64, 128), F32),
    held((QUADS + QUADS // 2, 64, 128), I16),
    held((QUADS + QUADS // 2, 64, 128), I16),
)


def first_adjoint_kernel(start_ref, source_ref, place_ref, inverse_ref, offset_ref, incoming_ref, blurred_ref, kyt_ref,
                         kxt_ref, bza_ref, main_ref, tail_ref, to_left_ref, to_right_ref, average_ref, total_ref,
                         depth_ref, swap_ref):
    step = pl.program_id(0)

    @pl.when(step == 0)
    def _():
        swap_ref[...] = digit_swap((512, 512))

    for slot in range(2 * SLOTS):
        total_ref[slot] = jnp.zeros((NY, 128), F32)

    def add(entry, carry):
        place = place_ref[entry]
        piece = incoming_ref[source_ref[entry] - step * incoming_ref.shape[0]].astype(F32)
        slot = place - step * (2 * SLOTS)
        total_ref[slot] = total_ref[slot] + piece * inverse_ref[place]
        return carry

    lax.fori_loop(start_ref[step * 2], start_ref[step * 2 + 2], add, 0)
    rows = []
    for r in range(8):
        rows.append(jnp.concatenate(
            [total_ref[r // 4 * SLOTS + h * 4 + r % 4].astype(BF16) for h in range(4)], axis=1))
    mixed = jnp.dot(jnp.concatenate(rows, axis=0), swap_ref[...], preferred_element_type=F32)
    for r in range(8):
        lanes = slice(r % 4 * 128, r % 4 * 128 + 128)
        for m in range(8):
            first = r * NY + m * 8
            ends = []
            for q in (0, 2):
                ends.append(swap_fours(mixed[first:first + 8, q * 128:(q + 1) * 128],
                                       mixed[first:first + 8, (q + 1) * 128:(q + 2) * 128]))
            for odd in range(2):
                quad = 2 * m + odd
                average_ref[r // 4, quad * 16:quad * 16 + 16, lanes] = jnp.concatenate(
                    [ends[0][odd], ends[1][odd]], axis=0).astype(BF16)
    quotients = [average_ref[k].astype(F32) / (blurred_ref[k].astype(F32) + offset_ref[step * 2 + k]) for k in range(2)]
    for k in range(2):
        adjoint_plane(step * 2 + k, quotients[k], kyt_ref[k], kxt_ref[k], depth_ref)

    @pl.when(step == VIEWS // 2 - 1)
    def _():
        scale = tall(32767.0 / partial_bound(offset_ref))
        adjoint_depth(scale, bza_ref, depth_ref, main_ref, tail_ref, to_left_ref, to_right_ref)


def first_adjoint(start, source, place, inverse, offset, incoming, blurred, kyt, kxt, bza):
    share = incoming.shape[0] // (VIEWS // 2)
    return pl.pallas_call(
        first_adjoint_kernel,
        grid=(VIEWS // 2,),
        out_shape=PARTIAL_SHAPES + (jax.ShapeDtypeStruct((VIEWS, ROWS, 2 * ROWS), BF16),),
        in_specs=smem(5) + [pl.BlockSpec((share, NY, 128), lambda view: (view, 0, 0)), per_view(ROWS, 2 * ROWS),
                            per_view(ROWS, ROWS), per_view(128, ROWS)] + vmem(1),
        out_specs=tuple(vmem(4)) + (per_view(ROWS, 2 * ROWS),),
        scratch_shapes=[pltpu.VMEM((2 * SLOTS, NY, 128), F32), pltpu.VMEM((QUADS, VIEWS * 64, ROWS), BF16),
                        pltpu.VMEM((512, 512), BF16)],
        name="first_adjoint",
        compiler_params=room(60),
    )(start, source, place, inverse, offset, incoming, blurred, kyt, kxt, bza)


def join_columns_kernel(offset_ref, edge_ref, main_ref, tail_ref, from_left_ref, from_right_ref, out_main_ref, out_tail_ref,
                        low_ref, high_ref):
    block = lane_block((64, 128))
    low_half = block < 2
    bound = partial_bound(offset_ref)
    scale = tall(32767.0 / bound)
    left_step = tall(bound * (edge_ref[0] / 32767.0))
    right_step = tall(bound * (edge_ref[1] / 32767.0))

    def pair(quad, carry):
        packed_left = from_fixed(from_left_ref[QUADS + quad], left_step)
        packed_right = from_fixed(from_right_ref[QUADS + quad], right_step)
        for second, member in enumerate((quad, quad + QUADS // 2)):
            rows = pl.ds(pl.multiple_of(member * 64, 64), 64)
            left = main_ref[0, rows, :] + from_fixed(from_left_ref[member], left_step)
            right = main_ref[1, rows, :] + from_fixed(from_right_ref[member], right_step)
            if second:
                extra = jnp.where(low_half, rotate(packed_left, 64), packed_right)
            else:
                extra = jnp.where(low_half, packed_left, rotate(packed_right, 64))
            tail = tail_ref[member] + extra
            out_main_ref[0, rows, :] = left
            out_main_ref[1, rows, :] = right
            out_tail_ref[member] = tail
            low = jnp.where(block == 1, rotate(left, 32), tail)
            low = jnp.where(block == 3, rotate(right, 96), low)
            high = jnp.where(block == 0, rotate(left, 32), tail)
            high = jnp.where(block == 2, rotate(right, 96), high)
            low_ref[member] = to_fixed(low, scale)
            high_ref[member] = to_fixed(high, scale)
        return carry

    lax.fori_loop(0, QUADS // 2, pair, 0)


def join_columns(offset, edges, main, tail, from_left, from_right):
    return pl.pallas_call(
        join_columns_kernel,
        out_shape=(
            held((2, 1024, 128), F32),
            held((QUADS, 64, 128), F32),
            held((QUADS, 64, 128), I16),
            held((QUADS, 64, 128), I16),
        ),
        in_specs=smem(2) + vmem(4),
        out_specs=tuple(vmem(4)),
        name="join_columns",
        compiler_params=room(48),
    )(offset, edges, *stay(main, tail, from_left, from_right))


def joined_planes(quad, steps, block, main_ref, tail_ref, from_low_ref, from_high_ref):
    rows = pl.ds(pl.multiple_of(quad * 64, 64), 64)
    low = from_fixed(from_low_ref[quad], steps[0])
    high = from_fixed(from_high_ref[quad], steps[1])
    left = main_ref[0, rows, :]
    left = left + jnp.where(block == 0, rotate(low, 96), 0.0) + jnp.where(block == 3, rotate(high, 96), 0.0)
    right = main_ref[1, rows, :]
    right = right + jnp.where(block == 0, rotate(low, 32), 0.0) + jnp.where(block == 3, rotate(high, 32), 0.0)
    tail = tail_ref[quad] + jnp.where(block % 2 == 0, low, high)
    return rows, left, right, tail


def depth_steps(bound, edge_ref):
    return tall(bound * (edge_ref[2] / 32767.0)), tall(bound * (edge_ref[3] / 32767.0))


def second_kernel(offset_ref, edge_ref, part_main_ref, part_tail_ref, from_low_ref, from_high_ref, estimate_main_ref,
                  estimate_tail_ref, scale_main_ref, scale_tail_ref, bzf_ref, bza_ref, average_ref, ky_ref, kx_ref,
                  kyt_ref, kxt_ref, own_estimate_ref, own_ref, own_tail_ref, to_left_ref, to_right_ref, new_main_ref,
                  tail_estimate_ref, planes_ref, depth_ref):
    step = pl.program_id(0)

    @pl.when(step == 0)
    def _():
        block = lane_block((64, 128))
        steps = depth_steps(partial_bound(offset_ref), edge_ref)

        def renew(quad, carry):
            rows, left, right, tail = joined_planes(
                quad, steps, block, part_main_ref, part_tail_ref, from_low_ref, from_high_ref)
            left = estimate_main_ref[0, rows, :] * left * scale_main_ref[0, rows, :]
            right = estimate_main_ref[1, rows, :] * right * scale_main_ref[1, rows, :]
            new_main_ref[0, rows, :] = left
            new_main_ref[1, rows, :] = right
            own_estimate_ref[quad] = own_lanes(left * scale_main_ref[0, rows, :], right * scale_main_ref[1, rows, :])
            tail_estimate_ref[quad] = estimate_tail_ref[quad] * tail * scale_tail_ref[quad]
            return carry

        lax.fori_loop(0, QUADS, renew, 0)
        forward_depth(new_main_ref, tail_estimate_ref, bzf_ref, planes_ref)

    views = [step * 2, step * 2 + 1]
    blurred = [forward_plane(views[k], planes_ref, ky_ref[k], kx_ref[k]) + offset_ref[views[k]] for k in range(2)]
    quotients = [average_ref[k].astype(F32) / blurred[k] for k in range(2)]
    for k in range(2):
        adjoint_plane(views[k], quotients[k], kyt_ref[k], kxt_ref[k], depth_ref)

    @pl.when(step == VIEWS // 2 - 1)
    def _():
        scale = tall(32767.0 / partial_bound(offset_ref))
        adjoint_depth(scale, bza_ref, depth_ref, own_ref, own_tail_ref, to_left_ref, to_right_ref, last=True)


def second(offset, edges, *operands):
    return pl.pallas_call(
        second_kernel,
        grid=(VIEWS // 2,),
        out_shape=(held((QUADS, 64, 128), F32),) * 3 + (held((QUADS, 64, 128), I16),) * 2,
        in_specs=smem(2) + vmem(10) + [per_view(ROWS, 2 * ROWS), per_view(ROWS, ROWS), per_view(ROWS, 128),
                                       per_view(ROWS, ROWS), per_view(128, ROWS)],
        out_specs=tuple(vmem(5)),
        scratch_shapes=[pltpu.VMEM((2, 1024, 128), F32), pltpu.VMEM((QUADS, 64, 128), F32),
                        pltpu.VMEM((VIEWS * 4, ROWS, ROWS), BF16), pltpu.VMEM((QUADS, VIEWS * 64, ROWS), BF16)],
        name="second",
        compiler_params=room(52),
    )(offset, edges, *stay(*operands[:4]), *operands[4:])


def join_own_kernel(offset_ref, edge_ref, own_ref, tail_ref, from_left_ref, from_right_ref, out_ref, low_ref, high_ref):
    block = lane_block((64, 128))
    near = lax.broadcasted_iota(I32, (64, 128), 1) % PART < HALO
    bound = partial_bound(offset_ref)
    scale = tall(32767.0 / bound)
    left_step = tall(bound * (edge_ref[0] / 32767.0))
    right_step = tall(bound * (edge_ref[1] / 32767.0))

    def four_quads(quad, carry):
        low = jnp.zeros((64, 128), F32)
        high = jnp.zeros((64, 128), F32)
        for k in range(4):
            member = quad + k * 4
            left = from_fixed(from_left_ref[member], left_step)
            right = from_fixed(from_right_ref[member], right_step)
            out_ref[member] = own_ref[member] + own_lanes(left, right)
            tail = tail_ref[member] + jnp.where(near, left, right)
            low = jnp.where(block == k, rotate(tail, PART * k), low)
            high = jnp.where(block == k, rotate(tail, PART * k - PART), high)
        low_ref[quad] = to_fixed(low, scale)
        high_ref[quad] = to_fixed(high, scale)
        return carry

    lax.fori_loop(0, QUADS // 4, four_quads, 0)


def join_own(offset, edges, own, tail, from_left, from_right):
    return pl.pallas_call(
        join_own_kernel,
        out_shape=(held((QUADS, 64, 128), F32), held((QUADS // 4, 64, 128), I16), held((QUADS // 4, 64, 128), I16)),
        in_specs=smem(2) + vmem(4),
        out_specs=tuple(vmem(3)),
        name="join_own",
        compiler_params=room(48),
    )(offset, edges, *stay(own, tail, from_left, from_right))


def finish_kernel(offset_ref, edge_ref, own_ref, from_low_ref, from_high_ref, estimate_ref, out_ref, value_ref):
    block = lane_block((64, 128))
    steps = depth_steps(partial_bound(offset_ref), edge_ref)

    def four_quads(quad, largest):
        low = from_fixed(from_low_ref[quad], steps[0])
        high = from_fixed(from_high_ref[quad], steps[1])
        for k in range(4):
            member = quad + k * 4
            summed = own_ref[member] + jnp.where(block == 0, rotate(low, -PART * k), 0.0)
            summed = summed + jnp.where(block == 3, rotate(high, 96 - PART * k), 0.0)
            value = estimate_ref[member] * summed
            value_ref[member] = value
            largest = jnp.maximum(largest, value)
        return largest

    largest = lax.fori_loop(0, QUADS // 4, four_quads, jnp.zeros((64, 128), F32))
    unit = (jnp.max(largest) * 64.0).astype(I32) + 1
    vector = jnp.full((16, 128), unit, I32)
    out_ref[1024:1040, :] = (vector >> 15).astype(I16)
    out_ref[1040:1056, :] = (vector & 32767).astype(I16)
    factor = (32767.0 * 64.0) / vector.astype(F32)

    def sixteen_rows(n, carry):
        for j in range(0, 16, 2):
            rows = slice(j * 4, j * 4 + 8)
            ends = [swap_fours(value_ref[n * 4 + 2 * m, rows, :], value_ref[n * 4 + 2 * m + 1, rows, :])
                    for m in range(2)]
            for odd in range(2):
                first = pl.multiple_of((j + odd) * NY + n * 16, 16)
                out_ref[pl.ds(first, 16), :] = to_fixed(
                    jnp.concatenate([ends[0][odd], ends[1][odd]], axis=0), factor)
        return carry

    lax.fori_loop(0, 4, sixteen_rows, 0)


def finish(offset, edges, own, from_low, from_high, estimate):
    return pl.pallas_call(
        finish_kernel,
        out_shape=held((1056, 128), I16),
        in_specs=smem(2) + vmem(4),
        out_specs=vmem(1)[0],
        scratch_shapes=[pltpu.VMEM((QUADS, 64, 128), F32)],
        name="finish",
        compiler_params=room(52),
    )(offset, edges, *stay(own, from_low, from_high, estimate))


def assemble_kernel(index_ref, *refs):
    chunk_refs, out_ref, buffer_ref = refs[:8], refs[8], refs[9]
    part = index_ref[0]

    @pl.when(pl.program_id(0) == 0)
    def _():
        for place in range(8):
            owner = ((part // 2 + place % 4) % 4) * 2 + (part % 2 if place < 4 else 1 - part % 2)
            buffer_ref[owner] = chunk_refs[place][...]

    block = lane_block((16, 128))
    even = block % 2 == 0
    units = []
    for half in range(2):
        unit = jnp.zeros((16, 128), F32)
        for k in range(4):
            digits = (buffer_ref[half * 4 + k, 1024:1040, :].astype(I32) * 32768
                      + buffer_ref[half * 4 + k, 1040:1056, :].astype(I32))
            unit = jnp.where(block == k, digits.astype(F32) * (1.0 / (64.0 * 32767.0)), unit)
        units.append(unit)
    step = pl.program_id(0)

    def sixteen_rows(n, carry):
        for j in range(4):
            rows = pl.ds(pl.multiple_of((step * 4 + j) * NY + n * 16, 16), 16)
            for half in range(2):
                c0, c1, c2, c3 = (buffer_ref[half * 4 + k, rows, :].astype(I32).astype(F32) for k in range(4))
                a0 = jnp.where(block < 2, c0, rotate(c2, 64))
                a1 = jnp.where(block < 2, c1, rotate(c3, 64))
                a2 = jnp.where(block < 2, rotate(c0, 64), c2)
                a3 = jnp.where(block < 2, rotate(c1, 64), c3)
                results = (jnp.where(even, a0, rotate(a1, 32)), jnp.where(even, rotate(a0, 96), a1),
                           jnp.where(even, a2, rotate(a3, 32)), jnp.where(even, rotate(a2, 96), a3))
                for h in range(4):
                    out_ref[h, 0, j, pl.ds(pl.multiple_of(n * 16, 16), 16), half * 128:(half + 1) * 128] = (
                        results[h] * units[half])
        return carry

    lax.fori_loop(0, 4, sixteen_rows, 0)


def assemble(index, chunks):
    return pl.pallas_call(
        assemble_kernel,
        grid=(4,),
        out_shape=jax.ShapeDtypeStruct((4, 4, 4, NY, 256), F32),
        in_specs=smem(1) + vmem(8),
        out_specs=pl.BlockSpec((4, 1, 4, NY, 256), lambda step: (0, step, 0, 0, 0)),
        scratch_shapes=[pltpu.VMEM((VIEWS, 1056, 128), I16)],
        name="assemble",
        compiler_params=room(58),
    )(index, *stay(*chunks)).reshape(64, NY, 256)


def to_neighbours(upward, downward, axis):
    count = lax.axis_size(axis)
    from_low = lax.ppermute(upward, axis, [(i, (i + 1) % count) for i in range(count)])
    from_high = lax.ppermute(downward, axis, [((i + 1) % count, i) for i in range(count)])
    return from_low, from_high


def gather_parts(own):
    parts = [own] + [
        lax.ppermute(own, "view", [((i + 2 * step) % VIEWS, i) for i in range(VIEWS)]) for step in (1, 3, 2)
    ]
    parts = [parts[0], parts[1], parts[3], parts[2]]
    return parts, [lax.ppermute(part, "view", [(i, i ^ 1) for i in range(VIEWS)]) for part in parts]


def column_sums(kernel, shift, positions, length):
    radius = (TAPS - 1) // 2
    source = (positions[None, :, None] - shift[:, None, None]
              - jnp.arange(TAPS, dtype=I32)[None, None, :] + radius)
    inside = (source >= 0) & (source < length)
    return jnp.sum(jnp.where(inside, kernel[:, None, :], 0.0), axis=2)


def program(estimate0, pieces, dest_block, slot_index, psf_shift, psf_taps, background):
    block_count = lax.axis_size("block")
    my_view = lax.axis_index("view")
    my_block = lax.axis_index("block")
    edges = jnp.stack([my_view > 0, my_view < VIEWS - 1, my_block > 0, my_block < block_count - 1]).astype(F32)
    targets = dest_block[:, :, 0].reshape(VIEWS, block_count, SLOTS)
    slots = slot_index.reshape(VIEWS, block_count, SLOTS)

    index = my_view.reshape(1).astype(I32)
    low, high = window_ends(index, estimate0)
    own_targets = lax.dynamic_slice(targets, (my_view, my_block, 0), (1, 1, SLOTS)).reshape(SLOTS)
    outgoing = pack_pieces(own_targets, pieces[0], block_count)
    low, high, outgoing = lax.optimization_barrier((low, high, outgoing))
    from_low, from_high = to_neighbours(high, low, "block")
    incoming = lax.all_to_all(outgoing.reshape(VIEWS * block_count, CAP, NY, 128), ("view", "block"), 0, 0, tiled=True)
    incoming = incoming.reshape(VIEWS * block_count * CAP, NY, 128)

    main = window_estimate(index, estimate0)
    kernel = psf_taps / jnp.sum(psf_taps, axis=2, keepdims=True)
    ky, kyt, kx, kxt, bzf, bza = build_bands(kernel.reshape(-1), psf_shift.reshape(-1))
    blurred, tail = forward(edges, main, from_low, from_high, bzf, ky, kx)

    earlier = jnp.tril(jnp.ones((SLOTS, SLOTS), jnp.bool_), -1)
    same = (targets[:, :, :, None] == targets[:, :, None, :]) & earlier[None, None]
    ranks = jnp.sum(same.astype(I32), axis=3)
    mine = targets == my_block
    received = jnp.arange(CAP, dtype=I32)
    slot_of = jnp.sum(
        jnp.where(mine[..., None] & (ranks[..., None] == received), slots[..., None] + 1, 0), axis=2
    ).reshape(VIEWS, block_count * CAP) - 1
    hits = slot_of[:, :, None] == jnp.arange(SLOTS, dtype=I32)
    counts = jnp.sum(hits.astype(I32), axis=1)
    inverse = 1.0 / jnp.maximum(counts, 1).astype(F32)
    entries = VIEWS * block_count * CAP
    number = jnp.arange(entries, dtype=I32)
    place_of = jnp.where(slot_of >= 0, slot_of + jnp.arange(VIEWS, dtype=I32)[:, None] * SLOTS, -1).reshape(entries)
    before = (place_of[None, :] >= 0) & (number[None, :] < number[:, None])
    position = jnp.where(place_of >= 0, jnp.sum(before.astype(I32), axis=1), -1)
    chosen = position[:, None] == number[None, :]
    source = jnp.sum(jnp.where(chosen, number[:, None], 0), axis=0)
    place = jnp.sum(jnp.where(chosen, place_of[:, None], 0), axis=0)
    start = jnp.sum(((place_of >= 0)[:, None]
                     & (number[:, None] // (block_count * CAP) < jnp.arange(VIEWS + 1))).astype(I32), axis=0)

    global_slot = (targets * SLOTS + slots).reshape(VIEWS, block_count * SLOTS)
    all_slots = jnp.arange(block_count * SLOTS, dtype=I32)
    occupied = jnp.any(global_slot[:, :, None] == all_slots, axis=1)
    mask = jnp.repeat(occupied.astype(F32), 4, axis=1)
    padded = jnp.pad(mask, ((0, 0), (2 * HALO, 2 * HALO)))
    window = lax.dynamic_slice_in_dim(padded, my_block * 64, 128, 1)
    depth = lax.broadcasted_iota(I32, (96, 128), 0) + HALO - lax.broadcasted_iota(I32, (96, 128), 1)
    tap = depth[None] - psf_shift[:, 0, None, None] + (TAPS - 1) // 2
    weight_depth = jnp.zeros((VIEWS, 96), F32)
    band = jnp.zeros((VIEWS, 96, 128), F32)
    for j in range(TAPS):
        band = jnp.where(tap == j, kernel[:, 0, j, None, None], band)
    weight_depth = jnp.sum(band * window[:, None, :], axis=2)
    weight_rows = column_sums(kernel[:, 1], psf_shift[:, 1], jnp.arange(NY, dtype=I32), NY)
    columns = my_view * PART - HALO + jnp.arange(2 * PART, dtype=I32)
    weight_columns = column_sums(kernel[:, 2], psf_shift[:, 2], columns, 256).reshape(VIEWS, 2, PART)
    by_group = weight_depth.reshape(VIEWS, 6, 16)
    planes = by_group[:, :, :, None, None] * weight_columns[:, None, None, :, :]
    planes = planes.transpose(0, 3, 2, 1, 4)
    weight_main = planes[:, :, :, 1:5].reshape(VIEWS, 2, 16, 128)
    weight_tail = jnp.stack([planes[:, :, :, 0], planes[:, :, :, 5]], axis=3)
    weight_tail = weight_tail.transpose(0, 2, 1, 3, 4).reshape(VIEWS, 16, 128)
    scale_main, scale_tail = build_weights(
        weight_rows.reshape(-1), jnp.repeat(weight_main, 4, axis=2), jnp.repeat(weight_tail, 4, axis=1))

    incoming, scale_main, scale_tail = lax.optimization_barrier((incoming, scale_main, scale_tail))
    part_main, part_tail, to_left, to_right, average = first_adjoint(
        start, source, place, inverse.reshape(-1), background, incoming, blurred, kyt, kxt, bza)
    from_left, from_right = to_neighbours(to_right, to_left, "view")
    part_main, part_tail, low, high = join_columns(background, edges, part_main, part_tail, from_left, from_right)
    from_low, from_high = to_neighbours(high, low, "block")

    estimate, own, own_tail, to_left, to_right = second(
        background, edges, part_main, part_tail, from_low, from_high, main, tail, scale_main, scale_tail,
        bzf, bza, average, ky, kx, kyt, kxt)
    from_left, from_right = to_neighbours(to_right, to_left, "view")
    own, low, high = join_own(background, edges, own, own_tail, from_left, from_right)
    from_low, from_high = to_neighbours(high, low, "block")
    own = finish(background, edges, own, from_low, from_high, estimate)

    mine, partners = gather_parts(own)
    return assemble(index, mine + partners)


def solution(mesh):
    return jax.shard_map(
        program,
        mesh=mesh,
        in_specs=(
            P("block", None, None),
            P("view", "block", None, None, None),
            P(),
            P(),
            P(),
            P(),
            P(),
        ),
        out_specs=P("block", None, None),
        check_vma=False,
    )
```

```python
import jax
import jax.numpy as jnp
from jax import lax
from jax.experimental import pallas as pl
from jax.experimental.pallas import tpu as pltpu
from jax.sharding import PartitionSpec as P


CAP = 2
TAPS = 21
HALO = 16
VIEWS = 8
SLOTS = 16
NY = 64
PART = 32
ROWS = 256
QUADS = 16

F32 = jnp.float32
BF16 = jnp.bfloat16
I32 = jnp.int32
I16 = jnp.int16


def lane_block(shape):
    return lax.broadcasted_iota(I32, shape, len(shape) - 1) // PART


def rotate(value, amount):
    return pltpu.roll(value, amount % 128, value.ndim - 1)


def digit_swap(shape):
    row = lax.broadcasted_iota(I32, shape, 0)
    column = lax.broadcasted_iota(I32, shape, 1)
    target = ((row // PART) % 4) * 128 + (row // 128) * PART + row % PART
    return jnp.where(column == target, 1.0, 0.0).astype(BF16)


def swap_fours(first, second):
    upper = lax.broadcasted_iota(I32, first.shape, 0) < 4
    return (jnp.where(upper, first, pltpu.roll(second, 4, 0)),
            jnp.where(upper, pltpu.roll(first, 4, 0), second))


def held(shape, dtype):
    return pltpu.VMEM(shape, dtype)


def stay(*arrays):
    return tuple(pltpu.with_memory_space_constraint(array, pltpu.VMEM) for array in arrays)


def room(mebibytes):
    return pltpu.CompilerParams(vmem_limit_bytes=mebibytes << 20)


def vmem(count):
    return [pl.BlockSpec(memory_space=pltpu.VMEM)] * count


def smem(count):
    return [pl.BlockSpec(memory_space=pltpu.SMEM)] * count


def to_fixed(value, scale):
    return (value * scale + 0.5).astype(I32).astype(I16)


def from_fixed(value, step):
    return value.astype(I32).astype(F32) * step


def partial_bound(offset_ref):
    total = 0.0
    for view in range(VIEWS):
        total = total + 2.0 / jnp.full((8, 128), offset_ref[view], F32)
    return total * 1.05


def band_kernel(taps_ref, shift_ref, ky_ref, kyt_ref, kx_ref, kxt_ref, bzf_ref, bza_ref):
    radius = (TAPS - 1) // 2

    def fill(difference, view, axis):
        result = jnp.zeros(difference.shape, F32)
        for tap in range(TAPS):
            result = jnp.where(difference == tap, taps_ref[(view * 3 + axis) * TAPS + tap], result)
        return result

    def one_view(view, carry):
        shift_z = shift_ref[view * 3]
        shift_y = shift_ref[view * 3 + 1]
        shift_x = shift_ref[view * 3 + 2]
        row = lax.broadcasted_iota(I32, (16, 2 * ROWS), 0)
        lane = lax.broadcasted_iota(I32, (16, 2 * ROWS), 1)
        offset = (lane // 16 - 16) * 4 + lane % 4 - row % 4
        same = (lane // 4) % 4 == row // 4
        for strip, target_ref in ((jnp.where(same, offset - shift_y + radius, -1), ky_ref),
                                  (jnp.where(same, -offset - shift_y + radius, -1), kyt_ref)):
            values = fill(strip, view, 1)
            for quad in range(QUADS):
                target_ref[view, quad * 16:(quad + 1) * 16, :] = values[
                    :, ROWS - quad * 16:2 * ROWS - quad * 16].astype(BF16)
        row = lax.broadcasted_iota(I32, (PART, 128), 0)
        lane = lax.broadcasted_iota(I32, (PART, 128), 1)
        for half in range(2):
            base = fill(half * PART + row - (lane % PART + HALO) - shift_x + radius, view, 2)
            for block in range(4):
                first = half * 128 + block * PART
                kx_ref[view, first:first + PART, :] = jnp.where(lane // PART == block, base, 0.0).astype(BF16)
            base = fill(half * PART + lane % PART - (row + HALO) - shift_x + radius, view, 2)
            for block in range(4):
                kxt_ref[view, block * PART:(block + 1) * PART, half * 128:(half + 1) * 128] = jnp.where(
                    lane // PART == block, base, 0.0).astype(BF16)
        row = lax.broadcasted_iota(I32, (64, 192), 0)
        lane = lax.broadcasted_iota(I32, (64, 192), 1)
        difference = jnp.where(lane % 4 == row % 4, lane // 4 - 16 - row // 4 - shift_z + radius, -1)
        bzf_ref[pl.ds(pl.multiple_of(view * 64, 64), 64), :] = fill(difference, view, 0).astype(BF16)
        return carry

    lax.fori_loop(0, VIEWS, one_view, 0)
    row = lax.broadcasted_iota(I32, (192, 128), 0)
    lane = lax.broadcasted_iota(I32, (192, 128), 1)
    left = lane < 64
    for pair in range(VIEWS // 2):
        shift = jnp.where(left, shift_ref[pair * 6], shift_ref[pair * 6 + 3])
        difference = jnp.where(lane % 4 == row % 4, row // 4 - 16 - (lane // 4) % 16 - shift + radius, -1)
        total = jnp.zeros((192, 128), F32)
        for tap in range(TAPS):
            value = jnp.where(left, taps_ref[pair * 6 * TAPS + tap], taps_ref[(pair * 6 + 3) * TAPS + tap])
            total = jnp.where(difference == tap, value, total)
        bza_ref[:, pair * 128:(pair + 1) * 128] = total.astype(BF16)


def build_bands(taps, shifts):
    return pl.pallas_call(
        band_kernel,
        out_shape=(
            jax.ShapeDtypeStruct((VIEWS, ROWS, ROWS), BF16),
            jax.ShapeDtypeStruct((VIEWS, ROWS, ROWS), BF16),
            jax.ShapeDtypeStruct((VIEWS, ROWS, 128), BF16),
            jax.ShapeDtypeStruct((VIEWS, 128, ROWS), BF16),
            jax.ShapeDtypeStruct((VIEWS * 64, 192), BF16),
            jax.ShapeDtypeStruct((192, VIEWS * 64), BF16),
        ),
        in_specs=smem(2),
        out_specs=tuple(vmem(6)),
        name="bands",
    )(taps, shifts)


def pack_kernel(index_ref, target_ref, pieces_ref, first_ref, last_ref, out_ref, low_ref, high_ref, stage_ref, swap_ref,
                sent_ref):
    step = pl.program_id(0)
    count = target_ref.shape[0]

    @pl.when(step == 0)
    def _():
        swap_ref[...] = digit_swap((512, 512))

    rows = []
    for k in range(4):
        for half in range(2):
            rows.append(jnp.concatenate(
                [pieces_ref[k, q, :, half * 128:(half + 1) * 128] for q in range(4)], axis=1))
    mixed = jnp.dot(jnp.concatenate(rows, axis=0), swap_ref[...], preferred_element_type=F32).astype(BF16)
    for k in range(4):
        piece = step * 4 + k
        target = target_ref[piece]
        rank = jnp.int32(0)
        for other in range(count):
            rank = rank + jnp.where((target_ref[other] == target) & (other < piece), 1, 0)
        slot = target * CAP + rank
        for half in range(2):
            first = (k * 2 + half) * NY
            for part in range(4):
                stage_ref[piece, half * 4 + part] = mixed[first:first + NY, part * 128:(part + 1) * 128]
        pltpu.make_async_copy(stage_ref.at[piece], out_ref.at[:, slot], sent_ref.at[piece]).start()

    part = index_ref[0]
    amount = (16 - PART * part + 256) % 256
    lane = lax.broadcasted_iota(I32, (32, 128), 1)
    column = part * PART - HALO + lane % 64
    inside = (column >= 0) & (column < 256)
    for source_ref, target_ref_out in ((first_ref, low_ref), (last_ref, high_ref)):
        planes = []
        for k in range(4):
            plane = source_ref[k]
            top = pltpu.roll(plane[:32], amount, 1)[:, :128]
            bottom = pltpu.roll(plane[32:], (amount + 64) % 256, 1)[:, :128]
            planes.append(jnp.where(inside, jnp.where(lane < 64, top, bottom), 0.0))
        for m in range(4):
            rows = slice(m * 8, m * 8 + 8)
            front = swap_fours(planes[0][rows], planes[1][rows])
            back = swap_fours(planes[2][rows], planes[3][rows])
            for odd in range(2):
                target_ref_out[m * 2 + odd, pl.ds(pl.multiple_of(step * 16, 16), 16), :] = jnp.concatenate(
                    [front[odd], back[odd]], axis=0).astype(BF16)

    @pl.when(step == 3)
    def _():
        for piece in range(count):
            pltpu.make_async_copy(stage_ref.at[piece], out_ref.at[:, 0], sent_ref.at[piece]).wait()


def pack_pieces(index, targets, pieces, estimate, block_count):
    count = pieces.shape[0]
    return pl.pallas_call(
        pack_kernel,
        grid=(4,),
        out_shape=(
            jax.ShapeDtypeStruct((VIEWS, block_count * CAP, NY, 128), BF16),
            jax.ShapeDtypeStruct((8, 64, 128), BF16),
            jax.ShapeDtypeStruct((8, 64, 128), BF16),
        ),
        in_specs=smem(2) + [pl.BlockSpec((4,) + pieces.shape[1:], lambda step: (step, 0, 0, 0)),
                            pl.BlockSpec((4, NY, 256), lambda step: (step, 0, 0)),
                            pl.BlockSpec((4, NY, 256), lambda step: (12 + step, 0, 0))],
        out_specs=(pl.BlockSpec(memory_space=pl.ANY),) + tuple(vmem(2)),
        scratch_shapes=[pltpu.VMEM((count, VIEWS, NY, 128), BF16), pltpu.VMEM((512, 512), BF16),
                        pltpu.SemaphoreType.DMA((count,))],
        name="pack",
    )(index, targets, pieces, estimate, estimate)


def window_kernel(index_ref, estimate_ref, main_ref):
    part = index_ref[0]
    block = lane_block((NY, 128))
    lane = lax.broadcasted_iota(I32, (NY, 128), 1) % PART

    def two_planes(step, carry):
        for half in range(2):
            column = (part + half) * PART - HALO + lane
            inside = (column >= 0) & (column < 256)
            planes = []
            for odd in range(2):
                result = jnp.zeros((NY, 128), F32)
                for h in range(4):
                    plane = estimate_ref[h * 16 + step * 2 + odd]
                    amount = (16 - PART * part - PART * half + PART * h + 512) % 256
                    result = jnp.where(block == h, pltpu.roll(plane, amount, 1)[:, :128], result)
                planes.append(jnp.where(inside, result, 0.0))
            for m in range(8):
                low, high = swap_fours(planes[0][m * 8:m * 8 + 8], planes[1][m * 8:m * 8 + 8])
                main_ref[half, pl.ds(pl.multiple_of(m * 128 + step * 8, 8), 8), :] = low
                main_ref[half, pl.ds(pl.multiple_of(m * 128 + 64 + step * 8, 8), 8), :] = high
        return carry

    lax.fori_loop(0, 8, two_planes, 0)


def window_estimate(index, estimate):
    return pl.pallas_call(
        window_kernel,
        out_shape=jax.ShapeDtypeStruct((2, 1024, 128), F32),
        in_specs=smem(1) + vmem(1),
        out_specs=vmem(1)[0],
        name="window",
    )(index, estimate)


def build_tail(edge_ref, from_low_ref, from_high_ref, tail_ref):
    block = lane_block((64, 128))

    def two_quads(quad, carry):
        low = from_low_ref[quad].astype(F32) * edge_ref[2]
        high = from_high_ref[quad].astype(F32) * edge_ref[3]
        for member in range(2):
            base = member * 64
            result = jnp.where(block == 0, rotate(low, -base), rotate(low, 32 - base))
            result = jnp.where(block == 1, rotate(high, 32 - base), result)
            tail_ref[quad + member * 8] = jnp.where(block == 3, rotate(high, 64 - base), result)
        return carry

    lax.fori_loop(0, QUADS // 2, two_quads, 0)


def weight_kernel(rows_ref, main_ref, tail_ref, out_main_ref, out_tail_ref):
    quarter = lax.broadcasted_iota(I32, (64, 128), 0) % 4

    def one_quad(quad, carry):
        rows = pl.ds(pl.multiple_of(quad * 64, 64), 64)
        totals = [jnp.zeros((64, 128), F32) for _ in range(3)]
        for view in range(VIEWS):
            factor = jnp.full((64, 128), rows_ref[view * NY + quad * 4], F32)
            for k in range(1, 4):
                factor = jnp.where(quarter == k, rows_ref[view * NY + quad * 4 + k], factor)
            totals[0] = totals[0] + factor * main_ref[view, 0]
            totals[1] = totals[1] + factor * main_ref[view, 1]
            totals[2] = totals[2] + factor * tail_ref[view]
        out_main_ref[0, rows, :] = 1.0 / jnp.maximum(totals[0], 1.0)
        out_main_ref[1, rows, :] = 1.0 / jnp.maximum(totals[1], 1.0)
        out_tail_ref[quad] = 1.0 / jnp.maximum(totals[2], 1.0)
        return carry

    lax.fori_loop(0, QUADS, one_quad, 0)


def build_weights(rows, main, tail):
    return pl.pallas_call(
        weight_kernel,
        out_shape=(
            jax.ShapeDtypeStruct((2, 1024, 128), F32),
            jax.ShapeDtypeStruct((QUADS, 64, 128), F32),
        ),
        in_specs=smem(1) + vmem(2),
        out_specs=tuple(vmem(2)),
        name="weights",
    )(rows, main, tail)


def forward_depth(main_ref, tail_ref, bzf_ref, planes_ref):
    block = lane_block((64, 128))

    def stacked(quad):
        rows = pl.ds(pl.multiple_of(quad * 64, 64), 64)
        left = main_ref[0, rows, :]
        right = main_ref[1, rows, :]
        tail = tail_ref[quad]
        turned = rotate(tail, 64)
        lower = jnp.concatenate([jnp.where(block == 0, tail, rotate(left, 32)),
                                 jnp.where(block == 0, turned, rotate(right, 32))], axis=1)
        upper = jnp.concatenate([jnp.where(block == 3, turned, rotate(left, 96)),
                                 jnp.where(block == 3, tail, rotate(right, 96))], axis=1)
        return jnp.concatenate([lower, jnp.concatenate([left, right], axis=1), upper], axis=0).astype(BF16)

    def two_quads(step, carry):
        both = jnp.concatenate([stacked(step * 2), stacked(step * 2 + 1)], axis=1)
        blurred = jnp.dot(bzf_ref[...], both, preferred_element_type=F32).astype(BF16)
        for member in range(2):
            first = pl.multiple_of(step * 32 + member * 16, 16)
            for group in range(VIEWS * 4):
                planes_ref[group, pl.ds(first, 16), :] = blurred[
                    group * 16:(group + 1) * 16, member * ROWS:(member + 1) * ROWS]
        return carry

    lax.fori_loop(0, QUADS // 2, two_quads, 0, unroll=2)


def forward_plane(view, planes_ref, ky, kx):
    volume = planes_ref[pl.ds(view * 4, 4)].reshape(4 * ROWS, ROWS)
    along_x = jnp.concatenate([jnp.dot(volume[r * 512:(r + 1) * 512], kx, preferred_element_type=F32)
                               for r in range(2)], axis=0).astype(BF16)
    side = jnp.concatenate([along_x[r * ROWS:(r + 1) * ROWS] for r in range(4)], axis=1)
    return jnp.dot(ky, side, preferred_element_type=F32)


def adjoint_plane(view, quotient, kyt, kxt, depth_ref):
    along_y = jnp.dot(kyt, quotient.astype(BF16), preferred_element_type=F32).astype(BF16)
    stacked = jnp.concatenate([along_y[:, r * 128:(r + 1) * 128] for r in range(4)], axis=0)
    along_x = jnp.concatenate([jnp.dot(stacked[r * 512:(r + 1) * 512], kxt, preferred_element_type=F32)
                               for r in range(2)], axis=0).astype(BF16)
    for r in range(4):
        first = pl.multiple_of(view * 64 + r * 16, 16)
        for quad in range(QUADS):
            depth_ref[quad, pl.ds(first, 16), :] = along_x[r * ROWS + quad * 16:r * ROWS + quad * 16 + 16]


def own_lanes(left, right):
    lane = lax.broadcasted_iota(I32, left.shape, 1) % PART
    return jnp.where(lane < HALO, rotate(left, 112), rotate(right, 16))


def adjoint_depth(scale, bza_ref, depth_ref, main_ref, tail_ref, to_left_ref, to_right_ref, last=False):
    block = lane_block((64, 128))
    low_half = block < 2
    near = lax.broadcasted_iota(I32, (64, 128), 1) % PART < HALO

    def pair(quad, carry):
        tails = []
        members = (quad, quad + QUADS // 2)
        both = jnp.concatenate([depth_ref[member] for member in members], axis=1)
        summed_both = jnp.dot(bza_ref[...], both, preferred_element_type=F32)
        for index, member in enumerate(members):
            summed = summed_both[:, index * ROWS:(index + 1) * ROWS]
            mains = []
            for half in range(2):
                lanes = slice(half * 128, (half + 1) * 128)
                lower = jnp.where(block < 3, rotate(summed[:64, lanes], 96), 0.0)
                upper = jnp.where(block > 0, rotate(summed[128:, lanes], 32), 0.0)
                mains.append(summed[64:128, lanes] + lower + upper)
            tail = jnp.where(block == 0, summed[:64, :128], summed[128:, 128:])
            tail = jnp.where(block == 1, rotate(summed[128:, :128], 64), tail)
            tail = jnp.where(block == 2, rotate(summed[:64, 128:], 64), tail)
            if last:
                main_ref[member] = own_lanes(*mains)
                tail_ref[member] = jnp.where(near, rotate(tail, 112), rotate(tail, 80))
                to_left_ref[member] = to_fixed(jnp.where(near, mains[0], rotate(tail, 16)), scale)
                to_right_ref[member] = to_fixed(jnp.where(near, rotate(tail, 48), mains[1]), scale)
                continue
            rows = pl.ds(pl.multiple_of(member * 64, 64), 64)
            main_ref[0, rows, :] = mains[0]
            main_ref[1, rows, :] = mains[1]
            tail_ref[member] = tail
            to_left_ref[member] = to_fixed(mains[0], scale)
            to_right_ref[member] = to_fixed(mains[1], scale)
            tails.append(tail)
        if last:
            return carry
        to_left_ref[QUADS + quad] = to_fixed(jnp.where(low_half, tails[0], rotate(tails[1], 64)), scale)
        to_right_ref[QUADS + quad] = to_fixed(jnp.where(low_half, rotate(tails[0], 64), tails[1]), scale)
        return carry

    lax.fori_loop(0, QUADS // 2, pair, 0, unroll=2)


def tall(value):
    return jnp.concatenate([value] * 8, axis=0)


def forward_kernel(edge_ref, main_ref, from_low_ref, from_high_ref, bzf_ref, ky_ref, kx_ref, out_ref, tail_ref,
                   planes_ref):
    build_tail(edge_ref, from_low_ref, from_high_ref, tail_ref)
    forward_depth(main_ref, tail_ref, bzf_ref, planes_ref)

    def one_view(view, carry):
        out_ref[view] = forward_plane(view, planes_ref, ky_ref[view], kx_ref[view]).astype(BF16)
        return carry

    lax.fori_loop(0, VIEWS, one_view, 0)


def forward(edges, main, from_low, from_high, bzf, ky, kx):
    return pl.pallas_call(
        forward_kernel,
        out_shape=(
            jax.ShapeDtypeStruct((VIEWS, ROWS, 2 * ROWS), BF16),
            jax.ShapeDtypeStruct((QUADS, 64, 128), F32),
        ),
        in_specs=smem(1) + vmem(6),
        out_specs=tuple(vmem(2)),
        scratch_shapes=[pltpu.VMEM((VIEWS * 4, ROWS, ROWS), BF16)],
        name="forward",
    )(edges, main, from_low, from_high, bzf, ky, kx)


def per_view(*shape):
    return pl.BlockSpec((2,) + shape, lambda step: (step,) + (0,) * len(shape))


PARTIAL_SHAPES = (
    held((2, 1024, 128), F32),
    held((QUADS, 64, 128), F32),
    held((QUADS + QUADS // 2, 64, 128), I16),
    held((QUADS + QUADS // 2, 64, 128), I16),
)


def first_adjoint_kernel(start_ref, source_ref, place_ref, inverse_ref, offset_ref, incoming_ref, blurred_ref, kyt_ref,
                         kxt_ref, bza_ref, main_ref, tail_ref, to_left_ref, to_right_ref, average_ref, total_ref,
                         depth_ref, swap_ref):
    step = pl.program_id(0)

    @pl.when(step == 0)
    def _():
        swap_ref[...] = digit_swap((512, 512))

    for slot in range(2 * SLOTS):
        total_ref[slot] = jnp.zeros((NY, 128), F32)

    def add(entry, carry):
        place = place_ref[entry]
        piece = incoming_ref[source_ref[entry] - step * incoming_ref.shape[0]].astype(F32)
        slot = place - step * (2 * SLOTS)
        total_ref[slot] = total_ref[slot] + piece * inverse_ref[place]
        return carry

    lax.fori_loop(start_ref[step * 2], start_ref[step * 2 + 2], add, 0)
    rows = []
    for r in range(8):
        rows.append(jnp.concatenate(
            [total_ref[r // 4 * SLOTS + h * 4 + r % 4].astype(BF16) for h in range(4)], axis=1))
    mixed = jnp.dot(jnp.concatenate(rows, axis=0), swap_ref[...], preferred_element_type=F32)
    for r in range(8):
        lanes = slice(r % 4 * 128, r % 4 * 128 + 128)
        for m in range(8):
            first = r * NY + m * 8
            ends = []
            for q in (0, 2):
                ends.append(swap_fours(mixed[first:first + 8, q * 128:(q + 1) * 128],
                                       mixed[first:first + 8, (q + 1) * 128:(q + 2) * 128]))
            for odd in range(2):
                quad = 2 * m + odd
                average_ref[r // 4, quad * 16:quad * 16 + 16, lanes] = jnp.concatenate(
                    [ends[0][odd], ends[1][odd]], axis=0).astype(BF16)
    quotients = [average_ref[k].astype(F32) / (blurred_ref[k].astype(F32) + offset_ref[step * 2 + k]) for k in range(2)]
    for k in range(2):
        adjoint_plane(step * 2 + k, quotients[k], kyt_ref[k], kxt_ref[k], depth_ref)

    @pl.when(step == VIEWS // 2 - 1)
    def _():
        scale = tall(32767.0 / partial_bound(offset_ref))
        adjoint_depth(scale, bza_ref, depth_ref, main_ref, tail_ref, to_left_ref, to_right_ref)


def first_adjoint(start, source, place, inverse, offset, incoming, blurred, kyt, kxt, bza):
    share = incoming.shape[0] // (VIEWS // 2)
    return pl.pallas_call(
        first_adjoint_kernel,
        grid=(VIEWS // 2,),
        out_shape=PARTIAL_SHAPES + (jax.ShapeDtypeStruct((VIEWS, ROWS, 2 * ROWS), BF16),),
        in_specs=smem(5) + [pl.BlockSpec((share, NY, 128), lambda view: (view, 0, 0)), per_view(ROWS, 2 * ROWS),
                            per_view(ROWS, ROWS), per_view(128, ROWS)] + vmem(1),
        out_specs=tuple(vmem(4)) + (per_view(ROWS, 2 * ROWS),),
        scratch_shapes=[pltpu.VMEM((2 * SLOTS, NY, 128), F32), pltpu.VMEM((QUADS, VIEWS * 64, ROWS), BF16),
                        pltpu.VMEM((512, 512), BF16)],
        name="first_adjoint",
        compiler_params=room(60),
    )(start, source, place, inverse, offset, incoming, blurred, kyt, kxt, bza)


def join_columns_kernel(offset_ref, edge_ref, main_ref, tail_ref, from_left_ref, from_right_ref, out_main_ref, out_tail_ref,
                        low_ref, high_ref):
    block = lane_block((64, 128))
    low_half = block < 2
    bound = partial_bound(offset_ref)
    scale = tall(32767.0 / bound)
    left_step = tall(bound * (edge_ref[0] / 32767.0))
    right_step = tall(bound * (edge_ref[1] / 32767.0))

    def pair(quad, carry):
        packed_left = from_fixed(from_left_ref[QUADS + quad], left_step)
        packed_right = from_fixed(from_right_ref[QUADS + quad], right_step)
        for second, member in enumerate((quad, quad + QUADS // 2)):
            rows = pl.ds(pl.multiple_of(member * 64, 64), 64)
            left = main_ref[0, rows, :] + from_fixed(from_left_ref[member], left_step)
            right = main_ref[1, rows, :] + from_fixed(from_right_ref[member], right_step)
            if second:
                extra = jnp.where(low_half, rotate(packed_left, 64), packed_right)
            else:
                extra = jnp.where(low_half, packed_left, rotate(packed_right, 64))
            tail = tail_ref[member] + extra
            out_main_ref[0, rows, :] = left
            out_main_ref[1, rows, :] = right
            out_tail_ref[member] = tail
            low = jnp.where(block == 1, rotate(left, 32), tail)
            low = jnp.where(block == 3, rotate(right, 96), low)
            high = jnp.where(block == 0, rotate(left, 32), tail)
            high = jnp.where(block == 2, rotate(right, 96), high)
            low_ref[member] = to_fixed(low, scale)
            high_ref[member] = to_fixed(high, scale)
        return carry

    lax.fori_loop(0, QUADS // 2, pair, 0)


def join_columns(offset, edges, main, tail, from_left, from_right):
    return pl.pallas_call(
        join_columns_kernel,
        out_shape=(
            held((2, 1024, 128), F32),
            held((QUADS, 64, 128), F32),
            held((QUADS, 64, 128), I16),
            held((QUADS, 64, 128), I16),
        ),
        in_specs=smem(2) + vmem(4),
        out_specs=tuple(vmem(4)),
        name="join_columns",
        compiler_params=room(48),
    )(offset, edges, *stay(main, tail, from_left, from_right))


def joined_planes(quad, steps, block, main_ref, tail_ref, from_low_ref, from_high_ref):
    rows = pl.ds(pl.multiple_of(quad * 64, 64), 64)
    low = from_fixed(from_low_ref[quad], steps[0])
    high = from_fixed(from_high_ref[quad], steps[1])
    left = main_ref[0, rows, :]
    left = left + jnp.where(block == 0, rotate(low, 96), 0.0) + jnp.where(block == 3, rotate(high, 96), 0.0)
    right = main_ref[1, rows, :]
    right = right + jnp.where(block == 0, rotate(low, 32), 0.0) + jnp.where(block == 3, rotate(high, 32), 0.0)
    tail = tail_ref[quad] + jnp.where(block % 2 == 0, low, high)
    return rows, left, right, tail


def depth_steps(bound, edge_ref):
    return tall(bound * (edge_ref[2] / 32767.0)), tall(bound * (edge_ref[3] / 32767.0))


def second_kernel(offset_ref, edge_ref, part_main_ref, part_tail_ref, from_low_ref, from_high_ref, estimate_main_ref,
                  estimate_tail_ref, scale_main_ref, scale_tail_ref, bzf_ref, bza_ref, average_ref, ky_ref, kx_ref,
                  kyt_ref, kxt_ref, own_estimate_ref, own_ref, own_tail_ref, to_left_ref, to_right_ref, new_main_ref,
                  tail_estimate_ref, planes_ref, depth_ref):
    step = pl.program_id(0)

    @pl.when(step == 0)
    def _():
        block = lane_block((64, 128))
        steps = depth_steps(partial_bound(offset_ref), edge_ref)

        def renew(quad, carry):
            rows, left, right, tail = joined_planes(
                quad, steps, block, part_main_ref, part_tail_ref, from_low_ref, from_high_ref)
            left = estimate_main_ref[0, rows, :] * left * scale_main_ref[0, rows, :]
            right = estimate_main_ref[1, rows, :] * right * scale_main_ref[1, rows, :]
            new_main_ref[0, rows, :] = left
            new_main_ref[1, rows, :] = right
            own_estimate_ref[quad] = own_lanes(left * scale_main_ref[0, rows, :], right * scale_main_ref[1, rows, :])
            tail_estimate_ref[quad] = estimate_tail_ref[quad] * tail * scale_tail_ref[quad]
            return carry

        lax.fori_loop(0, QUADS, renew, 0)
        forward_depth(new_main_ref, tail_estimate_ref, bzf_ref, planes_ref)

    views = [step * 2, step * 2 + 1]
    blurred = [forward_plane(views[k], planes_ref, ky_ref[k], kx_ref[k]) + offset_ref[views[k]] for k in range(2)]
    quotients = [average_ref[k].astype(F32) / blurred[k] for k in range(2)]
    for k in range(2):
        adjoint_plane(views[k], quotients[k], kyt_ref[k], kxt_ref[k], depth_ref)

    @pl.when(step == VIEWS // 2 - 1)
    def _():
        scale = tall(32767.0 / partial_bound(offset_ref))
        adjoint_depth(scale, bza_ref, depth_ref, own_ref, own_tail_ref, to_left_ref, to_right_ref, last=True)


def second(offset, edges, *operands):
    return pl.pallas_call(
        second_kernel,
        grid=(VIEWS // 2,),
        out_shape=(held((QUADS, 64, 128), F32),) * 3 + (held((QUADS, 64, 128), I16),) * 2,
        in_specs=smem(2) + vmem(10) + [per_view(ROWS, 2 * ROWS), per_view(ROWS, ROWS), per_view(ROWS, 128),
                                       per_view(ROWS, ROWS), per_view(128, ROWS)],
        out_specs=tuple(vmem(5)),
        scratch_shapes=[pltpu.VMEM((2, 1024, 128), F32), pltpu.VMEM((QUADS, 64, 128), F32),
                        pltpu.VMEM((VIEWS * 4, ROWS, ROWS), BF16), pltpu.VMEM((QUADS, VIEWS * 64, ROWS), BF16)],
        name="second",
        compiler_params=room(52),
    )(offset, edges, *stay(*operands[:4]), *operands[4:])


def join_own_kernel(offset_ref, edge_ref, own_ref, tail_ref, from_left_ref, from_right_ref, out_ref, low_ref, high_ref):
    block = lane_block((64, 128))
    near = lax.broadcasted_iota(I32, (64, 128), 1) % PART < HALO
    bound = partial_bound(offset_ref)
    scale = tall(32767.0 / bound)
    left_step = tall(bound * (edge_ref[0] / 32767.0))
    right_step = tall(bound * (edge_ref[1] / 32767.0))

    def four_quads(quad, carry):
        low = jnp.zeros((64, 128), F32)
        high = jnp.zeros((64, 128), F32)
        for k in range(4):
            member = quad + k * 4
            left = from_fixed(from_left_ref[member], left_step)
            right = from_fixed(from_right_ref[member], right_step)
            out_ref[member] = own_ref[member] + own_lanes(left, right)
            tail = tail_ref[member] + jnp.where(near, left, right)
            low = jnp.where(block == k, rotate(tail, PART * k), low)
            high = jnp.where(block == k, rotate(tail, PART * k - PART), high)
        low_ref[quad] = to_fixed(low, scale)
        high_ref[quad] = to_fixed(high, scale)
        return carry

    lax.fori_loop(0, QUADS // 4, four_quads, 0)


def join_own(offset, edges, own, tail, from_left, from_right):
    return pl.pallas_call(
        join_own_kernel,
        out_shape=(held((QUADS, 64, 128), F32), held((QUADS // 4, 64, 128), I16), held((QUADS // 4, 64, 128), I16)),
        in_specs=smem(2) + vmem(4),
        out_specs=tuple(vmem(3)),
        name="join_own",
        compiler_params=room(48),
    )(offset, edges, *stay(own, tail, from_left, from_right))


def finish_kernel(offset_ref, edge_ref, own_ref, from_low_ref, from_high_ref, estimate_ref, out_ref, value_ref):
    block = lane_block((64, 128))
    steps = depth_steps(partial_bound(offset_ref), edge_ref)

    def four_quads(quad, largest):
        low = from_fixed(from_low_ref[quad], steps[0])
        high = from_fixed(from_high_ref[quad], steps[1])
        for k in range(4):
            member = quad + k * 4
            summed = own_ref[member] + jnp.where(block == 0, rotate(low, -PART * k), 0.0)
            summed = summed + jnp.where(block == 3, rotate(high, 96 - PART * k), 0.0)
            value = estimate_ref[member] * summed
            value_ref[member] = value
            largest = jnp.maximum(largest, value)
        return largest

    largest = lax.fori_loop(0, QUADS // 4, four_quads, jnp.zeros((64, 128), F32))
    unit = (jnp.max(largest) * 64.0).astype(I32) + 1
    vector = jnp.full((16, 128), unit, I32)
    out_ref[1024:1040, :] = (vector >> 15).astype(I16)
    out_ref[1040:1056, :] = (vector & 32767).astype(I16)
    factor = (32767.0 * 64.0) / vector.astype(F32)

    def sixteen_rows(n, carry):
        for j in range(0, 16, 2):
            rows = slice(j * 4, j * 4 + 8)
            ends = [swap_fours(value_ref[n * 4 + 2 * m, rows, :], value_ref[n * 4 + 2 * m + 1, rows, :])
                    for m in range(2)]
            for odd in range(2):
                first = pl.multiple_of((j + odd) * NY + n * 16, 16)
                out_ref[pl.ds(first, 16), :] = to_fixed(
                    jnp.concatenate([ends[0][odd], ends[1][odd]], axis=0), factor)
        return carry

    lax.fori_loop(0, 4, sixteen_rows, 0)


def finish(offset, edges, own, from_low, from_high, estimate):
    return pl.pallas_call(
        finish_kernel,
        out_shape=held((1056, 128), I16),
        in_specs=smem(2) + vmem(4),
        out_specs=vmem(1)[0],
        scratch_shapes=[pltpu.VMEM((QUADS, 64, 128), F32)],
        name="finish",
        compiler_params=room(52),
    )(offset, edges, *stay(own, from_low, from_high, estimate))


def assemble_kernel(index_ref, *refs):
    chunk_refs, out_ref, buffer_ref = refs[:8], refs[8], refs[9]
    part = index_ref[0]

    @pl.when(pl.program_id(0) == 0)
    def _():
        for place in range(8):
            owner = ((part // 2 + place % 4) % 4) * 2 + (part % 2 if place < 4 else 1 - part % 2)
            buffer_ref[owner] = chunk_refs[place][...]

    block = lane_block((16, 128))
    even = block % 2 == 0
    units = []
    for half in range(2):
        unit = jnp.zeros((16, 128), F32)
        for k in range(4):
            digits = (buffer_ref[half * 4 + k, 1024:1040, :].astype(I32) * 32768
                      + buffer_ref[half * 4 + k, 1040:1056, :].astype(I32))
            unit = jnp.where(block == k, digits.astype(F32) * (1.0 / (64.0 * 32767.0)), unit)
        units.append(unit)
    step = pl.program_id(0)

    def sixteen_rows(n, carry):
        for j in range(4):
            rows = pl.ds(pl.multiple_of((step * 4 + j) * NY + n * 16, 16), 16)
            for half in range(2):
                c0, c1, c2, c3 = (buffer_ref[half * 4 + k, rows, :].astype(I32).astype(F32) for k in range(4))
                a0 = jnp.where(block < 2, c0, rotate(c2, 64))
                a1 = jnp.where(block < 2, c1, rotate(c3, 64))
                a2 = jnp.where(block < 2, rotate(c0, 64), c2)
                a3 = jnp.where(block < 2, rotate(c1, 64), c3)
                results = (jnp.where(even, a0, rotate(a1, 32)), jnp.where(even, rotate(a0, 96), a1),
                           jnp.where(even, a2, rotate(a3, 32)), jnp.where(even, rotate(a2, 96), a3))
                for h in range(4):
                    out_ref[h, 0, j, pl.ds(pl.multiple_of(n * 16, 16), 16), half * 128:(half + 1) * 128] = (
                        results[h] * units[half])
        return carry

    lax.fori_loop(0, 4, sixteen_rows, 0)


def assemble(index, chunks):
    return pl.pallas_call(
        assemble_kernel,
        grid=(4,),
        out_shape=jax.ShapeDtypeStruct((4, 4, 4, NY, 256), F32),
        in_specs=smem(1) + vmem(8),
        out_specs=pl.BlockSpec((4, 1, 4, NY, 256), lambda step: (0, step, 0, 0, 0)),
        scratch_shapes=[pltpu.VMEM((VIEWS, 1056, 128), I16)],
        name="assemble",
        compiler_params=room(58),
    )(index, *stay(*chunks)).reshape(64, NY, 256)


def to_neighbours(upward, downward, axis):
    count = lax.axis_size(axis)
    from_low = lax.ppermute(upward, axis, [(i, (i + 1) % count) for i in range(count)])
    from_high = lax.ppermute(downward, axis, [((i + 1) % count, i) for i in range(count)])
    return from_low, from_high


def gather_parts(own):
    parts = [own] + [
        lax.ppermute(own, "view", [((i + 2 * step) % VIEWS, i) for i in range(VIEWS)]) for step in (1, 3, 2)
    ]
    parts = [parts[0], parts[1], parts[3], parts[2]]
    return parts, [lax.ppermute(part, "view", [(i, i ^ 1) for i in range(VIEWS)]) for part in parts]


def column_sums(kernel, shift, positions, length):
    radius = (TAPS - 1) // 2
    source = (positions[None, :, None] - shift[:, None, None]
              - jnp.arange(TAPS, dtype=I32)[None, None, :] + radius)
    inside = (source >= 0) & (source < length)
    return jnp.sum(jnp.where(inside, kernel[:, None, :], 0.0), axis=2)


def program(estimate0, pieces, dest_block, slot_index, psf_shift, psf_taps, background):
    block_count = lax.axis_size("block")
    my_view = lax.axis_index("view")
    my_block = lax.axis_index("block")
    edges = jnp.stack([my_view > 0, my_view < VIEWS - 1, my_block > 0, my_block < block_count - 1]).astype(F32)
    targets = dest_block[:, :, 0].reshape(VIEWS, block_count, SLOTS)
    slots = slot_index.reshape(VIEWS, block_count, SLOTS)

    index = my_view.reshape(1).astype(I32)
    own_targets = lax.dynamic_slice(targets, (my_view, my_block, 0), (1, 1, SLOTS)).reshape(SLOTS)
    outgoing, low, high = pack_pieces(index, own_targets, pieces[0], estimate0, block_count)
    from_low, from_high = to_neighbours(high, low, "block")
    incoming = lax.all_to_all(outgoing.reshape(VIEWS * block_count, CAP, NY, 128), ("view", "block"), 0, 0, tiled=True)
    incoming = incoming.reshape(VIEWS * block_count * CAP, NY, 128)

    main = window_estimate(index, estimate0)
    kernel = psf_taps / jnp.sum(psf_taps, axis=2, keepdims=True)
    ky, kyt, kx, kxt, bzf, bza = build_bands(kernel.reshape(-1), psf_shift.reshape(-1))
    blurred, tail = forward(edges, main, from_low, from_high, bzf, ky, kx)

    earlier = jnp.tril(jnp.ones((SLOTS, SLOTS), jnp.bool_), -1)
    same = (targets[:, :, :, None] == targets[:, :, None, :]) & earlier[None, None]
    ranks = jnp.sum(same.astype(I32), axis=3)
    mine = targets == my_block
    received = jnp.arange(CAP, dtype=I32)
    slot_of = jnp.sum(
        jnp.where(mine[..., None] & (ranks[..., None] == received), slots[..., None] + 1, 0), axis=2
    ).reshape(VIEWS, block_count * CAP) - 1
    hits = slot_of[:, :, None] == jnp.arange(SLOTS, dtype=I32)
    counts = jnp.sum(hits.astype(I32), axis=1)
    inverse = 1.0 / jnp.maximum(counts, 1).astype(F32)
    entries = VIEWS * block_count * CAP
    number = jnp.arange(entries, dtype=I32)
    place_of = jnp.where(slot_of >= 0, slot_of + jnp.arange(VIEWS, dtype=I32)[:, None] * SLOTS, -1).reshape(entries)
    before = (place_of[None, :] >= 0) & (number[None, :] < number[:, None])
    position = jnp.where(place_of >= 0, jnp.sum(before.astype(I32), axis=1), -1)
    chosen = position[:, None] == number[None, :]
    source = jnp.sum(jnp.where(chosen, number[:, None], 0), axis=0)
    place = jnp.sum(jnp.where(chosen, place_of[:, None], 0), axis=0)
    start = jnp.sum(((place_of >= 0)[:, None]
                     & (number[:, None] // (block_count * CAP) < jnp.arange(VIEWS + 1))).astype(I32), axis=0)

    global_slot = (targets * SLOTS + slots).reshape(VIEWS, block_count * SLOTS)
    all_slots = jnp.arange(block_count * SLOTS, dtype=I32)
    occupied = jnp.any(global_slot[:, :, None] == all_slots, axis=1)
    mask = jnp.repeat(occupied.astype(F32), 4, axis=1)
    padded = jnp.pad(mask, ((0, 0), (2 * HALO, 2 * HALO)))
    window = lax.dynamic_slice_in_dim(padded, my_block * 64, 128, 1)
    depth = lax.broadcasted_iota(I32, (96, 128), 0) + HALO - lax.broadcasted_iota(I32, (96, 128), 1)
    tap = depth[None] - psf_shift[:, 0, None, None] + (TAPS - 1) // 2
    weight_depth = jnp.zeros((VIEWS, 96), F32)
    band = jnp.zeros((VIEWS, 96, 128), F32)
    for j in range(TAPS):
        band = jnp.where(tap == j, kernel[:, 0, j, None, None], band)
    weight_depth = jnp.sum(band * window[:, None, :], axis=2)
    weight_rows = column_sums(kernel[:, 1], psf_shift[:, 1], jnp.arange(NY, dtype=I32), NY)
    columns = my_view * PART - HALO + jnp.arange(2 * PART, dtype=I32)
    weight_columns = column_sums(kernel[:, 2], psf_shift[:, 2], columns, 256).reshape(VIEWS, 2, PART)
    by_group = weight_depth.reshape(VIEWS, 6, 16)
    planes = by_group[:, :, :, None, None] * weight_columns[:, None, None, :, :]
    planes = planes.transpose(0, 3, 2, 1, 4)
    weight_main = planes[:, :, :, 1:5].reshape(VIEWS, 2, 16, 128)
    weight_tail = jnp.stack([planes[:, :, :, 0], planes[:, :, :, 5]], axis=3)
    weight_tail = weight_tail.transpose(0, 2, 1, 3, 4).reshape(VIEWS, 16, 128)
    scale_main, scale_tail = build_weights(
        weight_rows.reshape(-1), jnp.repeat(weight_main, 4, axis=2), jnp.repeat(weight_tail, 4, axis=1))

    incoming, scale_main, scale_tail = lax.optimization_barrier((incoming, scale_main, scale_tail))
    part_main, part_tail, to_left, to_right, average = first_adjoint(
        start, source, place, inverse.reshape(-1), background, incoming, blurred, kyt, kxt, bza)
    from_left, from_right = to_neighbours(to_right, to_left, "view")
    part_main, part_tail, low, high = join_columns(background, edges, part_main, part_tail, from_left, from_right)
    from_low, from_high = to_neighbours(high, low, "block")

    estimate, own, own_tail, to_left, to_right = second(
        background, edges, part_main, part_tail, from_low, from_high, main, tail, scale_main, scale_tail,
        bzf, bza, average, ky, kx, kyt, kxt)
    from_left, from_right = to_neighbours(to_right, to_left, "view")
    own, low, high = join_own(background, edges, own, own_tail, from_left, from_right)
    from_low, from_high = to_neighbours(high, low, "block")
    own = finish(background, edges, own, from_low, from_high, estimate)

    mine, partners = gather_parts(own)
    return assemble(index, mine + partners)


def solution(mesh):
    return jax.shard_map(
        program,
        mesh=mesh,
        in_specs=(
            P("block", None, None),
            P("view", "block", None, None, None),
            P(),
            P(),
            P(),
            P(),
            P(),
        ),
        out_specs=P("block", None, None),
        check_vma=False,
    )
```

```python
import jax
import jax.numpy as jnp
from jax import lax
from jax.experimental import pallas as pl
from jax.experimental.pallas import tpu as pltpu
from jax.sharding import PartitionSpec as P


CAP = 2
TAPS = 21
HALO = 16
VIEWS = 8
SLOTS = 16
NY = 64
PART = 32
ROWS = 256
QUADS = 16

F32 = jnp.float32
BF16 = jnp.bfloat16
I32 = jnp.int32
I16 = jnp.int16


def lane_block(shape):
    return lax.broadcasted_iota(I32, shape, len(shape) - 1) // PART


def rotate(value, amount):
    return pltpu.roll(value, amount % 128, value.ndim - 1)


def digit_swap(shape):
    row = lax.broadcasted_iota(I32, shape, 0)
    column = lax.broadcasted_iota(I32, shape, 1)
    target = ((row // PART) % 4) * 128 + (row // 128) * PART + row % PART
    return jnp.where(column == target, 1.0, 0.0).astype(BF16)


def swap_fours(first, second):
    upper = lax.broadcasted_iota(I32, first.shape, 0) < 4
    return (jnp.where(upper, first, pltpu.roll(second, 4, 0)),
            jnp.where(upper, pltpu.roll(first, 4, 0), second))


def held(shape, dtype):
    return pltpu.VMEM(shape, dtype)


def stay(*arrays):
    return tuple(pltpu.with_memory_space_constraint(array, pltpu.VMEM) for array in arrays)


def room(mebibytes):
    return pltpu.CompilerParams(vmem_limit_bytes=mebibytes << 20)


def vmem(count):
    return [pl.BlockSpec(memory_space=pltpu.VMEM)] * count


def smem(count):
    return [pl.BlockSpec(memory_space=pltpu.SMEM)] * count


def to_fixed(value, scale):
    return (value * scale + 0.5).astype(I32).astype(I16)


def from_fixed(value, step):
    return value.astype(I32).astype(F32) * step


def partial_bound(offset_ref):
    total = 0.0
    for view in range(VIEWS):
        total = total + 2.0 / jnp.full((8, 128), offset_ref[view], F32)
    return total * 1.05


def band_kernel(taps_ref, shift_ref, ky_ref, kyt_ref, kx_ref, kxt_ref, bzf_ref, bza_ref):
    radius = (TAPS - 1) // 2

    def fill(difference, view, axis):
        result = jnp.zeros(difference.shape, F32)
        for tap in range(TAPS):
            result = jnp.where(difference == tap, taps_ref[(view * 3 + axis) * TAPS + tap], result)
        return result

    def one_view(view, carry):
        shift_z = shift_ref[view * 3]
        shift_y = shift_ref[view * 3 + 1]
        shift_x = shift_ref[view * 3 + 2]
        row = lax.broadcasted_iota(I32, (16, 2 * ROWS), 0)
        lane = lax.broadcasted_iota(I32, (16, 2 * ROWS), 1)
        offset = (lane // 16 - 16) * 4 + lane % 4 - row % 4
        same = (lane // 4) % 4 == row // 4
        for strip, target_ref in ((jnp.where(same, offset - shift_y + radius, -1), ky_ref),
                                  (jnp.where(same, -offset - shift_y + radius, -1), kyt_ref)):
            values = fill(strip, view, 1)
            for quad in range(QUADS):
                target_ref[view, quad * 16:(quad + 1) * 16, :] = values[
                    :, ROWS - quad * 16:2 * ROWS - quad * 16].astype(BF16)
        row = lax.broadcasted_iota(I32, (PART, 128), 0)
        lane = lax.broadcasted_iota(I32, (PART, 128), 1)
        for half in range(2):
            base = fill(half * PART + row - (lane % PART + HALO) - shift_x + radius, view, 2)
            for block in range(4):
                first = half * 128 + block * PART
                kx_ref[view, first:first + PART, :] = jnp.where(lane // PART == block, base, 0.0).astype(BF16)
            base = fill(half * PART + lane % PART - (row + HALO) - shift_x + radius, view, 2)
            for block in range(4):
                kxt_ref[view, block * PART:(block + 1) * PART, half * 128:(half + 1) * 128] = jnp.where(
                    lane // PART == block, base, 0.0).astype(BF16)
        row = lax.broadcasted_iota(I32, (64, 192), 0)
        lane = lax.broadcasted_iota(I32, (64, 192), 1)
        difference = jnp.where(lane % 4 == row % 4, lane // 4 - 16 - row // 4 - shift_z + radius, -1)
        bzf_ref[pl.ds(pl.multiple_of(view * 64, 64), 64), :] = fill(difference, view, 0).astype(BF16)
        return carry

    lax.fori_loop(0, VIEWS, one_view, 0)
    row = lax.broadcasted_iota(I32, (192, 128), 0)
    lane = lax.broadcasted_iota(I32, (192, 128), 1)
    left = lane < 64
    for pair in range(VIEWS // 2):
        shift = jnp.where(left, shift_ref[pair * 6], shift_ref[pair * 6 + 3])
        difference = jnp.where(lane % 4 == row % 4, row // 4 - 16 - (lane // 4) % 16 - shift + radius, -1)
        total = jnp.zeros((192, 128), F32)
        for tap in range(TAPS):
            value = jnp.where(left, taps_ref[pair * 6 * TAPS + tap], taps_ref[(pair * 6 + 3) * TAPS + tap])
            total = jnp.where(difference == tap, value, total)
        bza_ref[:, pair * 128:(pair + 1) * 128] = total.astype(BF16)


def build_bands(taps, shifts):
    return pl.pallas_call(
        band_kernel,
        out_shape=(
            jax.ShapeDtypeStruct((VIEWS, ROWS, ROWS), BF16),
            jax.ShapeDtypeStruct((VIEWS, ROWS, ROWS), BF16),
            jax.ShapeDtypeStruct((VIEWS, ROWS, 128), BF16),
            jax.ShapeDtypeStruct((VIEWS, 128, ROWS), BF16),
            jax.ShapeDtypeStruct((VIEWS * 64, 192), BF16),
            jax.ShapeDtypeStruct((192, VIEWS * 64), BF16),
        ),
        in_specs=smem(2),
        out_specs=tuple(vmem(6)),
        name="bands",
    )(taps, shifts)


def pack_kernel(index_ref, target_ref, pieces_ref, first_ref, last_ref, out_ref, low_ref, high_ref, stage_ref, swap_ref,
                sent_ref):
    step = pl.program_id(0)
    count = target_ref.shape[0]

    @pl.when(step == 0)
    def _():
        swap_ref[...] = digit_swap((512, 512))

    rows = []
    for k in range(4):
        for half in range(2):
            rows.append(jnp.concatenate(
                [pieces_ref[k, q, :, half * 128:(half + 1) * 128] for q in range(4)], axis=1))
    mixed = jnp.dot(jnp.concatenate(rows, axis=0), swap_ref[...], preferred_element_type=F32).astype(BF16)
    for k in range(4):
        piece = step * 4 + k
        target = target_ref[piece]
        rank = jnp.int32(0)
        for other in range(count):
            rank = rank + jnp.where((target_ref[other] == target) & (other < piece), 1, 0)
        slot = target * CAP + rank
        for half in range(2):
            first = (k * 2 + half) * NY
            for part in range(4):
                stage_ref[piece, half * 4 + part] = mixed[first:first + NY, part * 128:(part + 1) * 128]
        pltpu.make_async_copy(stage_ref.at[piece], out_ref.at[:, slot], sent_ref.at[piece]).start()

    part = index_ref[0]
    amount = (16 - PART * part + 256) % 256
    lane = lax.broadcasted_iota(I32, (32, 128), 1)
    column = part * PART - HALO + lane % 64
    inside = (column >= 0) & (column < 256)
    for source_ref, target_ref_out in ((first_ref, low_ref), (last_ref, high_ref)):
        planes = []
        for k in range(4):
            plane = source_ref[k]
            top = pltpu.roll(plane[:32], amount, 1)[:, :128]
            bottom = pltpu.roll(plane[32:], (amount + 64) % 256, 1)[:, :128]
            planes.append(jnp.where(inside, jnp.where(lane < 64, top, bottom), 0.0))
        for m in range(4):
            rows = slice(m * 8, m * 8 + 8)
            front = swap_fours(planes[0][rows], planes[1][rows])
            back = swap_fours(planes[2][rows], planes[3][rows])
            for odd in range(2):
                target_ref_out[m * 2 + odd, pl.ds(pl.multiple_of(step * 16, 16), 16), :] = jnp.concatenate(
                    [front[odd], back[odd]], axis=0).astype(BF16)

    @pl.when(step == 3)
    def _():
        for piece in range(count):
            pltpu.make_async_copy(stage_ref.at[piece], out_ref.at[:, 0], sent_ref.at[piece]).wait()


def pack_pieces(index, targets, pieces, estimate, block_count):
    count = pieces.shape[0]
    return pl.pallas_call(
        pack_kernel,
        grid=(4,),
        out_shape=(
            jax.ShapeDtypeStruct((VIEWS, block_count * CAP, NY, 128), BF16),
            jax.ShapeDtypeStruct((8, 64, 128), BF16),
            jax.ShapeDtypeStruct((8, 64, 128), BF16),
        ),
        in_specs=smem(2) + [pl.BlockSpec((4,) + pieces.shape[1:], lambda step: (step, 0, 0, 0)),
                            pl.BlockSpec((4, NY, 256), lambda step: (step, 0, 0)),
                            pl.BlockSpec((4, NY, 256), lambda step: (12 + step, 0, 0))],
        out_specs=(pl.BlockSpec(memory_space=pl.ANY),) + tuple(vmem(2)),
        scratch_shapes=[pltpu.VMEM((count, VIEWS, NY, 128), BF16), pltpu.VMEM((512, 512), BF16),
                        pltpu.SemaphoreType.DMA((count,))],
        name="pack",
    )(index, targets, pieces, estimate, estimate)


def window_kernel(index_ref, estimate_ref, main_ref):
    part = index_ref[0]
    block = lane_block((NY, 128))
    lane = lax.broadcasted_iota(I32, (NY, 128), 1) % PART

    def two_planes(step, carry):
        for half in range(2):
            column = (part + half) * PART - HALO + lane
            inside = (column >= 0) & (column < 256)
            planes = []
            for odd in range(2):
                result = jnp.zeros((NY, 128), F32)
                for h in range(4):
                    plane = estimate_ref[h * 16 + step * 2 + odd]
                    amount = (16 - PART * part - PART * half + PART * h + 512) % 256
                    result = jnp.where(block == h, pltpu.roll(plane, amount, 1)[:, :128], result)
                planes.append(jnp.where(inside, result, 0.0))
            for m in range(8):
                low, high = swap_fours(planes[0][m * 8:m * 8 + 8], planes[1][m * 8:m * 8 + 8])
                main_ref[half, pl.ds(pl.multiple_of(m * 128 + step * 8, 8), 8), :] = low
                main_ref[half, pl.ds(pl.multiple_of(m * 128 + 64 + step * 8, 8), 8), :] = high
        return carry

    lax.fori_loop(0, 8, two_planes, 0)


def window_estimate(index, estimate):
    return pl.pallas_call(
        window_kernel,
        out_shape=jax.ShapeDtypeStruct((2, 1024, 128), F32),
        in_specs=smem(1) + vmem(1),
        out_specs=vmem(1)[0],
        name="window",
    )(index, estimate)


def build_tail(edge_ref, from_low_ref, from_high_ref, tail_ref):
    block = lane_block((64, 128))

    def two_quads(quad, carry):
        low = from_low_ref[quad].astype(F32) * edge_ref[2]
        high = from_high_ref[quad].astype(F32) * edge_ref[3]
        for member in range(2):
            base = member * 64
            result = jnp.where(block == 0, rotate(low, -base), rotate(low, 32 - base))
            result = jnp.where(block == 1, rotate(high, 32 - base), result)
            tail_ref[quad + member * 8] = jnp.where(block == 3, rotate(high, 64 - base), result)
        return carry

    lax.fori_loop(0, QUADS // 2, two_quads, 0)


def weight_kernel(rows_ref, main_ref, tail_ref, out_main_ref, out_tail_ref):
    quarter = lax.broadcasted_iota(I32, (64, 128), 0) % 4

    def one_quad(quad, carry):
        rows = pl.ds(pl.multiple_of(quad * 64, 64), 64)
        totals = [jnp.zeros((64, 128), F32) for _ in range(3)]
        for view in range(VIEWS):
            factor = jnp.full((64, 128), rows_ref[view * NY + quad * 4], F32)
            for k in range(1, 4):
                factor = jnp.where(quarter == k, rows_ref[view * NY + quad * 4 + k], factor)
            totals[0] = totals[0] + factor * main_ref[view, 0]
            totals[1] = totals[1] + factor * main_ref[view, 1]
            totals[2] = totals[2] + factor * tail_ref[view]
        out_main_ref[0, rows, :] = 1.0 / jnp.maximum(totals[0], 1.0)
        out_main_ref[1, rows, :] = 1.0 / jnp.maximum(totals[1], 1.0)
        out_tail_ref[quad] = 1.0 / jnp.maximum(totals[2], 1.0)
        return carry

    lax.fori_loop(0, QUADS, one_quad, 0)


def build_weights(rows, main, tail):
    return pl.pallas_call(
        weight_kernel,
        out_shape=(
            jax.ShapeDtypeStruct((2, 1024, 128), F32),
            jax.ShapeDtypeStruct((QUADS, 64, 128), F32),
        ),
        in_specs=smem(1) + vmem(2),
        out_specs=tuple(vmem(2)),
        name="weights",
    )(rows, main, tail)


def forward_depth(main_ref, tail_ref, bzf_ref, planes_ref):
    block = lane_block((64, 128))

    def stacked(quad):
        rows = pl.ds(pl.multiple_of(quad * 64, 64), 64)
        left = main_ref[0, rows, :]
        right = main_ref[1, rows, :]
        tail = tail_ref[quad]
        turned = rotate(tail, 64)
        lower = jnp.concatenate([jnp.where(block == 0, tail, rotate(left, 32)),
                                 jnp.where(block == 0, turned, rotate(right, 32))], axis=1)
        upper = jnp.concatenate([jnp.where(block == 3, turned, rotate(left, 96)),
                                 jnp.where(block == 3, tail, rotate(right, 96))], axis=1)
        return jnp.concatenate([lower, jnp.concatenate([left, right], axis=1), upper], axis=0).astype(BF16)

    def two_quads(step, carry):
        both = jnp.concatenate([stacked(step * 2), stacked(step * 2 + 1)], axis=1)
        blurred = jnp.dot(bzf_ref[...], both, preferred_element_type=F32).astype(BF16)
        for member in range(2):
            first = pl.multiple_of(step * 32 + member * 16, 16)
            for group in range(VIEWS * 4):
                planes_ref[group, pl.ds(first, 16), :] = blurred[
                    group * 16:(group + 1) * 16, member * ROWS:(member + 1) * ROWS]
        return carry

    lax.fori_loop(0, QUADS // 2, two_quads, 0, unroll=2)


def forward_plane(view, planes_ref, ky, kx):
    volume = planes_ref[pl.ds(view * 4, 4)].reshape(4 * ROWS, ROWS)
    along_x = jnp.concatenate([jnp.dot(volume[r * 512:(r + 1) * 512], kx, preferred_element_type=F32)
                               for r in range(2)], axis=0).astype(BF16)
    side = jnp.concatenate([along_x[r * ROWS:(r + 1) * ROWS] for r in range(4)], axis=1)
    return jnp.dot(ky, side, preferred_element_type=F32)


def adjoint_plane(view, quotient, kyt, kxt, depth_ref):
    along_y = jnp.dot(kyt, quotient.astype(BF16), preferred_element_type=F32).astype(BF16)
    stacked = jnp.concatenate([along_y[:, r * 128:(r + 1) * 128] for r in range(4)], axis=0)
    along_x = jnp.concatenate([jnp.dot(stacked[r * 512:(r + 1) * 512], kxt, preferred_element_type=F32)
                               for r in range(2)], axis=0).astype(BF16)
    for r in range(4):
        first = pl.multiple_of(view * 64 + r * 16, 16)
        for quad in range(QUADS):
            depth_ref[quad, pl.ds(first, 16), :] = along_x[r * ROWS + quad * 16:r * ROWS + quad * 16 + 16]


def own_lanes(left, right):
    lane = lax.broadcasted_iota(I32, left.shape, 1) % PART
    return jnp.where(lane < HALO, rotate(left, 112), rotate(right, 16))


def adjoint_depth(scale, bza_ref, depth_ref, main_ref, tail_ref, to_left_ref, to_right_ref, last=False):
    block = lane_block((64, 128))
    low_half = block < 2
    near = lax.broadcasted_iota(I32, (64, 128), 1) % PART < HALO

    def pair(quad, carry):
        tails = []
        members = (quad, quad + QUADS // 2)
        both = jnp.concatenate([depth_ref[member] for member in members], axis=1)
        summed_both = jnp.dot(bza_ref[...], both, preferred_element_type=F32)
        for index, member in enumerate(members):
            summed = summed_both[:, index * ROWS:(index + 1) * ROWS]
            mains = []
            for half in range(2):
                lanes = slice(half * 128, (half + 1) * 128)
                lower = jnp.where(block < 3, rotate(summed[:64, lanes], 96), 0.0)
                upper = jnp.where(block > 0, rotate(summed[128:, lanes], 32), 0.0)
                mains.append(summed[64:128, lanes] + lower + upper)
            tail = jnp.where(block == 0, summed[:64, :128], summed[128:, 128:])
            tail = jnp.where(block == 1, rotate(summed[128:, :128], 64), tail)
            tail = jnp.where(block == 2, rotate(summed[:64, 128:], 64), tail)
            if last:
                main_ref[member] = own_lanes(*mains)
                tail_ref[member] = jnp.where(near, rotate(tail, 112), rotate(tail, 80))
                to_left_ref[member] = to_fixed(jnp.where(near, mains[0], rotate(tail, 16)), scale)
                to_right_ref[member] = to_fixed(jnp.where(near, rotate(tail, 48), mains[1]), scale)
                continue
            rows = pl.ds(pl.multiple_of(member * 64, 64), 64)
            main_ref[0, rows, :] = mains[0]
            main_ref[1, rows, :] = mains[1]
            tail_ref[member] = tail
            to_left_ref[member] = to_fixed(mains[0], scale)
            to_right_ref[member] = to_fixed(mains[1], scale)
            tails.append(tail)
        if last:
            return carry
        to_left_ref[QUADS + quad] = to_fixed(jnp.where(low_half, tails[0], rotate(tails[1], 64)), scale)
        to_right_ref[QUADS + quad] = to_fixed(jnp.where(low_half, rotate(tails[0], 64), tails[1]), scale)
        return carry

    lax.fori_loop(0, QUADS // 2, pair, 0, unroll=2)


def tall(value):
    return jnp.concatenate([value] * 8, axis=0)


def forward_kernel(edge_ref, main_ref, from_low_ref, from_high_ref, bzf_ref, ky_ref, kx_ref, out_ref, tail_ref,
                   planes_ref):
    build_tail(edge_ref, from_low_ref, from_high_ref, tail_ref)
    forward_depth(main_ref, tail_ref, bzf_ref, planes_ref)

    def one_view(view, carry):
        out_ref[view] = forward_plane(view, planes_ref, ky_ref[view], kx_ref[view]).astype(BF16)
        return carry

    lax.fori_loop(0, VIEWS, one_view, 0)


def forward(edges, main, from_low, from_high, bzf, ky, kx):
    return pl.pallas_call(
        forward_kernel,
        out_shape=(
            jax.ShapeDtypeStruct((VIEWS, ROWS, 2 * ROWS), BF16),
            jax.ShapeDtypeStruct((QUADS, 64, 128), F32),
        ),
        in_specs=smem(1) + vmem(6),
        out_specs=tuple(vmem(2)),
        scratch_shapes=[pltpu.VMEM((VIEWS * 4, ROWS, ROWS), BF16)],
        name="forward",
    )(edges, main, from_low, from_high, bzf, ky, kx)


def per_view(*shape):
    return pl.BlockSpec((2,) + shape, lambda step: (step,) + (0,) * len(shape))


PARTIAL_SHAPES = (
    held((2, 1024, 128), F32),
    held((QUADS, 64, 128), F32),
    held((QUADS + QUADS // 2, 64, 128), I16),
    held((QUADS + QUADS // 2, 64, 128), I16),
)


def first_adjoint_kernel(start_ref, source_ref, place_ref, inverse_ref, offset_ref, incoming_ref, blurred_ref, kyt_ref,
                         kxt_ref, bza_ref, main_ref, tail_ref, to_left_ref, to_right_ref, average_ref, total_ref,
                         depth_ref, swap_ref):
    step = pl.program_id(0)

    @pl.when(step == 0)
    def _():
        swap_ref[...] = digit_swap((512, 512))

    for slot in range(2 * SLOTS):
        total_ref[slot] = jnp.zeros((NY, 128), F32)

    def add(entry, carry):
        place = place_ref[entry]
        piece = incoming_ref[source_ref[entry] - step * incoming_ref.shape[0]].astype(F32)
        slot = place - step * (2 * SLOTS)
        total_ref[slot] = total_ref[slot] + piece * inverse_ref[place]
        return carry

    lax.fori_loop(start_ref[step * 2], start_ref[step * 2 + 2], add, 0)
    rows = []
    for r in range(8):
        rows.append(jnp.concatenate(
            [total_ref[r // 4 * SLOTS + h * 4 + r % 4].astype(BF16) for h in range(4)], axis=1))
    mixed = jnp.dot(jnp.concatenate(rows, axis=0), swap_ref[...], preferred_element_type=F32)
    for r in range(8):
        lanes = slice(r % 4 * 128, r % 4 * 128 + 128)
        for m in range(8):
            first = r * NY + m * 8
            ends = []
            for q in (0, 2):
                ends.append(swap_fours(mixed[first:first + 8, q * 128:(q + 1) * 128],
                                       mixed[first:first + 8, (q + 1) * 128:(q + 2) * 128]))
            for odd in range(2):
                quad = 2 * m + odd
                average_ref[r // 4, quad * 16:quad * 16 + 16, lanes] = jnp.concatenate(
                    [ends[0][odd], ends[1][odd]], axis=0).astype(BF16)
    quotients = [average_ref[k].astype(F32) / (blurred_ref[k].astype(F32) + offset_ref[step * 2 + k]) for k in range(2)]
    for k in range(2):
        adjoint_plane(step * 2 + k, quotients[k], kyt_ref[k], kxt_ref[k], depth_ref)

    @pl.when(step == VIEWS // 2 - 1)
    def _():
        scale = tall(32767.0 / partial_bound(offset_ref))
        adjoint_depth(scale, bza_ref, depth_ref, main_ref, tail_ref, to_left_ref, to_right_ref)


def first_adjoint(start, source, place, inverse, offset, incoming, blurred, kyt, kxt, bza):
    share = incoming.shape[0] // (VIEWS // 2)
    return pl.pallas_call(
        first_adjoint_kernel,
        grid=(VIEWS // 2,),
        out_shape=PARTIAL_SHAPES + (jax.ShapeDtypeStruct((VIEWS, ROWS, 2 * ROWS), BF16),),
        in_specs=smem(5) + [pl.BlockSpec((share, NY, 128), lambda view: (view, 0, 0)), per_view(ROWS, 2 * ROWS),
                            per_view(ROWS, ROWS), per_view(128, ROWS)] + vmem(1),
        out_specs=tuple(vmem(4)) + (per_view(ROWS, 2 * ROWS),),
        scratch_shapes=[pltpu.VMEM((2 * SLOTS, NY, 128), F32), pltpu.VMEM((QUADS, VIEWS * 64, ROWS), BF16),
                        pltpu.VMEM((512, 512), BF16)],
        name="first_adjoint",
        compiler_params=room(60),
    )(start, source, place, inverse, offset, incoming, blurred, kyt, kxt, bza)


def join_columns_kernel(offset_ref, edge_ref, main_ref, tail_ref, from_left_ref, from_right_ref, out_main_ref, out_tail_ref,
                        low_ref, high_ref):
    block = lane_block((64, 128))
    low_half = block < 2
    bound = partial_bound(offset_ref)
    scale = tall(32767.0 / bound)
    left_step = tall(bound * (edge_ref[0] / 32767.0))
    right_step = tall(bound * (edge_ref[1] / 32767.0))

    def pair(quad, carry):
        packed_left = from_fixed(from_left_ref[QUADS + quad], left_step)
        packed_right = from_fixed(from_right_ref[QUADS + quad], right_step)
        for second, member in enumerate((quad, quad + QUADS // 2)):
            rows = pl.ds(pl.multiple_of(member * 64, 64), 64)
            left = main_ref[0, rows, :] + from_fixed(from_left_ref[member], left_step)
            right = main_ref[1, rows, :] + from_fixed(from_right_ref[member], right_step)
            if second:
                extra = jnp.where(low_half, rotate(packed_left, 64), packed_right)
            else:
                extra = jnp.where(low_half, packed_left, rotate(packed_right, 64))
            tail = tail_ref[member] + extra
            out_main_ref[0, rows, :] = left
            out_main_ref[1, rows, :] = right
            out_tail_ref[member] = tail
            low = jnp.where(block == 1, rotate(left, 32), tail)
            low = jnp.where(block == 3, rotate(right, 96), low)
            high = jnp.where(block == 0, rotate(left, 32), tail)
            high = jnp.where(block == 2, rotate(right, 96), high)
            low_ref[member] = to_fixed(low, scale)
            high_ref[member] = to_fixed(high, scale)
        return carry

    lax.fori_loop(0, QUADS // 2, pair, 0)


def join_columns(offset, edges, main, tail, from_left, from_right):
    return pl.pallas_call(
        join_columns_kernel,
        out_shape=(
            held((2, 1024, 128), F32),
            held((QUADS, 64, 128), F32),
            held((QUADS, 64, 128), I16),
            held((QUADS, 64, 128), I16),
        ),
        in_specs=smem(2) + vmem(4),
        out_specs=tuple(vmem(4)),
        name="join_columns",
        compiler_params=room(48),
    )(offset, edges, *stay(main, tail, from_left, from_right))


def joined_planes(quad, steps, block, main_ref, tail_ref, from_low_ref, from_high_ref):
    rows = pl.ds(pl.multiple_of(quad * 64, 64), 64)
    low = from_fixed(from_low_ref[quad], steps[0])
    high = from_fixed(from_high_ref[quad], steps[1])
    left = main_ref[0, rows, :]
    left = left + jnp.where(block == 0, rotate(low, 96), 0.0) + jnp.where(block == 3, rotate(high, 96), 0.0)
    right = main_ref[1, rows, :]
    right = right + jnp.where(block == 0, rotate(low, 32), 0.0) + jnp.where(block == 3, rotate(high, 32), 0.0)
    tail = tail_ref[quad] + jnp.where(block % 2 == 0, low, high)
    return rows, left, right, tail


def depth_steps(bound, edge_ref):
    return tall(bound * (edge_ref[2] / 32767.0)), tall(bound * (edge_ref[3] / 32767.0))


def second_kernel(offset_ref, edge_ref, part_main_ref, part_tail_ref, from_low_ref, from_high_ref, estimate_main_ref,
                  estimate_tail_ref, scale_main_ref, scale_tail_ref, bzf_ref, bza_ref, average_ref, ky_ref, kx_ref,
                  kyt_ref, kxt_ref, own_estimate_ref, own_ref, own_tail_ref, to_left_ref, to_right_ref, new_main_ref,
                  tail_estimate_ref, planes_ref, depth_ref):
    step = pl.program_id(0)

    @pl.when(step == 0)
    def _():
        block = lane_block((64, 128))
        steps = depth_steps(partial_bound(offset_ref), edge_ref)

        def renew(quad, carry):
            rows, left, right, tail = joined_planes(
                quad, steps, block, part_main_ref, part_tail_ref, from_low_ref, from_high_ref)
            left = estimate_main_ref[0, rows, :] * left * scale_main_ref[0, rows, :]
            right = estimate_main_ref[1, rows, :] * right * scale_main_ref[1, rows, :]
            new_main_ref[0, rows, :] = left
            new_main_ref[1, rows, :] = right
            own_estimate_ref[quad] = own_lanes(left * scale_main_ref[0, rows, :], right * scale_main_ref[1, rows, :])
            tail_estimate_ref[quad] = estimate_tail_ref[quad] * tail * scale_tail_ref[quad]
            return carry

        lax.fori_loop(0, QUADS, renew, 0)
        forward_depth(new_main_ref, tail_estimate_ref, bzf_ref, planes_ref)

    views = [step * 2, step * 2 + 1]
    blurred = [forward_plane(views[k], planes_ref, ky_ref[k], kx_ref[k]) + offset_ref[views[k]] for k in range(2)]
    quotients = [average_ref[k].astype(F32) / blurred[k] for k in range(2)]
    for k in range(2):
        adjoint_plane(views[k], quotients[k], kyt_ref[k], kxt_ref[k], depth_ref)

    @pl.when(step == VIEWS // 2 - 1)
    def _():
        scale = tall(32767.0 / partial_bound(offset_ref))
        adjoint_depth(scale, bza_ref, depth_ref, own_ref, own_tail_ref, to_left_ref, to_right_ref, last=True)


def second(offset, edges, *operands):
    return pl.pallas_call(
        second_kernel,
        grid=(VIEWS // 2,),
        out_shape=(held((QUADS, 64, 128), F32),) * 3 + (held((QUADS, 64, 128), I16),) * 2,
        in_specs=smem(2) + vmem(10) + [per_view(ROWS, 2 * ROWS), per_view(ROWS, ROWS), per_view(ROWS, 128),
                                       per_view(ROWS, ROWS), per_view(128, ROWS)],
        out_specs=tuple(vmem(5)),
        scratch_shapes=[pltpu.VMEM((2, 1024, 128), F32), pltpu.VMEM((QUADS, 64, 128), F32),
                        pltpu.VMEM((VIEWS * 4, ROWS, ROWS), BF16), pltpu.VMEM((QUADS, VIEWS * 64, ROWS), BF16)],
        name="second",
        compiler_params=room(52),
    )(offset, edges, *stay(*operands[:4]), *operands[4:])


def join_own_kernel(offset_ref, edge_ref, own_ref, tail_ref, from_left_ref, from_right_ref, out_ref, low_ref, high_ref):
    block = lane_block((64, 128))
    near = lax.broadcasted_iota(I32, (64, 128), 1) % PART < HALO
    bound = partial_bound(offset_ref)
    scale = tall(32767.0 / bound)
    left_step = tall(bound * (edge_ref[0] / 32767.0))
    right_step = tall(bound * (edge_ref[1] / 32767.0))

    def four_quads(quad, carry):
        low = jnp.zeros((64, 128), F32)
        high = jnp.zeros((64, 128), F32)
        for k in range(4):
            member = quad + k * 4
            left = from_fixed(from_left_ref[member], left_step)
            right = from_fixed(from_right_ref[member], right_step)
            out_ref[member] = own_ref[member] + own_lanes(left, right)
            tail = tail_ref[member] + jnp.where(near, left, right)
            low = jnp.where(block == k, rotate(tail, PART * k), low)
            high = jnp.where(block == k, rotate(tail, PART * k - PART), high)
        low_ref[quad] = to_fixed(low, scale)
        high_ref[quad] = to_fixed(high, scale)
        return carry

    lax.fori_loop(0, QUADS // 4, four_quads, 0)


def join_own(offset, edges, own, tail, from_left, from_right):
    return pl.pallas_call(
        join_own_kernel,
        out_shape=(held((QUADS, 64, 128), F32), held((QUADS // 4, 64, 128), I16), held((QUADS // 4, 64, 128), I16)),
        in_specs=smem(2) + vmem(4),
        out_specs=tuple(vmem(3)),
        name="join_own",
        compiler_params=room(48),
    )(offset, edges, *stay(own, tail, from_left, from_right))


def finish_kernel(offset_ref, edge_ref, own_ref, from_low_ref, from_high_ref, estimate_ref, out_ref, value_ref):
    block = lane_block((64, 128))
    steps = depth_steps(partial_bound(offset_ref), edge_ref)

    def four_quads(quad, largest):
        low = from_fixed(from_low_ref[quad], steps[0])
        high = from_fixed(from_high_ref[quad], steps[1])
        for k in range(4):
            member = quad + k * 4
            summed = own_ref[member] + jnp.where(block == 0, rotate(low, -PART * k), 0.0)
            summed = summed + jnp.where(block == 3, rotate(high, 96 - PART * k), 0.0)
            value = estimate_ref[member] * summed
            value_ref[member] = value
            largest = jnp.maximum(largest, value)
        return largest

    largest = lax.fori_loop(0, QUADS // 4, four_quads, jnp.zeros((64, 128), F32))
    unit = (jnp.max(largest) * 64.0).astype(I32) + 1
    vector = jnp.full((16, 128), unit, I32)
    out_ref[1024:1040, :] = (vector >> 15).astype(I16)
    out_ref[1040:1056, :] = (vector & 32767).astype(I16)
    factor = (32767.0 * 64.0) / vector.astype(F32)

    def sixteen_rows(n, carry):
        for j in range(0, 16, 2):
            rows = slice(j * 4, j * 4 + 8)
            ends = [swap_fours(value_ref[n * 4 + 2 * m, rows, :], value_ref[n * 4 + 2 * m + 1, rows, :])
                    for m in range(2)]
            for odd in range(2):
                first = pl.multiple_of((j + odd) * NY + n * 16, 16)
                out_ref[pl.ds(first, 16), :] = to_fixed(
                    jnp.concatenate([ends[0][odd], ends[1][odd]], axis=0), factor)
        return carry

    lax.fori_loop(0, 4, sixteen_rows, 0)


def finish(offset, edges, own, from_low, from_high, estimate):
    return pl.pallas_call(
        finish_kernel,
        out_shape=held((1056, 128), I16),
        in_specs=smem(2) + vmem(4),
        out_specs=vmem(1)[0],
        scratch_shapes=[pltpu.VMEM((QUADS, 64, 128), F32)],
        name="finish",
        compiler_params=room(52),
    )(offset, edges, *stay(own, from_low, from_high, estimate))


def assemble_kernel(index_ref, *refs):
    chunk_refs, out_ref, buffer_ref = refs[:8], refs[8], refs[9]
    part = index_ref[0]

    @pl.when(pl.program_id(0) == 0)
    def _():
        for place in range(8):
            owner = ((part // 2 + place % 4) % 4) * 2 + (part % 2 if place < 4 else 1 - part % 2)
            buffer_ref[owner] = chunk_refs[place][...]

    block = lane_block((16, 128))
    even = block % 2 == 0
    units = []
    for half in range(2):
        unit = jnp.zeros((16, 128), F32)
        for k in range(4):
            digits = (buffer_ref[half * 4 + k, 1024:1040, :].astype(I32) * 32768
                      + buffer_ref[half * 4 + k, 1040:1056, :].astype(I32))
            unit = jnp.where(block == k, digits.astype(F32) * (1.0 / (64.0 * 32767.0)), unit)
        units.append(unit)
    step = pl.program_id(0)

    def sixteen_rows(n, carry):
        lines = pl.ds(pl.multiple_of(n * 16, 16), 16)
        for j in (0, 2):
            first = pl.multiple_of((step * 4 + j) * NY + n * 16, 16)
            for half in range(2):
                c0, c1, c2, c3 = (
                    buffer_ref[half * 4 + k, pl.ds(first, 16), :].astype(I32)
                    | (buffer_ref[half * 4 + k, pl.ds(first + NY, 16), :].astype(I32) << 16) for k in range(4))
                a0 = jnp.where(block < 2, c0, rotate(c2, 64))
                a1 = jnp.where(block < 2, c1, rotate(c3, 64))
                a2 = jnp.where(block < 2, rotate(c0, 64), c2)
                a3 = jnp.where(block < 2, rotate(c1, 64), c3)
                results = (jnp.where(even, a0, rotate(a1, 32)), jnp.where(even, rotate(a0, 96), a1),
                           jnp.where(even, a2, rotate(a3, 32)), jnp.where(even, rotate(a2, 96), a3))
                lanes = slice(half * 128, (half + 1) * 128)
                for h in range(4):
                    out_ref[h, 0, j, lines, lanes] = (results[h] & 65535).astype(F32) * units[half]
                    out_ref[h, 0, j + 1, lines, lanes] = (results[h] >> 16).astype(F32) * units[half]
        return carry

    lax.fori_loop(0, 4, sixteen_rows, 0)


def assemble(index, chunks):
    return pl.pallas_call(
        assemble_kernel,
        grid=(4,),
        out_shape=jax.ShapeDtypeStruct((4, 4, 4, NY, 256), F32),
        in_specs=smem(1) + vmem(8),
        out_specs=pl.BlockSpec((4, 1, 4, NY, 256), lambda step: (0, step, 0, 0, 0)),
        scratch_shapes=[pltpu.VMEM((VIEWS, 1056, 128), I16)],
        name="assemble",
        compiler_params=room(58),
    )(index, *stay(*chunks)).reshape(64, NY, 256)


def to_neighbours(upward, downward, axis):
    count = lax.axis_size(axis)
    from_low = lax.ppermute(upward, axis, [(i, (i + 1) % count) for i in range(count)])
    from_high = lax.ppermute(downward, axis, [((i + 1) % count, i) for i in range(count)])
    return from_low, from_high


def gather_parts(own):
    parts = [own] + [
        lax.ppermute(own, "view", [((i + 2 * step) % VIEWS, i) for i in range(VIEWS)]) for step in (1, 3, 2)
    ]
    parts = [parts[0], parts[1], parts[3], parts[2]]
    return parts, [lax.ppermute(part, "view", [(i, i ^ 1) for i in range(VIEWS)]) for part in parts]


def column_sums(kernel, shift, positions, length):
    radius = (TAPS - 1) // 2
    source = (positions[None, :, None] - shift[:, None, None]
              - jnp.arange(TAPS, dtype=I32)[None, None, :] + radius)
    inside = (source >= 0) & (source < length)
    return jnp.sum(jnp.where(inside, kernel[:, None, :], 0.0), axis=2)


def program(estimate0, pieces, dest_block, slot_index, psf_shift, psf_taps, background):
    block_count = lax.axis_size("block")
    my_view = lax.axis_index("view")
    my_block = lax.axis_index("block")
    edges = jnp.stack([my_view > 0, my_view < VIEWS - 1, my_block > 0, my_block < block_count - 1]).astype(F32)
    targets = dest_block[:, :, 0].reshape(VIEWS, block_count, SLOTS)
    slots = slot_index.reshape(VIEWS, block_count, SLOTS)

    index = my_view.reshape(1).astype(I32)
    own_targets = lax.dynamic_slice(targets, (my_view, my_block, 0), (1, 1, SLOTS)).reshape(SLOTS)
    outgoing, low, high = pack_pieces(index, own_targets, pieces[0], estimate0, block_count)
    from_low, from_high = to_neighbours(high, low, "block")
    incoming = lax.all_to_all(outgoing.reshape(VIEWS * block_count, CAP, NY, 128), ("view", "block"), 0, 0, tiled=True)
    incoming = incoming.reshape(VIEWS * block_count * CAP, NY, 128)

    main = window_estimate(index, estimate0)
    kernel = psf_taps / jnp.sum(psf_taps, axis=2, keepdims=True)
    ky, kyt, kx, kxt, bzf, bza = build_bands(kernel.reshape(-1), psf_shift.reshape(-1))
    blurred, tail = forward(edges, main, from_low, from_high, bzf, ky, kx)

    earlier = jnp.tril(jnp.ones((SLOTS, SLOTS), jnp.bool_), -1)
    same = (targets[:, :, :, None] == targets[:, :, None, :]) & earlier[None, None]
    ranks = jnp.sum(same.astype(I32), axis=3)
    mine = targets == my_block
    received = jnp.arange(CAP, dtype=I32)
    slot_of = jnp.sum(
        jnp.where(mine[..., None] & (ranks[..., None] == received), slots[..., None] + 1, 0), axis=2
    ).reshape(VIEWS, block_count * CAP) - 1
    hits = slot_of[:, :, None] == jnp.arange(SLOTS, dtype=I32)
    counts = jnp.sum(hits.astype(I32), axis=1)
    inverse = 1.0 / jnp.maximum(counts, 1).astype(F32)
    entries = VIEWS * block_count * CAP
    number = jnp.arange(entries, dtype=I32)
    place_of = jnp.where(slot_of >= 0, slot_of + jnp.arange(VIEWS, dtype=I32)[:, None] * SLOTS, -1).reshape(entries)
    before = (place_of[None, :] >= 0) & (number[None, :] < number[:, None])
    position = jnp.where(place_of >= 0, jnp.sum(before.astype(I32), axis=1), -1)
    chosen = position[:, None] == number[None, :]
    source = jnp.sum(jnp.where(chosen, number[:, None], 0), axis=0)
    place = jnp.sum(jnp.where(chosen, place_of[:, None], 0), axis=0)
    start = jnp.sum(((place_of >= 0)[:, None]
                     & (number[:, None] // (block_count * CAP) < jnp.arange(VIEWS + 1))).astype(I32), axis=0)

    global_slot = (targets * SLOTS + slots).reshape(VIEWS, block_count * SLOTS)
    all_slots = jnp.arange(block_count * SLOTS, dtype=I32)
    occupied = jnp.any(global_slot[:, :, None] == all_slots, axis=1)
    mask = jnp.repeat(occupied.astype(F32), 4, axis=1)
    padded = jnp.pad(mask, ((0, 0), (2 * HALO, 2 * HALO)))
    window = lax.dynamic_slice_in_dim(padded, my_block * 64, 128, 1)
    depth = lax.broadcasted_iota(I32, (96, 128), 0) + HALO - lax.broadcasted_iota(I32, (96, 128), 1)
    tap = depth[None] - psf_shift[:, 0, None, None] + (TAPS - 1) // 2
    weight_depth = jnp.zeros((VIEWS, 96), F32)
    band = jnp.zeros((VIEWS, 96, 128), F32)
    for j in range(TAPS):
        band = jnp.where(tap == j, kernel[:, 0, j, None, None], band)
    weight_depth = jnp.sum(band * window[:, None, :], axis=2)
    weight_rows = column_sums(kernel[:, 1], psf_shift[:, 1], jnp.arange(NY, dtype=I32), NY)
    columns = my_view * PART - HALO + jnp.arange(2 * PART, dtype=I32)
    weight_columns = column_sums(kernel[:, 2], psf_shift[:, 2], columns, 256).reshape(VIEWS, 2, PART)
    by_group = weight_depth.reshape(VIEWS, 6, 16)
    planes = by_group[:, :, :, None, None] * weight_columns[:, None, None, :, :]
    planes = planes.transpose(0, 3, 2, 1, 4)
    weight_main = planes[:, :, :, 1:5].reshape(VIEWS, 2, 16, 128)
    weight_tail = jnp.stack([planes[:, :, :, 0], planes[:, :, :, 5]], axis=3)
    weight_tail = weight_tail.transpose(0, 2, 1, 3, 4).reshape(VIEWS, 16, 128)
    scale_main, scale_tail = build_weights(
        weight_rows.reshape(-1), jnp.repeat(weight_main, 4, axis=2), jnp.repeat(weight_tail, 4, axis=1))

    incoming, scale_main, scale_tail = lax.optimization_barrier((incoming, scale_main, scale_tail))
    part_main, part_tail, to_left, to_right, average = first_adjoint(
        start, source, place, inverse.reshape(-1), background, incoming, blurred, kyt, kxt, bza)
    from_left, from_right = to_neighbours(to_right, to_left, "view")
    part_main, part_tail, low, high = join_columns(background, edges, part_main, part_tail, from_left, from_right)
    from_low, from_high = to_neighbours(high, low, "block")

    estimate, own, own_tail, to_left, to_right = second(
        background, edges, part_main, part_tail, from_low, from_high, main, tail, scale_main, scale_tail,
        bzf, bza, average, ky, kx, kyt, kxt)
    from_left, from_right = to_neighbours(to_right, to_left, "view")
    own, low, high = join_own(background, edges, own, own_tail, from_left, from_right)
    from_low, from_high = to_neighbours(high, low, "block")
    own = finish(background, edges, own, from_low, from_high, estimate)

    mine, partners = gather_parts(own)
    return assemble(index, mine + partners)


def solution(mesh):
    return jax.shard_map(
        program,
        mesh=mesh,
        in_specs=(
            P("block", None, None),
            P("view", "block", None, None, None),
            P(),
            P(),
            P(),
            P(),
            P(),
        ),
        out_specs=P("block", None, None),
        check_vma=False,
    )
```

```python
import jax
import jax.numpy as jnp
from jax import lax
from jax.experimental import pallas as pl
from jax.experimental.pallas import tpu as pltpu
from jax.sharding import PartitionSpec as P


CAP = 2
TAPS = 21
HALO = 16
VIEWS = 8
SLOTS = 16
NY = 64
PART = 32
ROWS = 256
QUADS = 16

F32 = jnp.float32
BF16 = jnp.bfloat16
I32 = jnp.int32
I16 = jnp.int16


def lane_block(shape):
    return lax.broadcasted_iota(I32, shape, len(shape) - 1) // PART


def rotate(value, amount):
    return pltpu.roll(value, amount % 128, value.ndim - 1)


def digit_swap(shape):
    row = lax.broadcasted_iota(I32, shape, 0)
    column = lax.broadcasted_iota(I32, shape, 1)
    target = ((row // PART) % 4) * 128 + (row // 128) * PART + row % PART
    return jnp.where(column == target, 1.0, 0.0).astype(BF16)


def swap_fours(first, second):
    upper = lax.broadcasted_iota(I32, first.shape, 0) < 4
    return (jnp.where(upper, first, pltpu.roll(second, 4, 0)),
            jnp.where(upper, pltpu.roll(first, 4, 0), second))


def held(shape, dtype):
    return pltpu.VMEM(shape, dtype)


def stay(*arrays):
    return tuple(pltpu.with_memory_space_constraint(array, pltpu.VMEM) for array in arrays)


def room(mebibytes):
    return pltpu.CompilerParams(vmem_limit_bytes=mebibytes << 20)


def vmem(count):
    return [pl.BlockSpec(memory_space=pltpu.VMEM)] * count


def smem(count):
    return [pl.BlockSpec(memory_space=pltpu.SMEM)] * count


def to_fixed(value, scale):
    return (value * scale + 0.5).astype(I32).astype(I16)


def from_fixed(value, step):
    return value.astype(I32).astype(F32) * step


def partial_bound(offset_ref):
    total = 0.0
    for view in range(VIEWS):
        total = total + 2.0 / jnp.full((8, 128), offset_ref[view], F32)
    return total * 1.05


def band_kernel(taps_ref, shift_ref, ky_ref, kyt_ref, kx_ref, kxt_ref, bzf_ref, bza_ref, swap_ref):
    swap_ref[...] = digit_swap((512, 512))
    radius = (TAPS - 1) // 2

    def fill(difference, view, axis):
        result = jnp.zeros(difference.shape, F32)
        for tap in range(TAPS):
            result = jnp.where(difference == tap, taps_ref[(view * 3 + axis) * TAPS + tap], result)
        return result

    def one_view(view, carry):
        shift_z = shift_ref[view * 3]
        shift_y = shift_ref[view * 3 + 1]
        shift_x = shift_ref[view * 3 + 2]
        row = lax.broadcasted_iota(I32, (16, 2 * ROWS), 0)
        lane = lax.broadcasted_iota(I32, (16, 2 * ROWS), 1)
        offset = (lane // 16 - 16) * 4 + lane % 4 - row % 4
        same = (lane // 4) % 4 == row // 4
        for strip, target_ref in ((jnp.where(same, offset - shift_y + radius, -1), ky_ref),
                                  (jnp.where(same, -offset - shift_y + radius, -1), kyt_ref)):
            values = fill(strip, view, 1)
            for quad in range(QUADS):
                target_ref[view, quad * 16:(quad + 1) * 16, :] = values[
                    :, ROWS - quad * 16:2 * ROWS - quad * 16].astype(BF16)
        row = lax.broadcasted_iota(I32, (PART, 128), 0)
        lane = lax.broadcasted_iota(I32, (PART, 128), 1)
        for half in range(2):
            base = fill(half * PART + row - (lane % PART + HALO) - shift_x + radius, view, 2)
            for block in range(4):
                first = half * 128 + block * PART
                kx_ref[view, first:first + PART, :] = jnp.where(lane // PART == block, base, 0.0).astype(BF16)
            base = fill(half * PART + lane % PART - (row + HALO) - shift_x + radius, view, 2)
            for block in range(4):
                kxt_ref[view, block * PART:(block + 1) * PART, half * 128:(half + 1) * 128] = jnp.where(
                    lane // PART == block, base, 0.0).astype(BF16)
        row = lax.broadcasted_iota(I32, (64, 192), 0)
        lane = lax.broadcasted_iota(I32, (64, 192), 1)
        difference = jnp.where(lane % 4 == row % 4, lane // 4 - 16 - row // 4 - shift_z + radius, -1)
        bzf_ref[pl.ds(pl.multiple_of(view * 64, 64), 64), :] = fill(difference, view, 0).astype(BF16)
        return carry

    lax.fori_loop(0, VIEWS, one_view, 0)
    row = lax.broadcasted_iota(I32, (192, 128), 0)
    lane = lax.broadcasted_iota(I32, (192, 128), 1)
    left = lane < 64
    for pair in range(VIEWS // 2):
        shift = jnp.where(left, shift_ref[pair * 6], shift_ref[pair * 6 + 3])
        difference = jnp.where(lane % 4 == row % 4, row // 4 - 16 - (lane // 4) % 16 - shift + radius, -1)
        total = jnp.zeros((192, 128), F32)
        for tap in range(TAPS):
            value = jnp.where(left, taps_ref[pair * 6 * TAPS + tap], taps_ref[(pair * 6 + 3) * TAPS + tap])
            total = jnp.where(difference == tap, value, total)
        bza_ref[:, pair * 128:(pair + 1) * 128] = total.astype(BF16)


def build_bands(taps, shifts):
    return pl.pallas_call(
        band_kernel,
        out_shape=(
            jax.ShapeDtypeStruct((VIEWS, ROWS, ROWS), BF16),
            jax.ShapeDtypeStruct((VIEWS, ROWS, ROWS), BF16),
            jax.ShapeDtypeStruct((VIEWS, ROWS, 128), BF16),
            jax.ShapeDtypeStruct((VIEWS, 128, ROWS), BF16),
            jax.ShapeDtypeStruct((VIEWS * 64, 192), BF16),
            jax.ShapeDtypeStruct((192, VIEWS * 64), BF16),
            jax.ShapeDtypeStruct((512, 512), BF16),
        ),
        in_specs=smem(2),
        out_specs=tuple(vmem(7)),
        name="bands",
    )(taps, shifts)


def pack_kernel(index_ref, target_ref, pieces_ref, first_ref, last_ref, out_ref, low_ref, high_ref, stage_ref, swap_ref,
                sent_ref):
    step = pl.program_id(0)
    count = target_ref.shape[0]

    @pl.when(step == 0)
    def _():
        swap_ref[...] = digit_swap((512, 512))

    rows = []
    for k in range(4):
        for half in range(2):
            rows.append(jnp.concatenate(
                [pieces_ref[k, q, :, half * 128:(half + 1) * 128] for q in range(4)], axis=1))
    mixed = jnp.dot(jnp.concatenate(rows, axis=0), swap_ref[...], preferred_element_type=F32).astype(BF16)
    for k in range(4):
        piece = step * 4 + k
        target = target_ref[piece]
        rank = jnp.int32(0)
        for other in range(count):
            rank = rank + jnp.where((target_ref[other] == target) & (other < piece), 1, 0)
        slot = target * CAP + rank
        for half in range(2):
            first = (k * 2 + half) * NY
            for part in range(4):
                stage_ref[piece, half * 4 + part] = mixed[first:first + NY, part * 128:(part + 1) * 128]
        pltpu.make_async_copy(stage_ref.at[piece], out_ref.at[:, slot], sent_ref.at[piece]).start()

    part = index_ref[0]
    amount = (16 - PART * part + 256) % 256
    lane = lax.broadcasted_iota(I32, (32, 128), 1)
    column = part * PART - HALO + lane % 64
    inside = (column >= 0) & (column < 256)
    for source_ref, target_ref_out in ((first_ref, low_ref), (last_ref, high_ref)):
        planes = []
        for k in range(4):
            plane = source_ref[k]
            top = pltpu.roll(plane[:32], amount, 1)[:, :128]
            bottom = pltpu.roll(plane[32:], (amount + 64) % 256, 1)[:, :128]
            planes.append(jnp.where(inside, jnp.where(lane < 64, top, bottom), 0.0))
        for m in range(4):
            rows = slice(m * 8, m * 8 + 8)
            front = swap_fours(planes[0][rows], planes[1][rows])
            back = swap_fours(planes[2][rows], planes[3][rows])
            for odd in range(2):
                target_ref_out[m * 2 + odd, pl.ds(pl.multiple_of(step * 16, 16), 16), :] = jnp.concatenate(
                    [front[odd], back[odd]], axis=0).astype(BF16)

    @pl.when(step == 3)
    def _():
        for piece in range(count):
            pltpu.make_async_copy(stage_ref.at[piece], out_ref.at[:, 0], sent_ref.at[piece]).wait()


def pack_pieces(index, targets, pieces, estimate, block_count):
    count = pieces.shape[0]
    return pl.pallas_call(
        pack_kernel,
        grid=(4,),
        out_shape=(
            jax.ShapeDtypeStruct((VIEWS, block_count * CAP, NY, 128), BF16),
            jax.ShapeDtypeStruct((8, 64, 128), BF16),
            jax.ShapeDtypeStruct((8, 64, 128), BF16),
        ),
        in_specs=smem(2) + [pl.BlockSpec((4,) + pieces.shape[1:], lambda step: (step, 0, 0, 0)),
                            pl.BlockSpec((4, NY, 256), lambda step: (step, 0, 0)),
                            pl.BlockSpec((4, NY, 256), lambda step: (12 + step, 0, 0))],
        out_specs=(pl.BlockSpec(memory_space=pl.ANY),) + tuple(vmem(2)),
        scratch_shapes=[pltpu.VMEM((count, VIEWS, NY, 128), BF16), pltpu.VMEM((512, 512), BF16),
                        pltpu.SemaphoreType.DMA((count,))],
        name="pack",
    )(index, targets, pieces, estimate, estimate)


def window_kernel(index_ref, estimate_ref, main_ref):
    part = index_ref[0]
    block = lane_block((NY, 128))
    lane = lax.broadcasted_iota(I32, (NY, 128), 1) % PART

    def two_planes(step, carry):
        for half in range(2):
            column = (part + half) * PART - HALO + lane
            inside = (column >= 0) & (column < 256)
            planes = []
            for odd in range(2):
                result = jnp.zeros((NY, 128), F32)
                for h in range(4):
                    plane = estimate_ref[h * 16 + step * 2 + odd]
                    amount = (16 - PART * part - PART * half + PART * h + 512) % 256
                    result = jnp.where(block == h, pltpu.roll(plane, amount, 1)[:, :128], result)
                planes.append(jnp.where(inside, result, 0.0))
            for m in range(8):
                low, high = swap_fours(planes[0][m * 8:m * 8 + 8], planes[1][m * 8:m * 8 + 8])
                main_ref[half, pl.ds(pl.multiple_of(m * 128 + step * 8, 8), 8), :] = low
                main_ref[half, pl.ds(pl.multiple_of(m * 128 + 64 + step * 8, 8), 8), :] = high
        return carry

    lax.fori_loop(0, 8, two_planes, 0)


def window_estimate(index, estimate):
    return pl.pallas_call(
        window_kernel,
        out_shape=jax.ShapeDtypeStruct((2, 1024, 128), F32),
        in_specs=smem(1) + vmem(1),
        out_specs=vmem(1)[0],
        name="window",
    )(index, estimate)


def build_tail(edge_ref, from_low_ref, from_high_ref, tail_ref):
    block = lane_block((64, 128))

    def two_quads(quad, carry):
        low = from_low_ref[quad].astype(F32) * edge_ref[2]
        high = from_high_ref[quad].astype(F32) * edge_ref[3]
        for member in range(2):
            base = member * 64
            result = jnp.where(block == 0, rotate(low, -base), rotate(low, 32 - base))
            result = jnp.where(block == 1, rotate(high, 32 - base), result)
            tail_ref[quad + member * 8] = jnp.where(block == 3, rotate(high, 64 - base), result)
        return carry

    lax.fori_loop(0, QUADS // 2, two_quads, 0)


def weight_kernel(rows_ref, main_ref, tail_ref, out_main_ref, out_tail_ref):
    quarter = lax.broadcasted_iota(I32, (64, 128), 0) % 4

    def one_quad(quad, carry):
        rows = pl.ds(pl.multiple_of(quad * 64, 64), 64)
        totals = [jnp.zeros((64, 128), F32) for _ in range(3)]
        for view in range(VIEWS):
            factor = jnp.full((64, 128), rows_ref[view * NY + quad * 4], F32)
            for k in range(1, 4):
                factor = jnp.where(quarter == k, rows_ref[view * NY + quad * 4 + k], factor)
            totals[0] = totals[0] + factor * main_ref[view, 0]
            totals[1] = totals[1] + factor * main_ref[view, 1]
            totals[2] = totals[2] + factor * tail_ref[view]
        out_main_ref[0, rows, :] = 1.0 / jnp.maximum(totals[0], 1.0)
        out_main_ref[1, rows, :] = 1.0 / jnp.maximum(totals[1], 1.0)
        out_tail_ref[quad] = 1.0 / jnp.maximum(totals[2], 1.0)
        return carry

    lax.fori_loop(0, QUADS, one_quad, 0)


def build_weights(rows, main, tail):
    return pl.pallas_call(
        weight_kernel,
        out_shape=(
            jax.ShapeDtypeStruct((2, 1024, 128), F32),
            jax.ShapeDtypeStruct((QUADS, 64, 128), F32),
        ),
        in_specs=smem(1) + vmem(2),
        out_specs=tuple(vmem(2)),
        name="weights",
    )(rows, main, tail)


def forward_depth(main_ref, tail_ref, bzf_ref, planes_ref):
    block = lane_block((64, 128))

    def stacked(quad):
        rows = pl.ds(pl.multiple_of(quad * 64, 64), 64)
        left = main_ref[0, rows, :]
        right = main_ref[1, rows, :]
        tail = tail_ref[quad]
        turned = rotate(tail, 64)
        lower = jnp.concatenate([jnp.where(block == 0, tail, rotate(left, 32)),
                                 jnp.where(block == 0, turned, rotate(right, 32))], axis=1)
        upper = jnp.concatenate([jnp.where(block == 3, turned, rotate(left, 96)),
                                 jnp.where(block == 3, tail, rotate(right, 96))], axis=1)
        return jnp.concatenate([lower, jnp.concatenate([left, right], axis=1), upper], axis=0).astype(BF16)

    def two_quads(step, carry):
        both = jnp.concatenate([stacked(step * 2), stacked(step * 2 + 1)], axis=1)
        blurred = jnp.dot(bzf_ref[...], both, preferred_element_type=F32).astype(BF16)
        for member in range(2):
            first = pl.multiple_of(step * 32 + member * 16, 16)
            for group in range(VIEWS * 4):
                planes_ref[group, pl.ds(first, 16), :] = blurred[
                    group * 16:(group + 1) * 16, member * ROWS:(member + 1) * ROWS]
        return carry

    lax.fori_loop(0, QUADS // 2, two_quads, 0, unroll=2)


def forward_plane(view, planes_ref, ky, kx):
    volume = planes_ref[pl.ds(view * 4, 4)].reshape(4 * ROWS, ROWS)
    along_x = jnp.concatenate([jnp.dot(volume[r * 512:(r + 1) * 512], kx, preferred_element_type=F32)
                               for r in range(2)], axis=0).astype(BF16)
    side = jnp.concatenate([along_x[r * ROWS:(r + 1) * ROWS] for r in range(4)], axis=1)
    return jnp.dot(ky, side, preferred_element_type=F32)


def adjoint_plane(view, quotient, kyt, kxt, depth_ref):
    along_y = jnp.dot(kyt, quotient.astype(BF16), preferred_element_type=F32).astype(BF16)
    stacked = jnp.concatenate([along_y[:, r * 128:(r + 1) * 128] for r in range(4)], axis=0)
    along_x = jnp.concatenate([jnp.dot(stacked[r * 512:(r + 1) * 512], kxt, preferred_element_type=F32)
                               for r in range(2)], axis=0).astype(BF16)
    for r in range(4):
        first = pl.multiple_of(view * 64 + r * 16, 16)
        for quad in range(QUADS):
            depth_ref[quad, pl.ds(first, 16), :] = along_x[r * ROWS + quad * 16:r * ROWS + quad * 16 + 16]


def own_lanes(left, right):
    lane = lax.broadcasted_iota(I32, left.shape, 1) % PART
    return jnp.where(lane < HALO, rotate(left, 112), rotate(right, 16))


def adjoint_depth(scale, bza_ref, depth_ref, main_ref, tail_ref, to_left_ref, to_right_ref, last=False):
    block = lane_block((64, 128))
    low_half = block < 2
    near = lax.broadcasted_iota(I32, (64, 128), 1) % PART < HALO

    def pair(quad, carry):
        tails = []
        members = (quad, quad + QUADS // 2)
        both = jnp.concatenate([depth_ref[member] for member in members], axis=1)
        summed_both = jnp.dot(bza_ref[...], both, preferred_element_type=F32)
        for index, member in enumerate(members):
            summed = summed_both[:, index * ROWS:(index + 1) * ROWS]
            mains = []
            for half in range(2):
                lanes = slice(half * 128, (half + 1) * 128)
                lower = jnp.where(block < 3, rotate(summed[:64, lanes], 96), 0.0)
                upper = jnp.where(block > 0, rotate(summed[128:, lanes], 32), 0.0)
                mains.append(summed[64:128, lanes] + lower + upper)
            tail = jnp.where(block == 0, summed[:64, :128], summed[128:, 128:])
            tail = jnp.where(block == 1, rotate(summed[128:, :128], 64), tail)
            tail = jnp.where(block == 2, rotate(summed[:64, 128:], 64), tail)
            if last:
                main_ref[member] = own_lanes(*mains)
                tail_ref[member] = jnp.where(near, rotate(tail, 112), rotate(tail, 80))
                to_left_ref[member] = to_fixed(jnp.where(near, mains[0], rotate(tail, 16)), scale)
                to_right_ref[member] = to_fixed(jnp.where(near, rotate(tail, 48), mains[1]), scale)
                continue
            rows = pl.ds(pl.multiple_of(member * 64, 64), 64)
            main_ref[0, rows, :] = mains[0]
            main_ref[1, rows, :] = mains[1]
            tail_ref[member] = tail
            to_left_ref[member] = to_fixed(mains[0], scale)
            to_right_ref[member] = to_fixed(mains[1], scale)
            tails.append(tail)
        if last:
            return carry
        to_left_ref[QUADS + quad] = to_fixed(jnp.where(low_half, tails[0], rotate(tails[1], 64)), scale)
        to_right_ref[QUADS + quad] = to_fixed(jnp.where(low_half, rotate(tails[0], 64), tails[1]), scale)
        return carry

    lax.fori_loop(0, QUADS // 2, pair, 0, unroll=2)


def tall(value):
    return jnp.concatenate([value] * 8, axis=0)


def forward_kernel(edge_ref, main_ref, from_low_ref, from_high_ref, bzf_ref, ky_ref, kx_ref, out_ref, tail_ref,
                   planes_ref):
    build_tail(edge_ref, from_low_ref, from_high_ref, tail_ref)
    forward_depth(main_ref, tail_ref, bzf_ref, planes_ref)

    def one_view(view, carry):
        out_ref[view] = forward_plane(view, planes_ref, ky_ref[view], kx_ref[view]).astype(BF16)
        return carry

    lax.fori_loop(0, VIEWS, one_view, 0)


def forward(edges, main, from_low, from_high, bzf, ky, kx):
    return pl.pallas_call(
        forward_kernel,
        out_shape=(
            jax.ShapeDtypeStruct((VIEWS, ROWS, 2 * ROWS), BF16),
            jax.ShapeDtypeStruct((QUADS, 64, 128), F32),
        ),
        in_specs=smem(1) + vmem(6),
        out_specs=tuple(vmem(2)),
        scratch_shapes=[pltpu.VMEM((VIEWS * 4, ROWS, ROWS), BF16)],
        name="forward",
    )(edges, main, from_low, from_high, bzf, ky, kx)


def per_view(*shape):
    return pl.BlockSpec((2,) + shape, lambda step: (step,) + (0,) * len(shape))


PARTIAL_SHAPES = (
    held((2, 1024, 128), F32),
    held((QUADS, 64, 128), F32),
    held((QUADS + QUADS // 2, 64, 128), I16),
    held((QUADS + QUADS // 2, 64, 128), I16),
)


def first_adjoint_kernel(start_ref, source_ref, place_ref, inverse_ref, offset_ref, incoming_ref, blurred_ref, kyt_ref,
                         kxt_ref, bza_ref, swap_ref, main_ref, tail_ref, to_left_ref, to_right_ref, average_ref,
                         total_ref, depth_ref):
    step = pl.program_id(0)

    for slot in range(2 * SLOTS):
        total_ref[slot] = jnp.zeros((NY, 128), F32)

    def add(entry, carry):
        place = place_ref[entry]
        piece = incoming_ref[source_ref[entry] - step * incoming_ref.shape[0]].astype(F32)
        slot = place - step * (2 * SLOTS)
        total_ref[slot] = total_ref[slot] + piece * inverse_ref[place]
        return carry

    lax.fori_loop(start_ref[step * 2], start_ref[step * 2 + 2], add, 0)
    rows = []
    for r in range(8):
        rows.append(jnp.concatenate(
            [total_ref[r // 4 * SLOTS + h * 4 + r % 4].astype(BF16) for h in range(4)], axis=1))
    mixed = jnp.dot(jnp.concatenate(rows, axis=0), swap_ref[...], preferred_element_type=F32)
    for r in range(8):
        lanes = slice(r % 4 * 128, r % 4 * 128 + 128)
        for m in range(8):
            first = r * NY + m * 8
            ends = []
            for q in (0, 2):
                ends.append(swap_fours(mixed[first:first + 8, q * 128:(q + 1) * 128],
                                       mixed[first:first + 8, (q + 1) * 128:(q + 2) * 128]))
            for odd in range(2):
                quad = 2 * m + odd
                average_ref[r // 4, quad * 16:quad * 16 + 16, lanes] = jnp.concatenate(
                    [ends[0][odd], ends[1][odd]], axis=0).astype(BF16)
    quotients = [average_ref[k].astype(F32) / (blurred_ref[k].astype(F32) + offset_ref[step * 2 + k]) for k in range(2)]
    for k in range(2):
        adjoint_plane(step * 2 + k, quotients[k], kyt_ref[k], kxt_ref[k], depth_ref)

    @pl.when(step == VIEWS // 2 - 1)
    def _():
        scale = tall(32767.0 / partial_bound(offset_ref))
        adjoint_depth(scale, bza_ref, depth_ref, main_ref, tail_ref, to_left_ref, to_right_ref)


def first_adjoint(start, source, place, inverse, offset, incoming, blurred, kyt, kxt, bza, swap):
    share = incoming.shape[0] // (VIEWS // 2)
    return pl.pallas_call(
        first_adjoint_kernel,
        grid=(VIEWS // 2,),
        out_shape=PARTIAL_SHAPES + (jax.ShapeDtypeStruct((VIEWS, ROWS, 2 * ROWS), BF16),),
        in_specs=smem(5) + [pl.BlockSpec((share, NY, 128), lambda view: (view, 0, 0)), per_view(ROWS, 2 * ROWS),
                            per_view(ROWS, ROWS), per_view(128, ROWS)] + vmem(2),
        out_specs=tuple(vmem(4)) + (per_view(ROWS, 2 * ROWS),),
        scratch_shapes=[pltpu.VMEM((2 * SLOTS, NY, 128), F32), pltpu.VMEM((QUADS, VIEWS * 64, ROWS), BF16)],
        name="first_adjoint",
        compiler_params=room(60),
    )(start, source, place, inverse, offset, incoming, blurred, kyt, kxt, bza, swap)


def join_columns_kernel(offset_ref, edge_ref, main_ref, tail_ref, from_left_ref, from_right_ref, out_main_ref, out_tail_ref,
                        low_ref, high_ref):
    block = lane_block((64, 128))
    low_half = block < 2
    bound = partial_bound(offset_ref)
    scale = tall(32767.0 / bound)
    left_step = tall(bound * (edge_ref[0] / 32767.0))
    right_step = tall(bound * (edge_ref[1] / 32767.0))

    def pair(quad, carry):
        packed_left = from_fixed(from_left_ref[QUADS + quad], left_step)
        packed_right = from_fixed(from_right_ref[QUADS + quad], right_step)
        for second, member in enumerate((quad, quad + QUADS // 2)):
            rows = pl.ds(pl.multiple_of(member * 64, 64), 64)
            left = main_ref[0, rows, :] + from_fixed(from_left_ref[member], left_step)
            right = main_ref[1, rows, :] + from_fixed(from_right_ref[member], right_step)
            if second:
                extra = jnp.where(low_half, rotate(packed_left, 64), packed_right)
            else:
                extra = jnp.where(low_half, packed_left, rotate(packed_right, 64))
            tail = tail_ref[member] + extra
            out_main_ref[0, rows, :] = left
            out_main_ref[1, rows, :] = right
            out_tail_ref[member] = tail
            low = jnp.where(block == 1, rotate(left, 32), tail)
            low = jnp.where(block == 3, rotate(right, 96), low)
            high = jnp.where(block == 0, rotate(left, 32), tail)
            high = jnp.where(block == 2, rotate(right, 96), high)
            low_ref[member] = to_fixed(low, scale)
            high_ref[member] = to_fixed(high, scale)
        return carry

    lax.fori_loop(0, QUADS // 2, pair, 0)


def join_columns(offset, edges, main, tail, from_left, from_right):
    return pl.pallas_call(
        join_columns_kernel,
        out_shape=(
            held((2, 1024, 128), F32),
            held((QUADS, 64, 128), F32),
            held((QUADS, 64, 128), I16),
            held((QUADS, 64, 128), I16),
        ),
        in_specs=smem(2) + vmem(4),
        out_specs=tuple(vmem(4)),
        name="join_columns",
        compiler_params=room(48),
    )(offset, edges, *stay(main, tail, from_left, from_right))


def joined_planes(quad, steps, block, main_ref, tail_ref, from_low_ref, from_high_ref):
    rows = pl.ds(pl.multiple_of(quad * 64, 64), 64)
    low = from_fixed(from_low_ref[quad], steps[0])
    high = from_fixed(from_high_ref[quad], steps[1])
    left = main_ref[0, rows, :]
    left = left + jnp.where(block == 0, rotate(low, 96), 0.0) + jnp.where(block == 3, rotate(high, 96), 0.0)
    right = main_ref[1, rows, :]
    right = right + jnp.where(block == 0, rotate(low, 32), 0.0) + jnp.where(block == 3, rotate(high, 32), 0.0)
    tail = tail_ref[quad] + jnp.where(block % 2 == 0, low, high)
    return rows, left, right, tail


def depth_steps(bound, edge_ref):
    return tall(bound * (edge_ref[2] / 32767.0)), tall(bound * (edge_ref[3] / 32767.0))


def second_kernel(offset_ref, edge_ref, part_main_ref, part_tail_ref, from_low_ref, from_high_ref, estimate_main_ref,
                  estimate_tail_ref, scale_main_ref, scale_tail_ref, bzf_ref, bza_ref, average_ref, ky_ref, kx_ref,
                  kyt_ref, kxt_ref, own_estimate_ref, own_ref, own_tail_ref, to_left_ref, to_right_ref, new_main_ref,
                  tail_estimate_ref, planes_ref, depth_ref):
    step = pl.program_id(0)

    @pl.when(step == 0)
    def _():
        block = lane_block((64, 128))
        steps = depth_steps(partial_bound(offset_ref), edge_ref)

        def renew(quad, carry):
            rows, left, right, tail = joined_planes(
                quad, steps, block, part_main_ref, part_tail_ref, from_low_ref, from_high_ref)
            left = estimate_main_ref[0, rows, :] * left * scale_main_ref[0, rows, :]
            right = estimate_main_ref[1, rows, :] * right * scale_main_ref[1, rows, :]
            new_main_ref[0, rows, :] = left
            new_main_ref[1, rows, :] = right
            own_estimate_ref[quad] = own_lanes(left * scale_main_ref[0, rows, :], right * scale_main_ref[1, rows, :])
            tail_estimate_ref[quad] = estimate_tail_ref[quad] * tail * scale_tail_ref[quad]
            return carry

        lax.fori_loop(0, QUADS, renew, 0)
        forward_depth(new_main_ref, tail_estimate_ref, bzf_ref, planes_ref)

    views = [step * 2, step * 2 + 1]
    blurred = [forward_plane(views[k], planes_ref, ky_ref[k], kx_ref[k]) + offset_ref[views[k]] for k in range(2)]
    quotients = [average_ref[k].astype(F32) / blurred[k] for k in range(2)]
    for k in range(2):
        adjoint_plane(views[k], quotients[k], kyt_ref[k], kxt_ref[k], depth_ref)

    @pl.when(step == VIEWS // 2 - 1)
    def _():
        scale = tall(32767.0 / partial_bound(offset_ref))
        adjoint_depth(scale, bza_ref, depth_ref, own_ref, own_tail_ref, to_left_ref, to_right_ref, last=True)


def second(offset, edges, *operands):
    return pl.pallas_call(
        second_kernel,
        grid=(VIEWS // 2,),
        out_shape=(held((QUADS, 64, 128), F32),) * 3 + (held((QUADS, 64, 128), I16),) * 2,
        in_specs=smem(2) + vmem(10) + [per_view(ROWS, 2 * ROWS), per_view(ROWS, ROWS), per_view(ROWS, 128),
                                       per_view(ROWS, ROWS), per_view(128, ROWS)],
        out_specs=tuple(vmem(5)),
        scratch_shapes=[pltpu.VMEM((2, 1024, 128), F32), pltpu.VMEM((QUADS, 64, 128), F32),
                        pltpu.VMEM((VIEWS * 4, ROWS, ROWS), BF16), pltpu.VMEM((QUADS, VIEWS * 64, ROWS), BF16)],
        name="second",
        compiler_params=room(52),
    )(offset, edges, *stay(*operands[:4]), *operands[4:])


def join_own_kernel(offset_ref, edge_ref, own_ref, tail_ref, from_left_ref, from_right_ref, out_ref, low_ref, high_ref):
    block = lane_block((64, 128))
    near = lax.broadcasted_iota(I32, (64, 128), 1) % PART < HALO
    bound = partial_bound(offset_ref)
    scale = tall(32767.0 / bound)
    left_step = tall(bound * (edge_ref[0] / 32767.0))
    right_step = tall(bound * (edge_ref[1] / 32767.0))

    def four_quads(quad, carry):
        low = jnp.zeros((64, 128), F32)
        high = jnp.zeros((64, 128), F32)
        for k in range(4):
            member = quad + k * 4
            left = from_fixed(from_left_ref[member], left_step)
            right = from_fixed(from_right_ref[member], right_step)
            out_ref[member] = own_ref[member] + own_lanes(left, right)
            tail = tail_ref[member] + jnp.where(near, left, right)
            low = jnp.where(block == k, rotate(tail, PART * k), low)
            high = jnp.where(block == k, rotate(tail, PART * k - PART), high)
        low_ref[quad] = to_fixed(low, scale)
        high_ref[quad] = to_fixed(high, scale)
        return carry

    lax.fori_loop(0, QUADS // 4, four_quads, 0)


def join_own(offset, edges, own, tail, from_left, from_right):
    return pl.pallas_call(
        join_own_kernel,
        out_shape=(held((QUADS, 64, 128), F32), held((QUADS // 4, 64, 128), I16), held((QUADS // 4, 64, 128), I16)),
        in_specs=smem(2) + vmem(4),
        out_specs=tuple(vmem(3)),
        name="join_own",
        compiler_params=room(48),
    )(offset, edges, *stay(own, tail, from_left, from_right))


def finish_kernel(offset_ref, edge_ref, own_ref, from_low_ref, from_high_ref, estimate_ref, out_ref, value_ref):
    block = lane_block((64, 128))
    steps = depth_steps(partial_bound(offset_ref), edge_ref)

    def four_quads(quad, largest):
        low = from_fixed(from_low_ref[quad], steps[0])
        high = from_fixed(from_high_ref[quad], steps[1])
        for k in range(4):
            member = quad + k * 4
            summed = own_ref[member] + jnp.where(block == 0, rotate(low, -PART * k), 0.0)
            summed = summed + jnp.where(block == 3, rotate(high, 96 - PART * k), 0.0)
            value = estimate_ref[member] * summed
            value_ref[member] = value
            largest = jnp.maximum(largest, value)
        return largest

    largest = lax.fori_loop(0, QUADS // 4, four_quads, jnp.zeros((64, 128), F32))
    unit = (jnp.max(largest) * 64.0).astype(I32) + 1
    vector = jnp.full((16, 128), unit, I32)
    out_ref[1024:1040, :] = (vector >> 15).astype(I16)
    out_ref[1040:1056, :] = (vector & 32767).astype(I16)
    factor = (32767.0 * 64.0) / vector.astype(F32)

    def sixteen_rows(n, carry):
        for j in range(0, 16, 2):
            rows = slice(j * 4, j * 4 + 8)
            ends = [swap_fours(value_ref[n * 4 + 2 * m, rows, :], value_ref[n * 4 + 2 * m + 1, rows, :])
                    for m in range(2)]
            for odd in range(2):
                first = pl.multiple_of((j + odd) * NY + n * 16, 16)
                out_ref[pl.ds(first, 16), :] = to_fixed(
                    jnp.concatenate([ends[0][odd], ends[1][odd]], axis=0), factor)
        return carry

    lax.fori_loop(0, 4, sixteen_rows, 0)


def finish(offset, edges, own, from_low, from_high, estimate):
    return pl.pallas_call(
        finish_kernel,
        out_shape=held((1056, 128), I16),
        in_specs=smem(2) + vmem(4),
        out_specs=vmem(1)[0],
        scratch_shapes=[pltpu.VMEM((QUADS, 64, 128), F32)],
        name="finish",
        compiler_params=room(52),
    )(offset, edges, *stay(own, from_low, from_high, estimate))


def assemble_kernel(index_ref, *refs):
    chunk_refs, out_ref, buffer_ref = refs[:8], refs[8], refs[9]
    part = index_ref[0]

    @pl.when(pl.program_id(0) == 0)
    def _():
        for place in range(8):
            owner = ((part // 2 + place % 4) % 4) * 2 + (part % 2 if place < 4 else 1 - part % 2)
            buffer_ref[owner] = chunk_refs[place][...]

    block = lane_block((16, 128))
    even = block % 2 == 0
    units = []
    for half in range(2):
        unit = jnp.zeros((16, 128), F32)
        for k in range(4):
            digits = (buffer_ref[half * 4 + k, 1024:1040, :].astype(I32) * 32768
                      + buffer_ref[half * 4 + k, 1040:1056, :].astype(I32))
            unit = jnp.where(block == k, digits.astype(F32) * (1.0 / (64.0 * 32767.0)), unit)
        units.append(unit)
    step = pl.program_id(0)

    def sixteen_rows(n, carry):
        lines = pl.ds(pl.multiple_of(n * 16, 16), 16)
        for j in (0, 2):
            first = pl.multiple_of((step * 4 + j) * NY + n * 16, 16)
            for half in range(2):
                c0, c1, c2, c3 = (
                    buffer_ref[half * 4 + k, pl.ds(first, 16), :].astype(I32)
                    | (buffer_ref[half * 4 + k, pl.ds(first + NY, 16), :].astype(I32) << 16) for k in range(4))
                a0 = jnp.where(block < 2, c0, rotate(c2, 64))
                a1 = jnp.where(block < 2, c1, rotate(c3, 64))
                a2 = jnp.where(block < 2, rotate(c0, 64), c2)
                a3 = jnp.where(block < 2, rotate(c1, 64), c3)
                results = (jnp.where(even, a0, rotate(a1, 32)), jnp.where(even, rotate(a0, 96), a1),
                           jnp.where(even, a2, rotate(a3, 32)), jnp.where(even, rotate(a2, 96), a3))
                lanes = slice(half * 128, (half + 1) * 128)
                for h in range(4):
                    out_ref[h, 0, j, lines, lanes] = (results[h] & 65535).astype(F32) * units[half]
                    out_ref[h, 0, j + 1, lines, lanes] = (results[h] >> 16).astype(F32) * units[half]
        return carry

    lax.fori_loop(0, 4, sixteen_rows, 0, unroll=2)


def assemble(index, chunks):
    return pl.pallas_call(
        assemble_kernel,
        grid=(4,),
        out_shape=jax.ShapeDtypeStruct((4, 4, 4, NY, 256), F32),
        in_specs=smem(1) + vmem(8),
        out_specs=pl.BlockSpec((4, 1, 4, NY, 256), lambda step: (0, step, 0, 0, 0)),
        scratch_shapes=[pltpu.VMEM((VIEWS, 1056, 128), I16)],
        name="assemble",
        compiler_params=room(58),
    )(index, *stay(*chunks)).reshape(64, NY, 256)


def to_neighbours(upward, downward, axis):
    count = lax.axis_size(axis)
    from_low = lax.ppermute(upward, axis, [(i, (i + 1) % count) for i in range(count)])
    from_high = lax.ppermute(downward, axis, [((i + 1) % count, i) for i in range(count)])
    return from_low, from_high


def gather_parts(own):
    parts = [own] + [
        lax.ppermute(own, "view", [((i + 2 * step) % VIEWS, i) for i in range(VIEWS)]) for step in (1, 3, 2)
    ]
    parts = [parts[0], parts[1], parts[3], parts[2]]
    return parts, [lax.ppermute(part, "view", [(i, i ^ 1) for i in range(VIEWS)]) for part in parts]


def column_sums(kernel, shift, positions, length):
    radius = (TAPS - 1) // 2
    source = (positions[None, :, None] - shift[:, None, None]
              - jnp.arange(TAPS, dtype=I32)[None, None, :] + radius)
    inside = (source >= 0) & (source < length)
    return jnp.sum(jnp.where(inside, kernel[:, None, :], 0.0), axis=2)


def program(estimate0, pieces, dest_block, slot_index, psf_shift, psf_taps, background):
    block_count = lax.axis_size("block")
    my_view = lax.axis_index("view")
    my_block = lax.axis_index("block")
    edges = jnp.stack([my_view > 0, my_view < VIEWS - 1, my_block > 0, my_block < block_count - 1]).astype(F32)
    targets = dest_block[:, :, 0].reshape(VIEWS, block_count, SLOTS)
    slots = slot_index.reshape(VIEWS, block_count, SLOTS)

    index = my_view.reshape(1).astype(I32)
    own_targets = lax.dynamic_slice(targets, (my_view, my_block, 0), (1, 1, SLOTS)).reshape(SLOTS)
    outgoing, low, high = pack_pieces(index, own_targets, pieces[0], estimate0, block_count)
    from_low, from_high = to_neighbours(high, low, "block")
    incoming = lax.all_to_all(outgoing.reshape(VIEWS * block_count, CAP, NY, 128), ("view", "block"), 0, 0, tiled=True)
    incoming = incoming.reshape(VIEWS * block_count * CAP, NY, 128)

    main = window_estimate(index, estimate0)
    kernel = psf_taps / jnp.sum(psf_taps, axis=2, keepdims=True)
    ky, kyt, kx, kxt, bzf, bza, swap = build_bands(kernel.reshape(-1), psf_shift.reshape(-1))
    blurred, tail = forward(edges, main, from_low, from_high, bzf, ky, kx)

    earlier = jnp.tril(jnp.ones((SLOTS, SLOTS), jnp.bool_), -1)
    same = (targets[:, :, :, None] == targets[:, :, None, :]) & earlier[None, None]
    ranks = jnp.sum(same.astype(I32), axis=3)
    mine = targets == my_block
    received = jnp.arange(CAP, dtype=I32)
    slot_of = jnp.sum(
        jnp.where(mine[..., None] & (ranks[..., None] == received), slots[..., None] + 1, 0), axis=2
    ).reshape(VIEWS, block_count * CAP) - 1
    hits = slot_of[:, :, None] == jnp.arange(SLOTS, dtype=I32)
    counts = jnp.sum(hits.astype(I32), axis=1)
    inverse = 1.0 / jnp.maximum(counts, 1).astype(F32)
    entries = VIEWS * block_count * CAP
    number = jnp.arange(entries, dtype=I32)
    place_of = jnp.where(slot_of >= 0, slot_of + jnp.arange(VIEWS, dtype=I32)[:, None] * SLOTS, -1).reshape(entries)
    before = (place_of[None, :] >= 0) & (number[None, :] < number[:, None])
    position = jnp.where(place_of >= 0, jnp.sum(before.astype(I32), axis=1), -1)
    chosen = position[:, None] == number[None, :]
    source = jnp.sum(jnp.where(chosen, number[:, None], 0), axis=0)
    place = jnp.sum(jnp.where(chosen, place_of[:, None], 0), axis=0)
    start = jnp.sum(((place_of >= 0)[:, None]
                     & (number[:, None] // (block_count * CAP) < jnp.arange(VIEWS + 1))).astype(I32), axis=0)

    global_slot = (targets * SLOTS + slots).reshape(VIEWS, block_count * SLOTS)
    all_slots = jnp.arange(block_count * SLOTS, dtype=I32)
    occupied = jnp.any(global_slot[:, :, None] == all_slots, axis=1)
    mask = jnp.repeat(occupied.astype(F32), 4, axis=1)
    padded = jnp.pad(mask, ((0, 0), (2 * HALO, 2 * HALO)))
    window = lax.dynamic_slice_in_dim(padded, my_block * 64, 128, 1)
    depth = lax.broadcasted_iota(I32, (96, 128), 0) + HALO - lax.broadcasted_iota(I32, (96, 128), 1)
    tap = depth[None] - psf_shift[:, 0, None, None] + (TAPS - 1) // 2
    weight_depth = jnp.zeros((VIEWS, 96), F32)
    band = jnp.zeros((VIEWS, 96, 128), F32)
    for j in range(TAPS):
        band = jnp.where(tap == j, kernel[:, 0, j, None, None], band)
    weight_depth = jnp.sum(band * window[:, None, :], axis=2)
    weight_rows = column_sums(kernel[:, 1], psf_shift[:, 1], jnp.arange(NY, dtype=I32), NY)
    columns = my_view * PART - HALO + jnp.arange(2 * PART, dtype=I32)
    weight_columns = column_sums(kernel[:, 2], psf_shift[:, 2], columns, 256).reshape(VIEWS, 2, PART)
    by_group = weight_depth.reshape(VIEWS, 6, 16)
    planes = by_group[:, :, :, None, None] * weight_columns[:, None, None, :, :]
    planes = planes.transpose(0, 3, 2, 1, 4)
    weight_main = planes[:, :, :, 1:5].reshape(VIEWS, 2, 16, 128)
    weight_tail = jnp.stack([planes[:, :, :, 0], planes[:, :, :, 5]], axis=3)
    weight_tail = weight_tail.transpose(0, 2, 1, 3, 4).reshape(VIEWS, 16, 128)
    scale_main, scale_tail = build_weights(
        weight_rows.reshape(-1), jnp.repeat(weight_main, 4, axis=2), jnp.repeat(weight_tail, 4, axis=1))

    incoming, scale_main, scale_tail = lax.optimization_barrier((incoming, scale_main, scale_tail))
    part_main, part_tail, to_left, to_right, average = first_adjoint(
        start, source, place, inverse.reshape(-1), background, incoming, blurred, kyt, kxt, bza, swap)
    from_left, from_right = to_neighbours(to_right, to_left, "view")
    part_main, part_tail, low, high = join_columns(background, edges, part_main, part_tail, from_left, from_right)
    from_low, from_high = to_neighbours(high, low, "block")

    estimate, own, own_tail, to_left, to_right = second(
        background, edges, part_main, part_tail, from_low, from_high, main, tail, scale_main, scale_tail,
        bzf, bza, average, ky, kx, kyt, kxt)
    from_left, from_right = to_neighbours(to_right, to_left, "view")
    own, low, high = join_own(background, edges, own, own_tail, from_left, from_right)
    from_low, from_high = to_neighbours(high, low, "block")
    own = finish(background, edges, own, from_low, from_high, estimate)

    mine, partners = gather_parts(own)
    return assemble(index, mine + partners)


def solution(mesh):
    return jax.shard_map(
        program,
        mesh=mesh,
        in_specs=(
            P("block", None, None),
            P("view", "block", None, None, None),
            P(),
            P(),
            P(),
            P(),
            P(),
        ),
        out_specs=P("block", None, None),
        check_vma=False,
    )
```
